128 devices in a mesh: depth: 8 (over y, z_hi), tan: 16 (over x, z_lo, core).
Axes of the slice: x: 4, y: 4, z: 4 (z_hi: 2, z_lo: 2; z = z_hi * 2 + z_lo), core: 2. Of those that a mesh axis runs over, the one named last changes fastest.
Arguments:
- displacement: float32 [3, 64, 512, 2048], P(None, 'depth', 'tan'), may hold values from -6 to 6
- stiffness: float32 [64, 512, 2048], P('depth', 'tan'), may hold values from 0.5 to 8
- node_list: int32 [512, 128], replicated, may hold values from 0 to 1048575, as said below
- active_count: int32 [512], replicated, may hold values from 1 to 128
- wear_class: int32 [512, 128], P('tan'), may hold values from 0 to 7
- pressure: float32 [512, 128], P('tan'), may hold values from 0.5 to 2
- slip_speed: float32 [512, 128], P('tan'), may hold values from 0.2 to 1.5
- rate_table: float32 [8], replicated, may hold values from 0.3 to 3
- tile_owner: int32 [512], replicated, may hold values from 0 to 15
- node_cell: int32 [1048576], replicated, may hold values from 0 to 65535, as said below
Outputs:
- new_displacement: float32 [3, 64, 512, 2048], P(None, 'depth', 'tan')
The draws below stay inside these ranges and needn't reach their ends.
Inputs may be any that keep to these rules, and one draw needn't show every extreme that they name: `node_list`: row i lists 128 different surface nodes, all from i * 2048 to (i + 1) * 2048 - 1; only the first active_count[i] slots are in contact. `node_cell`: different nodes may share a cell.
All inputs are finite; a program needn't handle non-finite values.
Results may differ from the reference program's by a relative error of at most 0.00007.
Values sent between devices are 32-bit elements; how exact they have to be, the bound alone decides.
No kernel may reach another device: no remote copies, remote signals or barrier semaphores. Data moves between devices by JAX's collectives and lax.ppermute only.
A program may use at most 192 MiB of HBM per device.

```python
import math
import jax
import jax.numpy as jnp

CT = 32
W = 2048
TILE_DEV = 32
SLOTS = 128
NCLASS = 8
SWEEPS = 2
ND = 64
NT = 512
NSURF = 1048576
NTILE = 512
TILE_NODES = 2048
N_TAN = 16


def ensure_node(row, target):
    present = jnp.any(row == target)
    replaced = row.at[row.shape[0] - 1].set(target)
    return jnp.where(present, row, replaced)


def draw_node_list(key, part):
    keys = jax.random.split(jax.random.fold_in(key, 11), NTILE)
    chosen = jax.vmap(lambda single: jax.random.permutation(single, TILE_NODES)[:SLOTS])(keys)
    chosen = chosen.astype(jnp.int32)
    first_row = ensure_node(chosen[0], jnp.int32(0))
    final_row = ensure_node(chosen[NTILE - 1], jnp.int32(TILE_NODES - 1))
    chosen = chosen.at[0].set(first_row)
    chosen = chosen.at[NTILE - 1].set(final_row)
    offsets = jnp.arange(NTILE, dtype=jnp.int32)[:, None] * TILE_NODES
    return (chosen + offsets).astype(jnp.int32)


def draw_active_count(key, part):
    first_key, second_key = jax.random.split(jax.random.fold_in(key, 23))
    heat = jax.random.randint(first_key, (N_TAN,), 1, 4)
    upper = jnp.repeat(SLOTS * heat // 3, TILE_DEV)
    raw = jax.random.randint(second_key, (NTILE,), 0, 1048576)
    counts = 1 + raw % upper
    counts = counts.at[0].set(SLOTS)
    counts = counts.at[1].set(1)
    return counts.astype(jnp.int32)


def draw_tile_owner(key, part):
    owners = jax.random.randint(jax.random.fold_in(key, 37), (NTILE,), 0, N_TAN)
    owners = owners.at[0].set(N_TAN - 1)
    owners = owners.at[1].set(0)
    return owners.astype(jnp.int32)


def draw_node_cell(key, part):
    cells = jax.random.randint(jax.random.fold_in(key, 41), (NSURF,), 0, CT * W)
    cells = cells.at[0].set(CT * W - 1)
    cells = cells.at[1].set(0)
    return cells.astype(jnp.int32)


def with_ends(drawn, key, low, largest):
    dims = drawn.shape
    index_at = [jax.random.randint(jax.random.fold_in(key, axis), (), 0, dims[axis]) for axis in range(len(dims))]
    drawn = drawn.at[tuple(index_at)].set(low)
    longest = dims.index(max(dims))
    index_at[longest] = (index_at[longest] + 1) % dims[longest]
    return drawn.at[tuple(index_at)].set(largest)


def levels(rng, dims, cuts, smallest, top_value):
    loudness = 1.0
    for position, blocks in cuts:
        draws = jax.random.uniform(jax.random.fold_in(jax.random.fold_in(rng, 6), position), (blocks,), jnp.float32, smallest / len(cuts), top_value / len(cuts))
        loudness = loudness * jnp.repeat(jnp.exp(draws), dims[position] // blocks).reshape((-1,) + (1,) * (len(dims) - 1 - position))
    return loudness


def scatter_about(rng, dims, scale, most, shards=(), kind=jnp.bfloat16):
    array = scale * jax.random.normal(rng, dims, jnp.float32)
    if shards:
        array = array * levels(rng, dims, shards, -0.22, 0.18)
    return jnp.clip(array, -most, most).astype(kind)


def setup_inputs(seed: int = 0) -> dict:
    key_of = jax.random.split(jax.random.key(seed), 11)
    displacement = scatter_about(key_of[0], (3, ND, NT, W), 1.0, 6.0, ((1, 8), (2, 16)), jnp.float32)
    stiffness = jnp.clip(jnp.exp(math.log(8.0) - 2.7725887 * jax.random.uniform(key_of[1], (ND, NT, W), jnp.float32) ** levels(key_of[1], (ND, NT, W), ((0, 8), (1, 16)), -0.2, 0.2)), 0.5, 8.0)
    node_list = draw_node_list(jax.random.fold_in(key_of[10], 71), 0)
    active_count = draw_active_count(jax.random.fold_in(key_of[10], 71), 0)
    wear_class = with_ends(jax.random.randint(key_of[4], (NTILE, SLOTS), 0, NCLASS), jax.random.fold_in(key_of[4], 1), 0, NCLASS - 1).astype(jnp.int32)
    pressure = jnp.clip(jnp.exp(math.log(2.0) - 1.3862944 * jax.random.uniform(key_of[5], (NTILE, SLOTS), jnp.float32) ** levels(key_of[5], (NTILE, SLOTS), ((0, 16),), -0.2, 0.2)), 0.5, 2.0)
    slip_speed = jnp.clip(0.2 + 1.3 * jax.random.uniform(key_of[6], (NTILE, SLOTS), jnp.float32) ** levels(key_of[6], (NTILE, SLOTS), ((0, 16),), -0.2, 0.2), 0.2, 1.5)
    rate_table = jnp.clip(jnp.exp(jax.random.uniform(key_of[7], (NCLASS,), jnp.float32, math.log(0.3), math.log(3.0))), 0.3, 3.0)
    tile_owner = draw_tile_owner(jax.random.fold_in(key_of[10], 71), 0)
    node_cell = draw_node_cell(jax.random.fold_in(key_of[10], 71), 0)
    return dict(displacement=displacement, stiffness=stiffness, node_list=node_list, active_count=active_count, wear_class=wear_class, pressure=pressure, slip_speed=slip_speed, rate_table=rate_table, tile_owner=tile_owner, node_cell=node_cell)


wear_step = 0.6
hardness = 4.0


def relax(values, stiff_ext):
    padded = jnp.pad(values, ((0, 0), (0, 0), (0, 0), (1, 1)))
    stiff_pad = jnp.pad(stiff_ext, ((0, 0), (0, 0), (1, 1)))
    center = stiff_pad[1:-1, 1:-1, 1:-1]
    selectors = [
        (slice(2, None), slice(1, -1), slice(1, -1)),
        (slice(None, -2), slice(1, -1), slice(1, -1)),
        (slice(1, -1), slice(2, None), slice(1, -1)),
        (slice(1, -1), slice(None, -2), slice(1, -1)),
        (slice(1, -1), slice(1, -1), slice(2, None)),
        (slice(1, -1), slice(1, -1), slice(None, -2)),
    ]
    numerator = jnp.zeros((values.shape[0],) + center.shape, jnp.float32)
    denominator = jnp.zeros(center.shape, jnp.float32)
    for chosen in selectors:
        weight = 0.5 * (center + stiff_pad[chosen])
        numerator = numerator + weight[None] * padded[(slice(None),) + chosen]
        denominator = denominator + weight
    return numerator, denominator


def reference(displacement, stiffness, node_list, active_count, wear_class, pressure, slip_speed, rate_table, tile_owner, node_cell):
    slot_pos = jnp.arange(SLOTS)[None, :]
    rate = rate_table[wear_class]
    product = pressure * slip_speed
    wear_depth = wear_step * rate * product / (1.0 + product / hardness)
    wear_depth = jnp.where(slot_pos < active_count[:, None], wear_depth, 0.0)
    cell_index = tile_owner[:, None] * (CT * W) + node_cell[node_list]
    surface = jnp.zeros((NSURF,), jnp.float32).at[cell_index.reshape(-1)].add(wear_depth.reshape(-1))
    surface = surface.reshape(NT, W)
    field = displacement.at[0, 0].add(surface)
    pinned = field[0, 0]
    stiff_ext = jnp.pad(stiffness, ((1, 1), (1, 1), (0, 0)))
    for repeat in range(SWEEPS):
        values = jnp.pad(field, ((0, 0), (1, 1), (1, 1), (0, 0)))
        numerator, denominator = relax(values, stiff_ext)
        field = numerator / denominator[None]
        field = field.at[0, 0].set(pinned)
    return field
```

```python
import jax
import jax.numpy as jnp
from jax import lax
from jax.experimental import pallas as pl
from jax.experimental.pallas import tpu as pltpu
from jax.sharding import PartitionSpec as P

wear_step = 0.6
hardness = 4.0
GROUP = 8
VMEM_LIMIT = 48 * 1024 * 1024


def shift_both(last, first, axis):
    size = lax.axis_size(axis)
    up = [(i, i + 1) for i in range(size - 1)]
    down = [(j, i) for i, j in up]
    return lax.ppermute(last, axis, up), lax.ppermute(first, axis, down)


def archard(class_ids, contact, sliding, rates):
    classes = jnp.arange(rates.shape[0])
    rate = jnp.sum(jnp.where(class_ids[:, :, None] == classes, rates, 0.0), axis=-1)
    product = contact * sliding
    return wear_step * rate * product / (1.0 + product / hardness)


def three_parts(value):
    high = value.astype(jnp.bfloat16).astype(jnp.float32)
    rest = value - high
    middle = rest.astype(jnp.bfloat16).astype(jnp.float32)
    return high, middle, rest - middle


def paint_kernel(
    where_ref, owner_ref, count_ref, wear_ref, list_ref, table_ref, out_ref,
    own_ref, side_ref, acc_ref, edge_ref,
):
    slots = wear_ref.shape[1]
    ntile = wear_ref.shape[0]
    rows_table = table_ref.shape[0] // ntile
    tile_len = rows_table * 128
    width = out_ref.shape[1]
    rows = out_ref.shape[0] - 16
    me = where_ref[0]
    on_top = where_ref[1]
    out_ref[...] = jnp.zeros_like(out_ref)

    @pl.when(on_top == 1)
    def _():
        acc_ref[...] = jnp.zeros_like(acc_ref)
        edge_ref[...] = jnp.zeros_like(edge_ref)

        def collect(i, carry):
            n_own, n_side = carry
            offset = owner_ref[i] - me
            own_ref[n_own] = i
            side_ref[n_side] = i
            n_own = n_own + jnp.where(offset == 0, 1, 0)
            n_side = n_side + jnp.where(offset * offset == 1, 1, 0)
            return n_own, n_side

        n_own, n_side = lax.fori_loop(
            0, ntile, collect, (jnp.int32(0), jnp.int32(0)), unroll=8
        )

        lane = lax.broadcasted_iota(jnp.int32, (1, slots), 1)
        table_row = lax.broadcasted_iota(jnp.int32, (rows_table, slots), 0)
        block = width // 8
        fine = lax.broadcasted_iota(jnp.int32, (block, slots), 0)
        coarse = lax.broadcasted_iota(jnp.int32, (rows * 8, slots), 0)
        fine_edge = lax.broadcasted_iota(jnp.int32, (128, slots), 0)
        edge_blocks = width // 128
        coarse_edge = lax.broadcasted_iota(jnp.int32, (2 * edge_blocks, slots), 0)

        def entry(tiles_ref, position, total):
            i = tiles_ref[jnp.minimum(position, total - 1)]
            live = jnp.where(position < total, count_ref[i], 0)
            local = list_ref[pl.ds(i, 1), :] - i * tile_len
            table = table_ref[pl.ds(pl.multiple_of(i * rows_table, 8), rows_table), :]
            column = jnp.broadcast_to(local & 127, (rows_table, slots))
            picked = jnp.take_along_axis(table, column, axis=1)
            cell = jnp.sum(
                jnp.where(table_row == (local >> 7), picked, 0), axis=0, keepdims=True
            )
            wear = jnp.where(lane < live, wear_ref[pl.ds(i, 1), :], 0.0)
            return i, cell, wear

        def one_hot(mask, value):
            return jnp.where(mask, value, 0.0).astype(jnp.bfloat16)

        def add(into_ref, parts, hot):
            total = into_ref[...]
            for part in parts:
                total = total + lax.dot_general(
                    jnp.concatenate(part, axis=1), hot, (((1,), (1,)), ((), ())),
                    preferred_element_type=jnp.float32,
                )
            into_ref[...] = total

        def own_group(g, carry):
            parts = ([], [], [])
            hots = []
            for j in range(GROUP):
                _, cell, wear = entry(own_ref, g * GROUP + j, n_own)
                col = cell % width
                a_index = (col // block) * rows + cell // width
                hots.append(one_hot(fine == col % block, 1.0))
                mask = coarse == a_index
                for part, value in zip(parts, three_parts(wear)):
                    part.append(one_hot(mask, value))
            add(acc_ref, parts, jnp.concatenate(hots, axis=1))
            return carry

        def side_group(g, carry):
            parts = ([], [], [])
            hots = []
            for j in range(GROUP):
                i, cell, wear = entry(side_ref, g * GROUP + j, n_side)
                below = owner_ref[i] > me
                col = cell % width
                wanted = jnp.where(below, 0, rows - 1)
                shift = jnp.where(below, edge_blocks, 0)
                a_index = jnp.where(cell // width == wanted, col // 128 + shift, -1)
                hots.append(one_hot(fine_edge == col % 128, 1.0))
                mask = coarse_edge == a_index
                for part, value in zip(parts, three_parts(wear)):
                    part.append(one_hot(mask, value))
            add(edge_ref, parts, jnp.concatenate(hots, axis=1))
            return carry

        lax.fori_loop(0, (n_own + GROUP - 1) // GROUP, own_group, 0)
        lax.fori_loop(0, (n_side + GROUP - 1) // GROUP, side_group, 0)
        for j in range(8):
            out_ref[8 : 8 + rows, j * block : (j + 1) * block] = acc_ref[
                j * rows : (j + 1) * rows, :
            ]
        for j in range(edge_blocks):
            out_ref[7:8, j * 128 : (j + 1) * 128] = edge_ref[j : j + 1, :]
            out_ref[8 + rows : 9 + rows, j * 128 : (j + 1) * 128] = edge_ref[
                edge_blocks + j : edge_blocks + j + 1, :
            ]


def paint(position, owner, counts, wear, lists, table, rows, width):
    ntile, slots = lists.shape
    whole = lambda shape: pl.BlockSpec(shape, lambda i, *_: (0,) * len(shape))
    return pl.pallas_call(
        paint_kernel,
        name="paint_band",
        grid_spec=pltpu.PrefetchScalarGridSpec(
            num_scalar_prefetch=3,
            grid=(1,),
            in_specs=[whole(wear.shape), whole(lists.shape), whole(table.shape)],
            out_specs=whole((rows + 16, width)),
            scratch_shapes=[
                pltpu.SMEM((ntile + 1,), jnp.int32),
                pltpu.SMEM((ntile + 1,), jnp.int32),
                pltpu.VMEM((rows * 8, width // 8), jnp.float32),
                pltpu.VMEM((2 * width // 128, 128), jnp.float32),
            ],
        ),
        out_shape=jax.ShapeDtypeStruct((rows + 16, width), jnp.float32),
        compiler_params=pltpu.CompilerParams(vmem_limit_bytes=VMEM_LIMIT),
    )(position, owner, counts, wear, lists, table)


def relax_tile(load, edge_before, edge_after, t, ntiles):
    row = lax.broadcasted_iota(jnp.int32, (8, 1), 0)
    centers = {}

    def neighbours(c):
        here = load(c, 0, t)
        centers[c] = here
        width = here.shape[1]
        lane = lax.broadcasted_iota(jnp.int32, here.shape, 1)
        above = load(c, 0, t - 1)[7:8] if t > 0 else edge_before(c)
        below = load(c, 0, t + 1)[0:1] if t < ntiles - 1 else edge_after(c)
        yield load(c, 1, t)
        yield load(c, -1, t)
        yield jnp.where(row == 7, below, pltpu.roll(here, 7, 0))
        yield jnp.where(row == 0, above, pltpu.roll(here, 1, 0))
        yield jnp.where(lane == width - 1, 0.0, pltpu.roll(here, width - 1, 1))
        yield jnp.where(lane == 0, 0.0, pltpu.roll(here, 1, 1))

    around = list(neighbours(3))
    weights = [centers[3] + s for s in around]
    total = weights[0]
    for w in weights[1:]:
        total = total + w
    inverse = 1.0 / total
    outs = []
    for c in range(3):
        acc = None
        for w, f in zip(weights, neighbours(c)):
            acc = w * f if acc is None else acc + w * f
        outs.append(acc * inverse)
    return outs, centers


def inner_kernel(with_surface, with_rows, *refs):
    (low, mid, high, s_low, s_mid, s_high, before, after, s_before, s_after) = refs[:10]
    rest = list(refs[10:])
    surface = rest.pop(0) if with_surface else None
    out = rest.pop(0)
    layer = pl.program_id(0) + 1
    ntiles = mid.shape[2] // 8
    f_refs = {-1: low, 0: mid, 1: high}
    s_refs = {-1: s_low, 0: s_mid, 1: s_high}
    if with_rows:
        first_row, last_row = rest

        @pl.when(layer == 1)
        def _():
            first_row[...] = jnp.zeros_like(first_row)
            last_row[...] = jnp.zeros_like(last_row)

    scale = jnp.where(layer == 1, 1.0, 0.0)

    def load(c, side, t):
        if c == 3:
            return s_refs[side][0, 8 * t : 8 * t + 8, :]
        value = f_refs[side][c, 0, 8 * t : 8 * t + 8, :]
        if with_surface and c == 0 and side == -1:
            value = value + scale * surface[8 * t + 8 : 8 * t + 16, :]
        return value

    def edge(f_ref, s_ref):
        return lambda c: s_ref[3, pl.ds(layer, 1), :] if c == 3 else f_ref[c, pl.ds(layer, 1), :]

    for t in range(ntiles):
        outs, _ = relax_tile(load, edge(before, s_before), edge(after, s_after), t, ntiles)
        for c in range(3):
            out[c, 0, 8 * t : 8 * t + 8, :] = outs[c]
            if with_rows and t == 0:
                first_row[c, pl.ds(layer, 1), :] = outs[c][0:1]
            if with_rows and t == ntiles - 1:
                last_row[c, pl.ds(layer, 1), :] = outs[c][7:8]


def relax_inner(field, stiffness, before, after, s_before, s_after, surface):
    _, layers, rows, width = field.shape
    with_surface = surface is not None
    whole = lambda shape: pl.BlockSpec(shape, lambda i: (0,) * len(shape))
    f_spec = lambda k: pl.BlockSpec((3, 1, rows, width), lambda i: (0, i + k, 0, 0))
    s_spec = lambda k: pl.BlockSpec((1, rows, width), lambda i: (i + k, 0, 0))
    args = [field] * 3 + [stiffness] * 3 + [before, after, s_before, s_after]
    in_specs = [f_spec(k) for k in range(3)] + [s_spec(k) for k in range(3)]
    in_specs += [whole(a.shape) for a in args[6:]]
    out_shape = [jax.ShapeDtypeStruct(field.shape, jnp.float32)]
    out_specs = [f_spec(1)]
    if with_surface:
        args.append(surface)
        in_specs.append(whole(surface.shape))
        out_shape += [jax.ShapeDtypeStruct((3, layers, width), jnp.float32)] * 2
        out_specs += [whole((3, layers, width))] * 2
    return pl.pallas_call(
        lambda *refs: inner_kernel(with_surface, with_surface, *refs),
        name="relax_inner_first" if with_surface else "relax_inner_second",
        grid=(layers - 2,),
        in_specs=in_specs,
        out_specs=out_specs,
        out_shape=out_shape,
        compiler_params=pltpu.CompilerParams(vmem_limit_bytes=VMEM_LIMIT),
    )(*args)


def face_kernel(first_sweep, rows_at, *refs):
    (where_ref, here, inside, s_here, s_inside, low, high, s_low, s_high,
     before, after, s_before, s_after) = refs[:13]
    rest = list(refs[13:])
    surface = rest.pop(0) if first_sweep else None
    rest.pop(0)
    out = rest.pop(0)
    ntiles = here.shape[2] // 8
    on_top = where_ref[1] == 1

    def one(face, outer, s_outer, sends):
        layer = 0 if face == 0 else s_before.shape[1] - 1

        def load(c, side, t):
            at = slice(8 * t, 8 * t + 8)
            if side == 1:
                return s_outer[3, at, :] if c == 3 else outer[c, at, :]
            if side == -1:
                return s_inside[0, at, :] if c == 3 else inside[c, 0, at, :]
            value = s_here[0, at, :] if c == 3 else here[c, 0, at, :]
            if first_sweep and c == 0 and face == 0:
                value = value + surface[8 * t + 8 : 8 * t + 16, :]
            return value

        def edge(f_ref, s_ref, surface_row):
            def get(c):
                if c == 3:
                    return s_ref[3, layer : layer + 1, :]
                if not first_sweep:
                    return f_ref[2 * c + face : 2 * c + face + 1, :]
                value = f_ref[c, layer : layer + 1, :]
                if c == 0 and face == 0:
                    value = value + surface[surface_row : surface_row + 1, :]
                return value
            return get

        for t in range(ntiles):
            outs, centers = relax_tile(
                load, edge(before, s_before, 7), edge(after, s_after, 8 + 8 * ntiles), t, ntiles
            )
            if face == 0:
                outs[0] = jnp.where(on_top, centers[0], outs[0])
            for c in range(3):
                out[c, 0, 8 * t : 8 * t + 8, :] = outs[c]
                if first_sweep:
                    send, first_row, last_row = sends
                    send[c, 8 * t : 8 * t + 8, :] = outs[c]
                    k = 2 * c + face
                    if t == 0:
                        first_row[k : k + 1, :] = outs[c][0:1]
                    if t == ntiles - 1:
                        last_row[k : k + 1, :] = outs[c][7:8]

    step = pl.program_id(0)

    @pl.when(step == 0)
    def _():
        if first_sweep:
            rest[2][6:8, :] = jnp.zeros_like(rest[2][6:8, :])
            rest[3][6:8, :] = jnp.zeros_like(rest[3][6:8, :])
        one(0, low, s_low, (rest[0], rest[2], rest[3]) if first_sweep else None)

    @pl.when(step == 1)
    def _():
        one(1, high, s_high, (rest[1], rest[2], rest[3]) if first_sweep else None)


def relax_faces(position, field, stiffness, low, high, s_low, s_high,
                before, after, s_before, s_after, surface, partial):
    _, layers, rows, width = field.shape
    first_sweep = surface is not None
    whole = lambda shape: pl.BlockSpec(shape, lambda i, *_: (0,) * len(shape))
    f_spec = lambda at: pl.BlockSpec((3, 1, rows, width), lambda i, *_: (0, at(i), 0, 0))
    s_spec = lambda at: pl.BlockSpec((1, rows, width), lambda i, *_: (at(i), 0, 0))
    outermost = lambda i: i * (layers - 1)
    inner = lambda i: 1 + i * (layers - 3)
    args = [field, field, stiffness, stiffness, low, high, s_low, s_high,
            before, after, s_before, s_after]
    in_specs = [f_spec(outermost), f_spec(inner), s_spec(outermost), s_spec(inner)]
    in_specs += [whole(a.shape) for a in args[4:]]
    out_shape = [jax.ShapeDtypeStruct(field.shape, jnp.float32)]
    out_specs = [f_spec(outermost)]
    if first_sweep:
        args.append(surface)
        in_specs.append(whole(surface.shape))
        plane = (3, rows, width)
        out_shape += [jax.ShapeDtypeStruct(plane, jnp.float32)] * 2
        out_shape += [jax.ShapeDtypeStruct((8, width), jnp.float32)] * 2
        out_specs += [whole(plane)] * 2 + [whole((8, width))] * 2
    args.append(partial)
    in_specs.append(pl.BlockSpec(memory_space=pl.ANY))
    return pl.pallas_call(
        lambda *refs: face_kernel(first_sweep, None, *refs),
        name="relax_faces_first" if first_sweep else "relax_faces_second",
        grid_spec=pltpu.PrefetchScalarGridSpec(
            num_scalar_prefetch=1, grid=(2,), in_specs=in_specs, out_specs=out_specs
        ),
        out_shape=out_shape,
        input_output_aliases={len(args): 0},
        compiler_params=pltpu.CompilerParams(vmem_limit_bytes=VMEM_LIMIT),
    )(position, *args)


def per_device(
    displacement,
    stiffness,
    node_list,
    active_count,
    wear_class,
    pressure,
    slip_speed,
    rate_table,
    tile_owner,
    node_cell,
):
    rows, width = displacement.shape[2:]
    position = jnp.stack(
        [lax.axis_index("tan"), (lax.axis_index("depth") == 0).astype(jnp.int32)]
    ).astype(jnp.int32)

    def joined(cut):
        return jnp.concatenate([cut(displacement), cut(stiffness[None])], axis=0)

    low, high = shift_both(joined(lambda a: a[:, -1]), joined(lambda a: a[:, 0]), "depth")
    before, after = shift_both(
        joined(lambda a: a[:, :, -1]), joined(lambda a: a[:, :, 0]), "tan"
    )
    wear = archard(wear_class, pressure, slip_speed, rate_table)
    wear = lax.all_gather(wear, "tan", axis=0, tiled=True)
    surface = paint(position, tile_owner, active_count, wear, node_list,
                    node_cell.reshape(-1, 128), rows, width)

    first, row_first, row_last = relax_inner(
        displacement, stiffness, before, after, before, after, surface
    )
    before_mid, after_mid = shift_both(row_last, row_first, "tan")
    first, send_low, send_high, edge_first, edge_last = relax_faces(
        position, displacement, stiffness, low, high, low, high,
        before, after, before, after, surface, first,
    )
    low_2, high_2 = shift_both(send_high, send_low, "depth")
    before_face, after_face = shift_both(edge_last, edge_first, "tan")
    result = relax_inner(first, stiffness, before_mid, after_mid, before, after, None)[0]
    return relax_faces(
        position, first, stiffness, low_2, high_2, low, high,
        before_face, after_face, before, after, None, result,
    )[0]


def solution(mesh):
    in_specs = (
        P(None, "depth", "tan", None),
        P("depth", "tan", None),
        P(),
        P(),
        P("tan", None),
        P("tan", None),
        P("tan", None),
        P(),
        P(),
        P(),
    )
    out_specs = P(None, "depth", "tan", None)
    return jax.shard_map(
        per_device, mesh=mesh, in_specs=in_specs, out_specs=out_specs, check_vma=False
    )
```

```python
import functools

import jax
import jax.numpy as jnp
from jax import lax
from jax.experimental import pallas as pl
from jax.experimental.pallas import tpu as pltpu
from jax.sharding import PartitionSpec as P

wear_step = 0.6
hardness = 4.0
GROUP = 8
VMEM_LIMIT = 48 * 1024 * 1024


def shift_both(last, first, axis):
    size = lax.axis_size(axis)
    up = [(i, i + 1) for i in range(size - 1)]
    down = [(j, i) for i, j in up]
    return lax.ppermute(last, axis, up), lax.ppermute(first, axis, down)


def wear_kernel(rates_ref, class_ref, contact_ref, sliding_ref, wear_ref):
    ids = class_ref[...]
    rate = jnp.zeros(ids.shape, jnp.float32)
    for k in range(rates_ref.shape[0]):
        rate = jnp.where(ids == k, rates_ref[k], rate)
    product = contact_ref[...] * sliding_ref[...]
    wear_ref[...] = wear_step * rate * product / (1.0 + product / hardness)


def archard(class_ids, contact, sliding, rates):
    near = pl.BlockSpec(memory_space=pltpu.VMEM)
    return pl.pallas_call(
        wear_kernel,
        name="archard",
        in_specs=[pl.BlockSpec(memory_space=pltpu.SMEM), near, near, near],
        out_specs=near,
        out_shape=jax.ShapeDtypeStruct(contact.shape, jnp.float32),
    )(rates, class_ids, contact, sliding)


def pack_kernel(field_ref, stiff_ref, wear_ref, first_ref, last_ref, sems):
    layers = field_ref.shape[1]
    copies = []
    for k, (to, layer) in enumerate(((last_ref, layers - 1), (first_ref, 0))):
        copies.append(pltpu.make_async_copy(
            field_ref.at[:, layer], to.at[pl.ds(0, 3)], sems.at[2 * k]))
        copies.append(pltpu.make_async_copy(
            stiff_ref.at[pl.ds(layer, 1)], to.at[pl.ds(3, 1)], sems.at[2 * k + 1]))
    for copy in copies:
        copy.start()
    for copy in copies:
        copy.wait()


def pack_faces(field, stiffness, wear):
    _, _, rows, width = field.shape
    face = jax.ShapeDtypeStruct((4, rows, width), jnp.float32)
    far = pl.BlockSpec(memory_space=pl.ANY)
    return pl.pallas_call(
        pack_kernel,
        name="pack_faces",
        in_specs=[far, far, far],
        out_specs=[far, far],
        out_shape=[face, face],
        scratch_shapes=[pltpu.SemaphoreType.DMA((4,))],
    )(field, stiffness, wear)


def rows_kernel(f_top, s_top, f_bottom, s_bottom, first_ref, last_ref):
    for l in range(f_top.shape[1]):
        first_ref[3, l : l + 1, :] = s_top[l, 0:1, :]
        last_ref[3, l : l + 1, :] = s_bottom[l, 7:8, :]
        for c in range(3):
            first_ref[c, l : l + 1, :] = f_top[c, l, 0:1, :]
            last_ref[c, l : l + 1, :] = f_bottom[c, l, 7:8, :]


def pack_rows(field, stiffness):
    _, layers, rows, width = field.shape
    bottom = rows // 8 - 1
    f_spec = lambda at: pl.BlockSpec((3, layers, 8, width), lambda i: (0, 0, at, 0))
    s_spec = lambda at: pl.BlockSpec((layers, 8, width), lambda i: (0, at, 0))
    out = jax.ShapeDtypeStruct((4, layers, width), jnp.float32)
    out_spec = pl.BlockSpec((4, layers, width), lambda i: (0, 0, 0))
    return pl.pallas_call(
        rows_kernel,
        name="pack_rows",
        grid=(1,),
        in_specs=[f_spec(0), s_spec(0), f_spec(bottom), s_spec(bottom)],
        out_specs=[out_spec, out_spec],
        out_shape=[out, out],
        compiler_params=pltpu.CompilerParams(vmem_limit_bytes=VMEM_LIMIT),
    )(field, stiffness, field, stiffness)


def swap_halves(wear):
    size = lax.axis_size("tan")
    return lax.ppermute(wear, "tan", [(i, i ^ 2) for i in range(size)])


def gather_wear(wear, other):
    size = lax.axis_size("tan")
    both = jnp.concatenate([wear, other], axis=0)
    groups = [[i for i in range(size) if (i // 2) % 2 == half] for half in range(2)]
    return lax.all_gather(both, "tan", axis=0, axis_index_groups=groups, tiled=True)


def three_parts(value):
    high = value.astype(jnp.bfloat16).astype(jnp.float32)
    rest = value - high
    middle = rest.astype(jnp.bfloat16).astype(jnp.float32)
    return high, middle, rest - middle


def paint_kernel(
    shard_tiles, where_ref, owner_ref, count_ref, wear_ref, list_ref, table_ref, out_ref,
    own_ref, side_ref, acc_ref, edge_ref,
):
    slots = wear_ref.shape[1]
    ntile = wear_ref.shape[0]
    rows_table = table_ref.shape[0] // ntile
    tile_len = rows_table * 128
    width = out_ref.shape[1]
    rows = out_ref.shape[0] - 16
    me = where_ref[0]
    on_top = where_ref[1]
    out_ref[...] = jnp.zeros_like(out_ref)

    @pl.when(on_top == 1)
    def _():
        acc_ref[...] = jnp.zeros_like(acc_ref)
        edge_ref[...] = jnp.zeros_like(edge_ref)

        def collect(i, carry):
            n_own, n_side = carry
            offset = owner_ref[i] - me
            own_ref[n_own] = i
            side_ref[n_side] = i
            n_own = n_own + jnp.where(offset == 0, 1, 0)
            n_side = n_side + jnp.where(offset * offset == 1, 1, 0)
            return n_own, n_side

        n_own, n_side = lax.fori_loop(
            0, ntile, collect, (jnp.int32(0), jnp.int32(0)), unroll=8
        )

        lane = lax.broadcasted_iota(jnp.int32, (1, slots), 1)
        table_row = lax.broadcasted_iota(jnp.int32, (rows_table, slots), 0)
        block = width // 8
        fine = lax.broadcasted_iota(jnp.int32, (block, slots), 0)
        coarse = lax.broadcasted_iota(jnp.int32, (rows * 8, slots), 0)
        fine_edge = lax.broadcasted_iota(jnp.int32, (128, slots), 0)
        edge_blocks = width // 128
        coarse_edge = lax.broadcasted_iota(jnp.int32, (2 * edge_blocks, slots), 0)

        def entry(tiles_ref, position, total):
            i = tiles_ref[jnp.minimum(position, total - 1)]
            live = jnp.where(position < total, count_ref[i], 0)
            local = list_ref[pl.ds(i, 1), :] - i * tile_len
            table = table_ref[pl.ds(pl.multiple_of(i * rows_table, 8), rows_table), :]
            column = jnp.broadcast_to(local & 127, (rows_table, slots))
            picked = jnp.take_along_axis(table, column, axis=1)
            cell = jnp.sum(
                jnp.where(table_row == (local >> 7), picked, 0), axis=0, keepdims=True
            )
            shard = i // shard_tiles
            half = jnp.where((shard // 2) % 2 == (me // 2) % 2, 0, 1)
            place = (shard // 4) * 4 + (shard % 2) * 2 + half
            at = place * shard_tiles + i % shard_tiles
            wear = jnp.where(lane < live, wear_ref[pl.ds(at, 1), :], 0.0)
            return i, cell, wear

        def one_hot(mask, value):
            return jnp.where(mask, value, 0.0).astype(jnp.bfloat16)

        def add(into_ref, parts, hot):
            total = into_ref[...]
            for part in parts:
                total = total + lax.dot_general(
                    jnp.concatenate(part, axis=1), hot, (((1,), (1,)), ((), ())),
                    preferred_element_type=jnp.float32,
                )
            into_ref[...] = total

        def own_group(g, carry):
            parts = ([], [], [])
            hots = []
            for j in range(GROUP):
                _, cell, wear = entry(own_ref, g * GROUP + j, n_own)
                col = cell % width
                a_index = (col // block) * rows + cell // width
                hots.append(one_hot(fine == col % block, 1.0))
                mask = coarse == a_index
                for part, value in zip(parts, three_parts(wear)):
                    part.append(one_hot(mask, value))
            add(acc_ref, parts, jnp.concatenate(hots, axis=1))
            return carry

        def side_group(g, carry):
            parts = ([], [], [])
            hots = []
            for j in range(GROUP):
                i, cell, wear = entry(side_ref, g * GROUP + j, n_side)
                below = owner_ref[i] > me
                col = cell % width
                wanted = jnp.where(below, 0, rows - 1)
                shift = jnp.where(below, edge_blocks, 0)
                a_index = jnp.where(cell // width == wanted, col // 128 + shift, -1)
                hots.append(one_hot(fine_edge == col % 128, 1.0))
                mask = coarse_edge == a_index
                for part, value in zip(parts, three_parts(wear)):
                    part.append(one_hot(mask, value))
            add(edge_ref, parts, jnp.concatenate(hots, axis=1))
            return carry

        lax.fori_loop(0, (n_own + GROUP - 1) // GROUP, own_group, 0)
        lax.fori_loop(0, (n_side + GROUP - 1) // GROUP, side_group, 0)
        for j in range(8):
            out_ref[8 : 8 + rows, j * block : (j + 1) * block] = acc_ref[
                j * rows : (j + 1) * rows, :
            ]
        for j in range(edge_blocks):
            out_ref[7:8, j * 128 : (j + 1) * 128] = edge_ref[j : j + 1, :]
            out_ref[8 + rows : 9 + rows, j * 128 : (j + 1) * 128] = edge_ref[
                edge_blocks + j : edge_blocks + j + 1, :
            ]


def paint(position, owner, counts, wear, lists, table, rows, width, shard_tiles):
    ntile, slots = lists.shape
    whole = lambda shape: pl.BlockSpec(shape, lambda i, *_: (0,) * len(shape))
    return pl.pallas_call(
        functools.partial(paint_kernel, shard_tiles),
        name="paint_band",
        grid_spec=pltpu.PrefetchScalarGridSpec(
            num_scalar_prefetch=3,
            grid=(1,),
            in_specs=[whole(wear.shape), whole(lists.shape), whole(table.shape)],
            out_specs=whole((rows + 16, width)),
            scratch_shapes=[
                pltpu.SMEM((ntile + 1,), jnp.int32),
                pltpu.SMEM((ntile + 1,), jnp.int32),
                pltpu.VMEM((rows * 8, width // 8), jnp.float32),
                pltpu.VMEM((2 * width // 128, 128), jnp.float32),
            ],
        ),
        out_shape=jax.ShapeDtypeStruct((rows + 16, width), jnp.float32),
        compiler_params=pltpu.CompilerParams(vmem_limit_bytes=VMEM_LIMIT),
    )(position, owner, counts, wear, lists, table)


def relax_tile(load, row_above, row_below):
    row = lax.broadcasted_iota(jnp.int32, (8, 1), 0)
    centers = {}

    def neighbours(c):
        here = load(c, 0)
        centers[c] = here
        width = here.shape[1]
        lane = lax.broadcasted_iota(jnp.int32, here.shape, 1)
        yield load(c, 1)
        yield load(c, -1)
        yield jnp.where(row == 7, row_below(c), pltpu.roll(here, 7, 0))
        yield jnp.where(row == 0, row_above(c), pltpu.roll(here, 1, 0))
        yield jnp.where(lane == width - 1, 0.0, pltpu.roll(here, width - 1, 1))
        yield jnp.where(lane == 0, 0.0, pltpu.roll(here, 1, 1))

    around = list(neighbours(3))
    weights = [centers[3] + s for s in around]
    total = weights[0]
    for w in weights[1:]:
        total = total + w
    inverse = 1.0 / total
    outs = []
    for c in range(3):
        acc = None
        for w, f in zip(weights, neighbours(c)):
            acc = w * f if acc is None else acc + w * f
        outs.append(acc * inverse)
    return outs, centers


def inner_kernel(first_sweep, *refs):
    (low, mid, high, s_low, s_mid, s_high, before, after, s_before, s_after) = refs[:10]
    rest = list(refs[10:])
    surface = rest.pop(0) if first_sweep else None
    out = rest.pop(0)
    layer = pl.program_id(0) + 1
    ntiles = mid.shape[2] // 8
    f_refs = {-1: low, 0: mid, 1: high}
    s_refs = {-1: s_low, 0: s_mid, 1: s_high}
    if first_sweep:
        first_row, last_row = rest

        @pl.when(layer == 1)
        def _():
            first_row[...] = jnp.zeros_like(first_row)
            last_row[...] = jnp.zeros_like(last_row)

    scale = jnp.where(layer == 1, 1.0, 0.0)

    for t in range(ntiles):

        def load(c, side):
            if c == 3:
                return s_refs[side][0, 8 * t : 8 * t + 8, :]
            value = f_refs[side][c, 0, 8 * t : 8 * t + 8, :]
            if first_sweep and c == 0 and side == -1:
                value = value + scale * surface[8 * t + 8 : 8 * t + 16, :]
            return value

        def beside(inside, at, f_edge, s_edge):
            def get(c):
                if inside:
                    return s_mid[0, at : at + 1, :] if c == 3 else mid[c, 0, at : at + 1, :]
                edge = s_edge.at[0] if c == 3 else f_edge.at[c]
                return edge[pl.ds(layer, 1), :]
            return get

        outs, _ = relax_tile(
            load,
            beside(t > 0, 8 * t - 1, before, s_before),
            beside(t < ntiles - 1, 8 * t + 8, after, s_after),
        )
        for c in range(3):
            out[c, 0, 8 * t : 8 * t + 8, :] = outs[c]
            if first_sweep and t == 0:
                first_row[c, pl.ds(layer, 1), :] = outs[c][0:1]
            if first_sweep and t == ntiles - 1:
                last_row[c, pl.ds(layer, 1), :] = outs[c][7:8]


def relax_inner(field, stiffness, before, after, s_before, s_after, surface):
    _, layers, rows, width = field.shape
    first_sweep = surface is not None
    whole = lambda shape: pl.BlockSpec(shape, lambda i: (0,) * len(shape))
    f_spec = lambda k: pl.BlockSpec((3, 1, rows, width), lambda i: (0, i + k, 0, 0))
    s_spec = lambda k: pl.BlockSpec((1, rows, width), lambda i: (i + k, 0, 0))
    f_edge = whole((3, layers, width))
    s_edge = pl.BlockSpec((1, layers, width), lambda i: (3, 0, 0))
    args = [field] * 3 + [stiffness] * 3 + [before, after, s_before, s_after]
    in_specs = [f_spec(k) for k in range(3)] + [s_spec(k) for k in range(3)]
    in_specs += [f_edge, f_edge, s_edge, s_edge]
    out_shape = [jax.ShapeDtypeStruct(field.shape, jnp.float32)]
    out_specs = [f_spec(1)]
    if first_sweep:
        args.append(surface)
        in_specs.append(whole(surface.shape))
        out_shape += [jax.ShapeDtypeStruct((3, layers, width), jnp.float32)] * 2
        out_specs += [f_edge] * 2
    return pl.pallas_call(
        functools.partial(inner_kernel, first_sweep),
        name="relax_inner_first" if first_sweep else "relax_inner_second",
        grid=(layers - 2,),
        in_specs=in_specs,
        out_specs=out_specs,
        out_shape=out_shape,
        compiler_params=pltpu.CompilerParams(vmem_limit_bytes=VMEM_LIMIT),
    )(*args)


def face_kernel(first_sweep, *refs):
    (where_ref, here, inside, s_here, s_inside, low, high, s_low, s_high,
     before, after, s_before, s_after) = refs[:13]
    rest = list(refs[13:])
    if first_sweep:
        surface, _, rows_in_first, rows_in_last, out = rest[:5]
        first_row, last_row, send_low, send_high = rest[5:]
    else:
        _, out = rest
    face = pl.program_id(0)
    t = pl.program_id(1)
    ntiles = here.shape[2] // 8
    layer = face * (before.shape[1] - 1)
    start = pl.multiple_of(8 * t, 8)
    pinned = jnp.logical_and(where_ref[1] == 1, face == 0)
    scale = jnp.where(face == 0, 1.0, 0.0)

    if first_sweep:
        @pl.when(jnp.logical_and(face == 0, t == 0))
        def _():
            first_row[...] = rows_in_first[...]
            last_row[...] = rows_in_last[...]

    def one(outer, s_outer, send):
        def load(c, side):
            if side == 1:
                return s_outer[0] if c == 3 else outer[c]
            if side == -1:
                return s_inside[0] if c == 3 else inside[c, 0]
            if c == 3:
                return s_here[0, pl.ds(start, 8), :]
            value = here[c, 0, pl.ds(start, 8), :]
            if first_sweep and c == 0:
                value = value + scale * surface[pl.ds(start + 8, 8), :]
            return value

        def beside(is_inside, at, f_edge, s_edge, surface_at):
            kept = jnp.clip(at, 0, 8 * ntiles - 1)

            def get(c):
                if c == 3:
                    near = s_here[0, pl.ds(kept, 1), :]
                    edge = s_edge[0, pl.ds(layer, 1), :]
                else:
                    near = here[c, 0, pl.ds(kept, 1), :]
                    edge = f_edge[c, pl.ds(layer, 1), :]
                value = jnp.where(is_inside, near, edge)
                if first_sweep and c == 0:
                    value = value + scale * surface[pl.ds(surface_at, 1), :]
                return value

            return get

        outs, centers = relax_tile(
            load,
            beside(t > 0, 8 * t - 1, before, s_before, 8 * t + 7),
            beside(t < ntiles - 1, 8 * t + 8, after, s_after, 8 * t + 16),
        )
        outs[0] = jnp.where(pinned, centers[0], outs[0])
        for c in range(3):
            out[c, 0] = outs[c]
            if first_sweep:
                send[c] = outs[c]
        if first_sweep:
            @pl.when(t == 0)
            def _():
                for c in range(3):
                    first_row[c, pl.ds(layer, 1), :] = outs[c][0:1]

            @pl.when(t == ntiles - 1)
            def _():
                for c in range(3):
                    last_row[c, pl.ds(layer, 1), :] = outs[c][7:8]

    @pl.when(face == 0)
    def _():
        one(low, s_low, send_low if first_sweep else None)

    @pl.when(face == 1)
    def _():
        one(high, s_high, send_high if first_sweep else None)


def relax_faces(position, field, stiffness, low, high, s_low, s_high,
                before, after, s_before, s_after, surface, partial):
    _, layers, rows, width = field.shape
    ntiles = rows // 8
    first_sweep = surface is not None
    whole = lambda shape: pl.BlockSpec(shape, lambda i, t, *_: (0,) * len(shape))
    outermost = lambda i: i * (layers - 1)
    inner = lambda i: 1 + i * (layers - 3)
    low_at = lambda i, t: jnp.where(i == 0, t, ntiles - 1)
    high_at = lambda i, t: jnp.where(i == 0, 0, t)
    plane = lambda at: pl.BlockSpec((3, 8, width), lambda i, t, *_: (0, at(i, t), 0))
    s_plane = lambda at: pl.BlockSpec((1, 8, width), lambda i, t, *_: (3, at(i, t), 0))
    f_edge = whole((3, layers, width))
    s_edge = pl.BlockSpec((1, layers, width), lambda i, t, *_: (3, 0, 0))
    f_out = pl.BlockSpec((3, 1, 8, width), lambda i, t, *_: (0, outermost(i), t, 0))
    args = [field, field, stiffness, stiffness, low, high, s_low, s_high,
            before, after, s_before, s_after]
    in_specs = [
        pl.BlockSpec((3, 1, rows, width), lambda i, t, *_: (0, outermost(i), 0, 0)),
        pl.BlockSpec((3, 1, 8, width), lambda i, t, *_: (0, inner(i), t, 0)),
        pl.BlockSpec((1, rows, width), lambda i, t, *_: (outermost(i), 0, 0)),
        pl.BlockSpec((1, 8, width), lambda i, t, *_: (inner(i), t, 0)),
        plane(low_at), plane(high_at), s_plane(low_at), s_plane(high_at),
        f_edge, f_edge, s_edge, s_edge,
    ]
    out_shape = [jax.ShapeDtypeStruct(field.shape, jnp.float32)]
    out_specs = [f_out]
    if first_sweep:
        args.append(surface)
        in_specs.append(whole(surface.shape))
    aliases = {len(args) + 1: 0}
    args.append(partial[0])
    in_specs.append(pl.BlockSpec(memory_space=pl.ANY))
    if first_sweep:
        aliases.update({len(args) + 1: 1, len(args) + 2: 2})
        args += partial[1:]
        in_specs += [f_edge, f_edge]
        out_shape += [jax.ShapeDtypeStruct((3, layers, width), jnp.float32)] * 2
        out_shape += [jax.ShapeDtypeStruct((3, rows, width), jnp.float32)] * 2
        out_specs += [f_edge, f_edge, plane(low_at), plane(high_at)]
    return pl.pallas_call(
        functools.partial(face_kernel, first_sweep),
        name="relax_faces_first" if first_sweep else "relax_faces_second",
        grid_spec=pltpu.PrefetchScalarGridSpec(
            num_scalar_prefetch=1, grid=(2, ntiles), in_specs=in_specs, out_specs=out_specs
        ),
        out_shape=out_shape,
        input_output_aliases=aliases,
        compiler_params=pltpu.CompilerParams(vmem_limit_bytes=VMEM_LIMIT),
    )(position, *args)


def per_device(
    displacement,
    stiffness,
    node_list,
    active_count,
    wear_class,
    pressure,
    slip_speed,
    rate_table,
    tile_owner,
    node_cell,
):
    rows, width = displacement.shape[2:]
    position = jnp.stack(
        [lax.axis_index("tan"), (lax.axis_index("depth") == 0).astype(jnp.int32)]
    ).astype(jnp.int32)

    wear = archard(wear_class, pressure, slip_speed, rate_table)
    other = swap_halves(wear)
    face_first, face_last = pack_faces(displacement, stiffness, wear)
    face_first, face_last, other = lax.optimization_barrier((face_first, face_last, other))
    wear = gather_wear(wear, other)
    low, high = shift_both(face_last, face_first, "depth")
    row_first, row_last = pack_rows(displacement, stiffness)
    before, after = shift_both(row_last, row_first, "tan")
    surface = paint(position, tile_owner, active_count, wear, node_list,
                    node_cell.reshape(-1, 128), rows, width, wear_class.shape[0])

    first, row_first, row_last = relax_inner(
        displacement, stiffness, before, after, before, after, surface
    )
    first, row_first, row_last, send_low, send_high = relax_faces(
        position, displacement, stiffness, low, high, low, high,
        before, after, before, after, surface, (first, row_first, row_last),
    )
    low_2, high_2 = shift_both(send_high, send_low, "depth")
    before_2, after_2 = shift_both(row_last, row_first, "tan")
    result = relax_inner(first, stiffness, before_2, after_2, before, after, None)[0]
    return relax_faces(
        position, first, stiffness, low_2, high_2, low, high,
        before_2, after_2, before, after, None, (result,),
    )[0]


def solution(mesh):
    in_specs = (
        P(None, "depth", "tan", None),
        P("depth", "tan", None),
        P(),
        P(),
        P("tan", None),
        P("tan", None),
        P("tan", None),
        P(),
        P(),
        P(),
    )
    out_specs = P(None, "depth", "tan", None)
    return jax.shard_map(
        per_device, mesh=mesh, in_specs=in_specs, out_specs=out_specs, check_vma=False
    )
```

```python
import functools

import jax
import jax.numpy as jnp
from jax import lax
from jax.experimental import pallas as pl
from jax.experimental.pallas import tpu as pltpu
from jax.sharding import PartitionSpec as P

wear_step = 0.6
hardness = 4.0
GROUP = 8
VMEM_LIMIT = 48 * 1024 * 1024


def shift_both(last, first, axis):
    size = lax.axis_size(axis)
    up = [(i, i + 1) for i in range(size - 1)]
    down = [(j, i) for i, j in up]
    return lax.ppermute(last, axis, up), lax.ppermute(first, axis, down)


def rows_kernel(rates_ref, class_ref, contact_ref, sliding_ref, f_top, s_top, f_bottom,
                s_bottom, wear_ref, first_ref, last_ref):
    ids = class_ref[...]
    rate = jnp.zeros(ids.shape, jnp.float32)
    for k in range(rates_ref.shape[0]):
        rate = jnp.where(ids == k, rates_ref[k], rate)
    product = contact_ref[...] * sliding_ref[...]
    wear_ref[...] = wear_step * rate * product / (1.0 + product / hardness)
    for l in range(f_top.shape[1]):
        first_ref[3, l : l + 1, :] = s_top[l, 0:1, :]
        last_ref[3, l : l + 1, :] = s_bottom[l, 7:8, :]
        for c in range(3):
            first_ref[c, l : l + 1, :] = f_top[c, l, 0:1, :]
            last_ref[c, l : l + 1, :] = f_bottom[c, l, 7:8, :]


def pack_rows(field, stiffness, class_ids, contact, sliding, rates):
    _, layers, rows, width = field.shape
    bottom = rows // 8 - 1
    f_spec = lambda at: pl.BlockSpec((3, layers, 8, width), lambda i: (0, 0, at, 0))
    s_spec = lambda at: pl.BlockSpec((layers, 8, width), lambda i: (0, at, 0))
    out = jax.ShapeDtypeStruct((4, layers, width), jnp.float32)
    out_spec = pl.BlockSpec((4, layers, width), lambda i: (0, 0, 0))
    slot_spec = pl.BlockSpec(contact.shape, lambda i: (0, 0))
    return pl.pallas_call(
        rows_kernel,
        name="pack_rows",
        grid=(1,),
        in_specs=[pl.BlockSpec(memory_space=pltpu.SMEM), slot_spec, slot_spec, slot_spec,
                  f_spec(0), s_spec(0), f_spec(bottom), s_spec(bottom)],
        out_specs=[slot_spec, out_spec, out_spec],
        out_shape=[jax.ShapeDtypeStruct(contact.shape, jnp.float32), out, out],
        compiler_params=pltpu.CompilerParams(vmem_limit_bytes=VMEM_LIMIT),
    )(rates, class_ids, contact, sliding, field, stiffness, field, stiffness)


def faces_kernel(field_ref, stiff_ref, after_ref, first_ref, last_ref):
    step = pl.program_id(0)

    def put(to):
        to[0:3] = field_ref[:, 0]
        to[3:4] = stiff_ref[...]

    pl.when(step == 0)(lambda: put(last_ref))
    pl.when(step == 1)(lambda: put(first_ref))


def pack_faces(field, stiffness, earlier):
    _, layers, rows, width = field.shape
    face = jax.ShapeDtypeStruct((4, rows, width), jnp.float32)
    layer = lambda i: (1 - i) * (layers - 1)
    whole = pl.BlockSpec((4, rows, width), lambda i: (0, 0, 0))
    return pl.pallas_call(
        faces_kernel,
        name="pack_faces",
        grid=(2,),
        in_specs=[
            pl.BlockSpec((3, 1, rows, width), lambda i: (0, layer(i), 0, 0)),
            pl.BlockSpec((1, rows, width), lambda i: (layer(i), 0, 0)),
            pl.BlockSpec(memory_space=pl.ANY),
        ],
        out_specs=[whole, whole],
        out_shape=[face, face],
        compiler_params=pltpu.CompilerParams(vmem_limit_bytes=VMEM_LIMIT),
    )(field, stiffness, earlier)


def swap_halves(wear):
    size = lax.axis_size("tan")
    return lax.ppermute(wear, "tan", [(i, i ^ 2) for i in range(size)])


def gather_wear(wear, other):
    size = lax.axis_size("tan")
    both = jnp.concatenate([wear, other], axis=0)
    groups = [[i for i in range(size) if (i // 2) % 2 == half] for half in range(2)]
    return lax.all_gather(both, "tan", axis=0, axis_index_groups=groups, tiled=True)


def three_parts(value):
    high = value.astype(jnp.bfloat16).astype(jnp.float32)
    rest = value - high
    middle = rest.astype(jnp.bfloat16).astype(jnp.float32)
    return high, middle, rest - middle


def paint_kernel(
    shard_tiles, where_ref, owner_ref, count_ref, wear_ref, list_ref, table_ref, out_ref,
    own_ref, side_ref, acc_ref, edge_ref,
):
    slots = wear_ref.shape[1]
    ntile = wear_ref.shape[0]
    rows_table = table_ref.shape[0] // ntile
    tile_len = rows_table * 128
    width = out_ref.shape[1]
    rows = out_ref.shape[0] - 16
    me = where_ref[0]
    on_top = where_ref[1]
    out_ref[...] = jnp.zeros_like(out_ref)

    @pl.when(on_top == 1)
    def _():
        acc_ref[...] = jnp.zeros_like(acc_ref)
        edge_ref[...] = jnp.zeros_like(edge_ref)

        def collect(i, carry):
            n_own, n_side = carry
            offset = owner_ref[i] - me
            own_ref[n_own] = i
            side_ref[n_side] = i
            n_own = n_own + jnp.where(offset == 0, 1, 0)
            n_side = n_side + jnp.where(offset * offset == 1, 1, 0)
            return n_own, n_side

        n_own, n_side = lax.fori_loop(
            0, ntile, collect, (jnp.int32(0), jnp.int32(0)), unroll=8
        )

        lane = lax.broadcasted_iota(jnp.int32, (1, slots), 1)
        table_row = lax.broadcasted_iota(jnp.int32, (rows_table, slots), 0)
        block = width // 8
        fine = lax.broadcasted_iota(jnp.int32, (block, slots), 0)
        coarse = lax.broadcasted_iota(jnp.int32, (rows * 8, slots), 0)
        fine_edge = lax.broadcasted_iota(jnp.int32, (128, slots), 0)
        edge_blocks = width // 128
        coarse_edge = lax.broadcasted_iota(jnp.int32, (2 * edge_blocks, slots), 0)

        def entry(tiles_ref, position, total):
            i = tiles_ref[jnp.minimum(position, total - 1)]
            live = jnp.where(position < total, count_ref[i], 0)
            local = list_ref[pl.ds(i, 1), :] - i * tile_len
            table = table_ref[pl.ds(pl.multiple_of(i * rows_table, 8), rows_table), :]
            column = jnp.broadcast_to(local & 127, (rows_table, slots))
            picked = jnp.take_along_axis(table, column, axis=1)
            cell = jnp.sum(
                jnp.where(table_row == (local >> 7), picked, 0), axis=0, keepdims=True
            )
            shard = i // shard_tiles
            half = jnp.where((shard // 2) % 2 == (me // 2) % 2, 0, 1)
            place = (shard // 4) * 4 + (shard % 2) * 2 + half
            at = place * shard_tiles + i % shard_tiles
            wear = jnp.where(lane < live, wear_ref[pl.ds(at, 1), :], 0.0)
            return i, cell, wear

        def one_hot(mask, value):
            return jnp.where(mask, value, 0.0).astype(jnp.bfloat16)

        def add(into_ref, parts, hot):
            total = into_ref[...]
            for part in parts:
                total = total + lax.dot_general(
                    jnp.concatenate(part, axis=1), hot, (((1,), (1,)), ((), ())),
                    preferred_element_type=jnp.float32,
                )
            into_ref[...] = total

        def own_group(g, carry):
            parts = ([], [], [])
            hots = []
            for j in range(GROUP):
                _, cell, wear = entry(own_ref, g * GROUP + j, n_own)
                col = cell % width
                a_index = (col // block) * rows + cell // width
                hots.append(one_hot(fine == col % block, 1.0))
                mask = coarse == a_index
                for part, value in zip(parts, three_parts(wear)):
                    part.append(one_hot(mask, value))
            add(acc_ref, parts, jnp.concatenate(hots, axis=1))
            return carry

        def side_group(g, carry):
            parts = ([], [], [])
            hots = []
            for j in range(GROUP):
                i, cell, wear = entry(side_ref, g * GROUP + j, n_side)
                below = owner_ref[i] > me
                col = cell % width
                wanted = jnp.where(below, 0, rows - 1)
                shift = jnp.where(below, edge_blocks, 0)
                a_index = jnp.where(cell // width == wanted, col // 128 + shift, -1)
                hots.append(one_hot(fine_edge == col % 128, 1.0))
                mask = coarse_edge == a_index
                for part, value in zip(parts, three_parts(wear)):
                    part.append(one_hot(mask, value))
            add(edge_ref, parts, jnp.concatenate(hots, axis=1))
            return carry

        lax.fori_loop(0, (n_own + GROUP - 1) // GROUP, own_group, 0)
        lax.fori_loop(0, (n_side + GROUP - 1) // GROUP, side_group, 0)
        for j in range(8):
            out_ref[8 : 8 + rows, j * block : (j + 1) * block] = acc_ref[
                j * rows : (j + 1) * rows, :
            ]
        for j in range(edge_blocks):
            out_ref[7:8, j * 128 : (j + 1) * 128] = edge_ref[j : j + 1, :]
            out_ref[8 + rows : 9 + rows, j * 128 : (j + 1) * 128] = edge_ref[
                edge_blocks + j : edge_blocks + j + 1, :
            ]


def paint(position, owner, counts, wear, lists, table, rows, width, shard_tiles):
    ntile, slots = lists.shape
    whole = lambda shape: pl.BlockSpec(shape, lambda i, *_: (0,) * len(shape))
    return pl.pallas_call(
        functools.partial(paint_kernel, shard_tiles),
        name="paint_band",
        grid_spec=pltpu.PrefetchScalarGridSpec(
            num_scalar_prefetch=3,
            grid=(1,),
            in_specs=[whole(wear.shape), whole(lists.shape), whole(table.shape)],
            out_specs=whole((rows + 16, width)),
            scratch_shapes=[
                pltpu.SMEM((ntile + 1,), jnp.int32),
                pltpu.SMEM((ntile + 1,), jnp.int32),
                pltpu.VMEM((rows * 8, width // 8), jnp.float32),
                pltpu.VMEM((2 * width // 128, 128), jnp.float32),
            ],
        ),
        out_shape=jax.ShapeDtypeStruct((rows + 16, width), jnp.float32),
        compiler_params=pltpu.CompilerParams(vmem_limit_bytes=VMEM_LIMIT),
    )(position, owner, counts, wear, lists, table)


def relax_tile(load, row_above, row_below, has_high, has_low):
    row = lax.broadcasted_iota(jnp.int32, (8, 1), 0)
    centers = {}

    def neighbours(c):
        here = load(c, 0)
        centers[c] = here
        width = here.shape[1]
        lane = lax.broadcasted_iota(jnp.int32, here.shape, 1)
        yield load(c, 1)
        yield load(c, -1)
        yield jnp.where(row == 7, row_below(c), pltpu.roll(here, 7, 0))
        yield jnp.where(row == 0, row_above(c), pltpu.roll(here, 1, 0))
        yield jnp.where(lane == width - 1, 0.0, pltpu.roll(here, width - 1, 1))
        yield jnp.where(lane == 0, 0.0, pltpu.roll(here, 1, 1))

    around = list(neighbours(3))
    weights = [centers[3] + s for s in around]
    weights[0] = weights[0] * has_high
    weights[1] = weights[1] * has_low
    total = weights[0]
    for w in weights[1:]:
        total = total + w
    sums = []
    for c in range(3):
        acc = None
        for w, f in zip(weights, neighbours(c)):
            acc = w * f if acc is None else acc + w * f
        sums.append(acc)
    return sums, total, centers


def layer_kernel(first_sweep, *refs):
    (where_ref, low, mid, high, s_low, s_mid, s_high, before, after, s_before,
     s_after) = refs[:11]
    rest = list(refs[11:])
    surface = rest.pop(0) if first_sweep else None
    out, totals = rest[:2]
    layer = pl.program_id(0)
    last = pl.num_programs(0) - 1
    ntiles = mid.shape[2] // 8
    f_refs = {-1: low, 0: mid, 1: high}
    s_refs = {-1: s_low, 0: s_mid, 1: s_high}
    outermost = jnp.logical_or(layer == 0, layer == last)
    if first_sweep:
        first_row, last_row = rest[2:]

        @pl.when(layer == 0)
        def _():
            first_row[...] = jnp.zeros_like(first_row)
            last_row[...] = jnp.zeros_like(last_row)

    has_low = jnp.where(layer == 0, 0.0, 1.0)
    has_high = jnp.where(layer == last, 0.0, 1.0)
    scales = {0: jnp.where(layer == 0, 1.0, 0.0), -1: jnp.where(layer == 1, 1.0, 0.0)}
    pinned = jnp.logical_and(layer == 0, where_ref[1] == 1)

    for t in range(ntiles):
        at = slice(8 * t, 8 * t + 8)

        def load(c, side):
            if c == 3:
                return s_refs[side][0, at, :]
            value = f_refs[side][c, 0, at, :]
            if first_sweep and c == 0 and side <= 0:
                value = value + scales[side] * surface[8 * t + 8 : 8 * t + 16, :]
            return value

        def beside(inside, row, f_edge, s_edge):
            def get(c):
                if c == 3:
                    if inside:
                        return s_mid[0, row : row + 1, :]
                    return s_edge[0, pl.ds(layer, 1), :]
                value = mid[c, 0, row : row + 1, :] if inside else f_edge[c, pl.ds(layer, 1), :]
                if first_sweep and c == 0:
                    value = value + scales[0] * surface[row + 8 : row + 9, :]
                return value
            return get

        sums, total, centers = relax_tile(
            load,
            beside(t > 0, 8 * t - 1, before, s_before),
            beside(t < ntiles - 1, 8 * t + 8, after, s_after),
            has_high,
            has_low,
        )
        inverse = jnp.where(outermost, 1.0, 1.0 / total)
        outs = [part * inverse for part in sums]
        outs[0] = jnp.where(pinned, centers[0], outs[0])
        for c in range(3):
            out[c, 0, at, :] = outs[c]

        @pl.when(outermost)
        def _():
            totals[0, at, :] = total

        if first_sweep and t in (0, ntiles - 1):
            @pl.when(jnp.logical_not(outermost))
            def _():
                for c in range(3):
                    if t == 0:
                        first_row[c, pl.ds(layer, 1), :] = outs[c][0:1]
                    if t == ntiles - 1:
                        last_row[c, pl.ds(layer, 1), :] = outs[c][7:8]


def relax_layers(position, field, stiffness, before, after, s_before, s_after, surface):
    _, layers, rows, width = field.shape
    first_sweep = surface is not None
    whole = lambda shape: pl.BlockSpec(shape, lambda i, *_: (0,) * len(shape))
    at = lambda i, k: jnp.clip(i + k, 0, layers - 1)
    f_spec = lambda k: pl.BlockSpec((3, 1, rows, width), lambda i, *_: (0, at(i, k), 0, 0))
    s_spec = lambda k: pl.BlockSpec((1, rows, width), lambda i, *_: (at(i, k), 0, 0))
    f_edge = whole((3, layers, width))
    s_edge = pl.BlockSpec((1, layers, width), lambda i, *_: (3, 0, 0))
    sides = (-1, 0, 1)
    args = [field] * 3 + [stiffness] * 3 + [before, after, s_before, s_after]
    in_specs = [f_spec(k) for k in sides] + [s_spec(k) for k in sides]
    in_specs += [f_edge, f_edge, s_edge, s_edge]
    out_shape = [jax.ShapeDtypeStruct(field.shape, jnp.float32),
                 jax.ShapeDtypeStruct((2, rows, width), jnp.float32)]
    out_specs = [f_spec(0),
                 pl.BlockSpec((1, rows, width), lambda i, *_: (i // (layers // 2), 0, 0))]
    if first_sweep:
        args.append(surface)
        in_specs.append(whole(surface.shape))
        out_shape += [jax.ShapeDtypeStruct((3, layers, width), jnp.float32)] * 2
        out_specs += [f_edge] * 2
    return pl.pallas_call(
        functools.partial(layer_kernel, first_sweep),
        name="relax_layers_first" if first_sweep else "relax_layers_second",
        grid_spec=pltpu.PrefetchScalarGridSpec(
            num_scalar_prefetch=1, grid=(layers,), in_specs=in_specs, out_specs=out_specs
        ),
        out_shape=out_shape,
        compiler_params=pltpu.CompilerParams(vmem_limit_bytes=VMEM_LIMIT),
    )(position, *args)


def finish_first_kernel(face, *refs):
    where_ref, sums, s_here, totals, outer, s_outer = refs[:6]
    out, send, first_row, last_row = refs[-4:]
    ntiles = sums.shape[2] // 8
    pinned = where_ref[1] == 1
    if len(refs) > 10:
        first_row[...] = refs[6][...]
        last_row[...] = refs[7][...]
    else:
        first_row[...] = jnp.zeros_like(first_row)
        last_row[...] = jnp.zeros_like(last_row)
    for t in range(ntiles):
        at = slice(8 * t, 8 * t + 8)
        weight = s_here[0, at, :] + s_outer[0, at, :]
        inverse = 1.0 / (totals[0, at, :] + weight)
        for c in range(3):
            so_far = sums[c, 0, at, :]
            value = (so_far + weight * outer[c, at, :]) * inverse
            if face == 0 and c == 0:
                value = jnp.where(pinned, so_far, value)
            out[c, 0, at, :] = value
            send[c, at, :] = value
            k = 2 * c + face
            if t == 0:
                first_row[k : k + 1, :] = value[0:1]
            if t == ntiles - 1:
                last_row[k : k + 1, :] = value[7:8]


def finish_first(position, face, field, stiffness, totals, outer, edges):
    _, layers, rows, width = field.shape
    layer = face * (layers - 1)
    block = lambda shape, *at: pl.BlockSpec(shape, lambda i, *_: at)
    plane = block((3, rows, width), 0, 0, 0)
    own = block((3, 1, rows, width), 0, layer, 0, 0)
    edge = block((8, width), 0, 0)
    args = [field, stiffness, totals, outer, outer]
    in_specs = [own, block((1, rows, width), layer, 0, 0), block((1, rows, width), face, 0, 0),
                plane, block((1, rows, width), 3, 0, 0)]
    if edges is not None:
        args += edges
        in_specs += [edge, edge]
    edge_shape = jax.ShapeDtypeStruct((8, width), jnp.float32)
    return pl.pallas_call(
        functools.partial(finish_first_kernel, face),
        name="finish_first",
        grid_spec=pltpu.PrefetchScalarGridSpec(
            num_scalar_prefetch=1, grid=(1,), in_specs=in_specs,
            out_specs=[own, plane, edge, edge],
        ),
        out_shape=[jax.ShapeDtypeStruct(field.shape, jnp.float32),
                   jax.ShapeDtypeStruct((3, rows, width), jnp.float32),
                   edge_shape, edge_shape],
        input_output_aliases={1: 0},
        compiler_params=pltpu.CompilerParams(vmem_limit_bytes=VMEM_LIMIT),
    )(position, *args)


def finish_second_kernel(where_ref, sums, s_here, totals, low, high, s_low, s_high,
                         before, after, s_before, s_after, out):
    ntiles = sums.shape[2] // 8
    pinned = where_ref[1] == 1
    row = lax.broadcasted_iota(jnp.int32, (8, 1), 0)

    def one(face, outer, s_outer):
        layer = face * (s_before.shape[1] - 1)
        for t in range(ntiles):
            at = slice(8 * t, 8 * t + 8)
            here = s_here[0, at, :]
            weight = here + s_outer[0, at, :]
            inverse = 1.0 / (totals[0, at, :] + weight)
            for c in range(3):
                so_far = sums[c, 0, at, :]
                value = so_far + weight * outer[c, at, :]
                k = 2 * c + face
                if t == 0:
                    side = here + s_before[0, layer : layer + 1, :]
                    value = value + jnp.where(row == 0, side * before[k : k + 1, :], 0.0)
                if t == ntiles - 1:
                    side = here + s_after[0, layer : layer + 1, :]
                    value = value + jnp.where(row == 7, side * after[k : k + 1, :], 0.0)
                value = value * inverse
                if face == 0 and c == 0:
                    value = jnp.where(pinned, so_far, value)
                out[c, 0, at, :] = value

    step = pl.program_id(0)
    pl.when(step == 0)(lambda: one(0, low, s_low))
    pl.when(step == 1)(lambda: one(1, high, s_high))


def finish_second(position, field, stiffness, totals, low, high, s_low, s_high,
                  before, after, s_before, s_after):
    _, layers, rows, width = field.shape
    block = lambda shape, at: pl.BlockSpec(shape, lambda i, *_: at(i))
    layer = lambda i: i * (layers - 1)
    plane = block((3, rows, width), lambda i: (0, 0, 0))
    s_plane = block((1, rows, width), lambda i: (3, 0, 0))
    own = block((3, 1, rows, width), lambda i: (0, layer(i), 0, 0))
    edge = block((8, width), lambda i: (0, 0))
    s_edge = block((1, layers, width), lambda i: (3, 0, 0))
    return pl.pallas_call(
        finish_second_kernel,
        name="finish_second",
        grid_spec=pltpu.PrefetchScalarGridSpec(
            num_scalar_prefetch=1, grid=(2,),
            in_specs=[own, block((1, rows, width), lambda i: (layer(i), 0, 0)),
                      block((1, rows, width), lambda i: (i, 0, 0)),
                      plane, plane, s_plane, s_plane, edge, edge, s_edge, s_edge],
            out_specs=own,
        ),
        out_shape=jax.ShapeDtypeStruct(field.shape, jnp.float32),
        input_output_aliases={1: 0},
        compiler_params=pltpu.CompilerParams(vmem_limit_bytes=VMEM_LIMIT),
    )(position, field, stiffness, totals, low, high, s_low, s_high,
      before, after, s_before, s_after)


def per_device(
    displacement,
    stiffness,
    node_list,
    active_count,
    wear_class,
    pressure,
    slip_speed,
    rate_table,
    tile_owner,
    node_cell,
):
    rows, width = displacement.shape[2:]
    position = jnp.stack(
        [lax.axis_index("tan"), (lax.axis_index("depth") == 0).astype(jnp.int32)]
    ).astype(jnp.int32)

    wear, row_first, row_last = pack_rows(
        displacement, stiffness, wear_class, pressure, slip_speed, rate_table
    )
    other = swap_halves(wear)
    before, after = shift_both(row_last, row_first, "tan")
    face_first, face_last = pack_faces(displacement, stiffness, wear)
    face_first, face_last, other, before, after = lax.optimization_barrier(
        (face_first, face_last, other, before, after)
    )
    low, high = shift_both(face_last, face_first, "depth")
    wear = gather_wear(wear, other)
    surface = paint(position, tile_owner, active_count, wear, node_list,
                    node_cell.reshape(-1, 128), rows, width, wear_class.shape[0])

    first, totals, row_first, row_last = relax_layers(
        position, displacement, stiffness, before, after, before, after, surface
    )
    before_2, after_2 = shift_both(row_last, row_first, "tan")
    first, send_last, edge_first, edge_last = finish_first(
        position, 1, first, stiffness, totals, high, None
    )
    first, send_first, edge_first, edge_last = finish_first(
        position, 0, first, stiffness, totals, low, (edge_first, edge_last)
    )
    low_2, high_2 = shift_both(send_last, send_first, "depth")
    edge_before, edge_after = shift_both(edge_last, edge_first, "tan")
    result, totals = relax_layers(
        position, first, stiffness, before_2, after_2, before, after, None
    )
    return finish_second(position, result, stiffness, totals, low_2, high_2, low, high,
                         edge_before, edge_after, before, after)


def solution(mesh):
    in_specs = (
        P(None, "depth", "tan", None),
        P("depth", "tan", None),
        P(),
        P(),
        P("tan", None),
        P("tan", None),
        P("tan", None),
        P(),
        P(),
        P(),
    )
    out_specs = P(None, "depth", "tan", None)
    return jax.shard_map(
        per_device, mesh=mesh, in_specs=in_specs, out_specs=out_specs, check_vma=False
    )
```

```python
import functools

import jax
import jax.numpy as jnp
from jax import lax
from jax.experimental import pallas as pl
from jax.experimental.pallas import tpu as pltpu
from jax.sharding import PartitionSpec as P

wear_step = 0.6
hardness = 4.0
GROUP = 8
VMEM_LIMIT = 48 * 1024 * 1024


def shift_both(last, first, axis):
    size = lax.axis_size(axis)
    up = [(i, i + 1) for i in range(size - 1)]
    down = [(j, i) for i, j in up]
    return lax.ppermute(last, axis, up), lax.ppermute(first, axis, down)


def wear_kernel(rates_ref, class_ref, contact_ref, sliding_ref, wear_ref):
    ids = class_ref[...]
    rate = jnp.zeros(ids.shape, jnp.float32)
    for k in range(rates_ref.shape[0]):
        rate = jnp.where(ids == k, rates_ref[k], rate)
    product = contact_ref[...] * sliding_ref[...]
    wear_ref[...] = wear_step * rate * product / (1.0 + product / hardness)


def archard(class_ids, contact, sliding, rates):
    near = pl.BlockSpec(memory_space=pltpu.VMEM)
    return pl.pallas_call(
        wear_kernel,
        name="archard",
        in_specs=[pl.BlockSpec(memory_space=pltpu.SMEM), near, near, near],
        out_specs=near,
        out_shape=jax.ShapeDtypeStruct(contact.shape, jnp.float32),
    )(rates, class_ids, contact, sliding)


def rows_kernel(f_top, s_top, f_bottom, s_bottom, first_ref, last_ref):
    for l in range(f_top.shape[1]):
        for k in range(2):
            first_ref[4 * k + 3, l : l + 1, :] = s_top[l, k : k + 1, :]
            last_ref[4 * k + 3, l : l + 1, :] = s_bottom[l, 7 - k : 8 - k, :]
            for c in range(3):
                first_ref[4 * k + c, l : l + 1, :] = f_top[c, l, k : k + 1, :]
                last_ref[4 * k + c, l : l + 1, :] = f_bottom[c, l, 7 - k : 8 - k, :]


def pack_rows(field, stiffness):
    _, layers, rows, width = field.shape
    bottom = rows // 8 - 1
    f_spec = lambda at: pl.BlockSpec((3, layers, 8, width), lambda i: (0, 0, at, 0))
    s_spec = lambda at: pl.BlockSpec((layers, 8, width), lambda i: (0, at, 0))
    out = jax.ShapeDtypeStruct((8, layers, width), jnp.float32)
    out_spec = pl.BlockSpec((8, layers, width), lambda i: (0, 0, 0))
    return pl.pallas_call(
        rows_kernel,
        name="pack_rows",
        grid=(1,),
        in_specs=[f_spec(0), s_spec(0), f_spec(bottom), s_spec(bottom)],
        out_specs=[out_spec, out_spec],
        out_shape=[out, out],
        compiler_params=pltpu.CompilerParams(vmem_limit_bytes=VMEM_LIMIT),
    )(field, stiffness, field, stiffness)


def faces_kernel(field_ref, stiff_ref, after_ref, first_ref, last_ref):
    step = pl.program_id(0)

    def put(to):
        to[0:3] = field_ref[:, 0]
        to[3:4] = stiff_ref[...]

    pl.when(step == 0)(lambda: put(last_ref))
    pl.when(step == 1)(lambda: put(first_ref))


def pack_faces(field, stiffness, earlier):
    _, layers, rows, width = field.shape
    face = jax.ShapeDtypeStruct((4, rows, width), jnp.float32)
    layer = lambda i: (1 - i) * (layers - 1)
    whole = pl.BlockSpec((4, rows, width), lambda i: (0, 0, 0))
    return pl.pallas_call(
        faces_kernel,
        name="pack_faces",
        grid=(2,),
        in_specs=[
            pl.BlockSpec((3, 1, rows, width), lambda i: (0, layer(i), 0, 0)),
            pl.BlockSpec((1, rows, width), lambda i: (layer(i), 0, 0)),
            pl.BlockSpec(memory_space=pl.ANY),
        ],
        out_specs=[whole, whole],
        out_shape=[face, face],
        compiler_params=pltpu.CompilerParams(vmem_limit_bytes=VMEM_LIMIT),
    )(field, stiffness, earlier)


def swap_halves(wear):
    size = lax.axis_size("tan")
    return lax.ppermute(wear, "tan", [(i, i ^ 2) for i in range(size)])


def gather_wear(wear, other):
    size = lax.axis_size("tan")
    both = jnp.concatenate([wear, other], axis=0)
    groups = [[i for i in range(size) if (i // 2) % 2 == half] for half in range(2)]
    return lax.all_gather(both, "tan", axis=0, axis_index_groups=groups, tiled=True)


def three_parts(value):
    high = value.astype(jnp.bfloat16).astype(jnp.float32)
    rest = value - high
    middle = rest.astype(jnp.bfloat16).astype(jnp.float32)
    return high, middle, rest - middle


def paint_kernel(
    shard_tiles, where_ref, owner_ref, count_ref, wear_ref, list_ref, table_ref, out_ref,
    own_ref, side_ref, acc_ref, edge_ref,
):
    slots = wear_ref.shape[1]
    ntile = wear_ref.shape[0]
    rows_table = table_ref.shape[0] // ntile
    tile_len = rows_table * 128
    width = out_ref.shape[1]
    rows = out_ref.shape[0] - 16
    me = where_ref[0]
    on_top = where_ref[1]
    out_ref[...] = jnp.zeros_like(out_ref)

    @pl.when(on_top == 1)
    def _():
        acc_ref[...] = jnp.zeros_like(acc_ref)
        edge_ref[...] = jnp.zeros_like(edge_ref)

        def collect(i, carry):
            n_own, n_side = carry
            offset = owner_ref[i] - me
            own_ref[n_own] = i
            side_ref[n_side] = i
            n_own = n_own + jnp.where(offset == 0, 1, 0)
            n_side = n_side + jnp.where(offset * offset == 1, 1, 0)
            return n_own, n_side

        n_own, n_side = lax.fori_loop(
            0, ntile, collect, (jnp.int32(0), jnp.int32(0)), unroll=8
        )

        lane = lax.broadcasted_iota(jnp.int32, (1, slots), 1)
        table_row = lax.broadcasted_iota(jnp.int32, (rows_table, slots), 0)
        block = width // 8
        fine = lax.broadcasted_iota(jnp.int32, (block, slots), 0)
        coarse = lax.broadcasted_iota(jnp.int32, (rows * 8, slots), 0)
        fine_edge = lax.broadcasted_iota(jnp.int32, (128, slots), 0)
        edge_blocks = width // 128
        coarse_edge = lax.broadcasted_iota(jnp.int32, (2 * edge_blocks, slots), 0)

        def entry(tiles_ref, position, total):
            i = tiles_ref[jnp.minimum(position, total - 1)]
            live = jnp.where(position < total, count_ref[i], 0)
            local = list_ref[pl.ds(i, 1), :] - i * tile_len
            table = table_ref[pl.ds(pl.multiple_of(i * rows_table, 8), rows_table), :]
            column = jnp.broadcast_to(local & 127, (rows_table, slots))
            picked = jnp.take_along_axis(table, column, axis=1)
            cell = jnp.sum(
                jnp.where(table_row == (local >> 7), picked, 0), axis=0, keepdims=True
            )
            shard = i // shard_tiles
            half = jnp.where((shard // 2) % 2 == (me // 2) % 2, 0, 1)
            place = (shard // 4) * 4 + (shard % 2) * 2 + half
            at = place * shard_tiles + i % shard_tiles
            wear = jnp.where(lane < live, wear_ref[pl.ds(at, 1), :], 0.0)
            return i, cell, wear

        def one_hot(mask, value):
            return jnp.where(mask, value, 0.0).astype(jnp.bfloat16)

        def add(into_ref, parts, hot):
            total = into_ref[...]
            for part in parts:
                total = total + lax.dot_general(
                    jnp.concatenate(part, axis=1), hot, (((1,), (1,)), ((), ())),
                    preferred_element_type=jnp.float32,
                )
            into_ref[...] = total

        def own_group(g, carry):
            parts = ([], [], [])
            hots = []
            for j in range(GROUP):
                _, cell, wear = entry(own_ref, g * GROUP + j, n_own)
                col = cell % width
                a_index = (col // block) * rows + cell // width
                hots.append(one_hot(fine == col % block, 1.0))
                mask = coarse == a_index
                for part, value in zip(parts, three_parts(wear)):
                    part.append(one_hot(mask, value))
            add(acc_ref, parts, jnp.concatenate(hots, axis=1))
            return carry

        def side_group(g, carry):
            parts = ([], [], [])
            hots = []
            for j in range(GROUP):
                i, cell, wear = entry(side_ref, g * GROUP + j, n_side)
                below = owner_ref[i] > me
                col = cell % width
                wanted = jnp.where(below, 0, rows - 1)
                shift = jnp.where(below, edge_blocks, 0)
                a_index = jnp.where(cell // width == wanted, col // 128 + shift, -1)
                hots.append(one_hot(fine_edge == col % 128, 1.0))
                mask = coarse_edge == a_index
                for part, value in zip(parts, three_parts(wear)):
                    part.append(one_hot(mask, value))
            add(edge_ref, parts, jnp.concatenate(hots, axis=1))
            return carry

        lax.fori_loop(0, (n_own + GROUP - 1) // GROUP, own_group, 0)
        lax.fori_loop(0, (n_side + GROUP - 1) // GROUP, side_group, 0)
        for j in range(8):
            out_ref[8 : 8 + rows, j * block : (j + 1) * block] = acc_ref[
                j * rows : (j + 1) * rows, :
            ]
        for j in range(edge_blocks):
            out_ref[7:8, j * 128 : (j + 1) * 128] = edge_ref[j : j + 1, :]
            out_ref[8 + rows : 9 + rows, j * 128 : (j + 1) * 128] = edge_ref[
                edge_blocks + j : edge_blocks + j + 1, :
            ]


def paint(position, owner, counts, wear, lists, table, rows, width, shard_tiles):
    ntile, slots = lists.shape
    whole = lambda shape: pl.BlockSpec(shape, lambda i, *_: (0,) * len(shape))
    return pl.pallas_call(
        functools.partial(paint_kernel, shard_tiles),
        name="paint_band",
        grid_spec=pltpu.PrefetchScalarGridSpec(
            num_scalar_prefetch=3,
            grid=(1,),
            in_specs=[whole(wear.shape), whole(lists.shape), whole(table.shape)],
            out_specs=whole((rows + 16, width)),
            scratch_shapes=[
                pltpu.SMEM((ntile + 1,), jnp.int32),
                pltpu.SMEM((ntile + 1,), jnp.int32),
                pltpu.VMEM((rows * 8, width // 8), jnp.float32),
                pltpu.VMEM((2 * width // 128, 128), jnp.float32),
            ],
        ),
        out_shape=jax.ShapeDtypeStruct((rows + 16, width), jnp.float32),
        compiler_params=pltpu.CompilerParams(vmem_limit_bytes=VMEM_LIMIT),
    )(position, owner, counts, wear, lists, table)


def relax_tile(load, beside, has_high, has_low):
    centers = {}

    def neighbours(c):
        here = load(c, 0)
        centers[c] = here
        width = here.shape[1]
        lane = lax.broadcasted_iota(jnp.int32, here.shape, 1)
        yield load(c, 1)
        yield load(c, -1)
        yield from beside(c, here)
        yield jnp.where(lane == width - 1, 0.0, pltpu.roll(here, width - 1, 1))
        yield jnp.where(lane == 0, 0.0, pltpu.roll(here, 1, 1))

    around = list(neighbours(3))
    weights = [centers[3] + s for s in around]
    weights[0] = weights[0] * has_high
    weights[1] = weights[1] * has_low
    total = weights[0]
    for w in weights[1:]:
        total = total + w
    sums = []
    for c in range(3):
        acc = None
        for w, f in zip(weights, neighbours(c)):
            acc = w * f if acc is None else acc + w * f
        sums.append(acc)
    return sums, total, centers


def relax_outside(out, near, s_near, far, inside, surface, at, layer):
    def load(c, side):
        here = s_near[0] if c == 3 else near[c]
        if c == 0:
            here = here + jnp.where(layer == 0, surface[at : at + 1, :], 0.0)
        return here if side == 0 else pltpu.roll(here, 7 if side == 1 else 1, 0)

    sums, total, _ = relax_tile(load, lambda c, here: (far[c], inside[c]), 1.0, 1.0)
    inverse = 1.0 / total
    between = jnp.logical_and(layer > 0, layer < out.shape[1] - 1)
    kept = jnp.logical_and(between, s_near[0] > 0.0)
    for c in range(3):
        out[c] = jnp.where(kept, sums[c] * inverse, 0.0)


def layer_kernel(first_sweep, *refs):
    (where_ref, low, mid, high, s_low, s_mid, s_high, before, after, s_before,
     s_after) = refs[:11]
    rest = list(refs[11:])
    surface = rest.pop(0) if first_sweep else None
    extra = rest[:4] + rest[6:]
    out, totals = rest[4:6] if first_sweep else rest
    layer = pl.program_id(0)
    last = pl.num_programs(0) - 1
    ntiles = mid.shape[2] // 8
    f_refs = {-1: low, 0: mid, 1: high}
    s_refs = {-1: s_low, 0: s_mid, 1: s_high}
    outermost = jnp.logical_or(layer == 0, layer == last)
    row = lax.broadcasted_iota(jnp.int32, (8, 1), 0)
    if first_sweep:

        @pl.when(layer == 0)
        def _():
            far_before, far_after, own_first, own_last, out_before, out_after = extra
            relax_outside(out_before, before, s_before, far_before, own_first, surface, 7, row)
            relax_outside(out_after, after, s_after, far_after, own_last, surface,
                          8 + 8 * ntiles, row)

    has_low = jnp.where(layer == 0, 0.0, 1.0)
    has_high = jnp.where(layer == last, 0.0, 1.0)
    scales = {0: jnp.where(layer == 0, 1.0, 0.0), -1: jnp.where(layer == 1, 1.0, 0.0)}
    pinned = jnp.logical_and(layer == 0, where_ref[1] == 1)

    for t in range(ntiles):
        at = slice(8 * t, 8 * t + 8)

        def load(c, side):
            if c == 3:
                return s_refs[side][0, at, :]
            value = f_refs[side][c, 0, at, :]
            if first_sweep and c == 0 and side <= 0:
                value = value + scales[side] * surface[8 * t + 8 : 8 * t + 16, :]
            return value

        def beside(inside, row, f_edge, s_edge):
            def get(c):
                if c == 3:
                    if inside:
                        return s_mid[0, row : row + 1, :]
                    return s_edge[0, pl.ds(layer, 1), :]
                value = mid[c, 0, row : row + 1, :] if inside else f_edge[c, pl.ds(layer, 1), :]
                if first_sweep and c == 0:
                    value = value + scales[0] * surface[row + 8 : row + 9, :]
                return value
            return get

        above = beside(t > 0, 8 * t - 1, before, s_before)
        below = beside(t < ntiles - 1, 8 * t + 8, after, s_after)

        def rolled(c, here):
            yield jnp.where(row == 7, below(c), pltpu.roll(here, 7, 0))
            yield jnp.where(row == 0, above(c), pltpu.roll(here, 1, 0))

        sums, total, centers = relax_tile(load, rolled, has_high, has_low)
        inverse = jnp.where(outermost, 1.0, 1.0 / total)
        outs = [part * inverse for part in sums]
        outs[0] = jnp.where(pinned, centers[0], outs[0])
        for c in range(3):
            out[c, 0, at, :] = outs[c]

        @pl.when(outermost)
        def _():
            totals[0, at, :] = total


def relax_layers(position, field, stiffness, before, after, s_before, s_after, surface,
                 own=()):
    _, layers, rows, width = field.shape
    first_sweep = surface is not None
    whole = lambda shape: pl.BlockSpec(shape, lambda i, *_: (0,) * len(shape))
    at = lambda i, k: jnp.clip(i + k, 0, layers - 1)
    f_spec = lambda k: pl.BlockSpec((3, 1, rows, width), lambda i, *_: (0, at(i, k), 0, 0))
    s_spec = lambda k: pl.BlockSpec((1, rows, width), lambda i, *_: (at(i, k), 0, 0))
    f_edge = whole((3, layers, width))
    s_edge = pl.BlockSpec((1, layers, width), lambda i, *_: (3, 0, 0))
    sides = (-1, 0, 1)
    args = [field] * 3 + [stiffness] * 3 + [before, after, s_before, s_after]
    in_specs = [f_spec(k) for k in sides] + [s_spec(k) for k in sides]
    in_specs += [f_edge, f_edge, s_edge, s_edge]
    out_shape = [jax.ShapeDtypeStruct(field.shape, jnp.float32),
                 jax.ShapeDtypeStruct((2, rows, width), jnp.float32)]
    out_specs = [f_spec(0),
                 pl.BlockSpec((1, rows, width), lambda i, *_: (i // (layers // 2), 0, 0))]
    if first_sweep:
        args.append(surface)
        in_specs.append(whole(surface.shape))
        args += [before, after, *own]
        near = pl.BlockSpec((4, layers, width), lambda i, *_: (0, 0, 0))
        far = pl.BlockSpec((4, layers, width), lambda i, *_: (1, 0, 0))
        in_specs += [far, far, near, near]
        out_shape += [jax.ShapeDtypeStruct((3, layers, width), jnp.float32)] * 2
        out_specs += [f_edge] * 2
    return pl.pallas_call(
        functools.partial(layer_kernel, first_sweep),
        name="relax_layers_first" if first_sweep else "relax_layers_second",
        grid_spec=pltpu.PrefetchScalarGridSpec(
            num_scalar_prefetch=1, grid=(layers,), in_specs=in_specs, out_specs=out_specs
        ),
        out_shape=out_shape,
        compiler_params=pltpu.CompilerParams(vmem_limit_bytes=VMEM_LIMIT),
    )(position, *args)


def finish_first_kernel(face, *refs):
    where_ref, sums, s_here, totals, outer, s_outer = refs[:6]
    out, send, first_row, last_row = refs[-4:]
    ntiles = sums.shape[2] // 8
    pinned = where_ref[1] == 1
    if len(refs) > 10:
        first_row[...] = refs[6][...]
        last_row[...] = refs[7][...]
    else:
        first_row[...] = jnp.zeros_like(first_row)
        last_row[...] = jnp.zeros_like(last_row)
    for t in range(ntiles):
        at = slice(8 * t, 8 * t + 8)
        weight = s_here[0, at, :] + s_outer[0, at, :]
        inverse = 1.0 / (totals[0, at, :] + weight)
        for c in range(3):
            so_far = sums[c, 0, at, :]
            value = (so_far + weight * outer[c, at, :]) * inverse
            if face == 0 and c == 0:
                value = jnp.where(pinned, so_far, value)
            out[c, 0, at, :] = value
            send[c, at, :] = value
            k = 2 * c + face
            if t == 0:
                first_row[k : k + 1, :] = value[0:1]
            if t == ntiles - 1:
                last_row[k : k + 1, :] = value[7:8]


def finish_first(position, face, field, stiffness, totals, outer, edges):
    _, layers, rows, width = field.shape
    layer = face * (layers - 1)
    block = lambda shape, *at: pl.BlockSpec(shape, lambda i, *_: at)
    plane = block((3, rows, width), 0, 0, 0)
    own = block((3, 1, rows, width), 0, layer, 0, 0)
    edge = block((8, width), 0, 0)
    args = [field, stiffness, totals, outer, outer]
    in_specs = [own, block((1, rows, width), layer, 0, 0), block((1, rows, width), face, 0, 0),
                plane, block((1, rows, width), 3, 0, 0)]
    if edges is not None:
        args += edges
        in_specs += [edge, edge]
    edge_shape = jax.ShapeDtypeStruct((8, width), jnp.float32)
    return pl.pallas_call(
        functools.partial(finish_first_kernel, face),
        name="finish_first",
        grid_spec=pltpu.PrefetchScalarGridSpec(
            num_scalar_prefetch=1, grid=(1,), in_specs=in_specs,
            out_specs=[own, plane, edge, edge],
        ),
        out_shape=[jax.ShapeDtypeStruct(field.shape, jnp.float32),
                   jax.ShapeDtypeStruct((3, rows, width), jnp.float32),
                   edge_shape, edge_shape],
        input_output_aliases={1: 0},
        compiler_params=pltpu.CompilerParams(vmem_limit_bytes=VMEM_LIMIT),
    )(position, *args)


def finish_second_kernel(where_ref, sums, s_here, totals, low, high, s_low, s_high,
                         before, after, s_before, s_after, out):
    ntiles = sums.shape[2] // 8
    pinned = where_ref[1] == 1
    row = lax.broadcasted_iota(jnp.int32, (8, 1), 0)

    def one(face, outer, s_outer):
        layer = face * (s_before.shape[1] - 1)
        for t in range(ntiles):
            at = slice(8 * t, 8 * t + 8)
            here = s_here[0, at, :]
            weight = here + s_outer[0, at, :]
            inverse = 1.0 / (totals[0, at, :] + weight)
            for c in range(3):
                so_far = sums[c, 0, at, :]
                value = so_far + weight * outer[c, at, :]
                k = 2 * c + face
                if t == 0:
                    side = here + s_before[0, layer : layer + 1, :]
                    value = value + jnp.where(row == 0, side * before[k : k + 1, :], 0.0)
                if t == ntiles - 1:
                    side = here + s_after[0, layer : layer + 1, :]
                    value = value + jnp.where(row == 7, side * after[k : k + 1, :], 0.0)
                value = value * inverse
                if face == 0 and c == 0:
                    value = jnp.where(pinned, so_far, value)
                out[c, 0, at, :] = value

    step = pl.program_id(0)
    pl.when(step == 0)(lambda: one(0, low, s_low))
    pl.when(step == 1)(lambda: one(1, high, s_high))


def finish_second(position, field, stiffness, totals, low, high, s_low, s_high,
                  before, after, s_before, s_after):
    _, layers, rows, width = field.shape
    block = lambda shape, at: pl.BlockSpec(shape, lambda i, *_: at(i))
    layer = lambda i: i * (layers - 1)
    plane = block((3, rows, width), lambda i: (0, 0, 0))
    s_plane = block((1, rows, width), lambda i: (3, 0, 0))
    own = block((3, 1, rows, width), lambda i: (0, layer(i), 0, 0))
    edge = block((8, width), lambda i: (0, 0))
    s_edge = block((1, layers, width), lambda i: (3, 0, 0))
    return pl.pallas_call(
        finish_second_kernel,
        name="finish_second",
        grid_spec=pltpu.PrefetchScalarGridSpec(
            num_scalar_prefetch=1, grid=(2,),
            in_specs=[own, block((1, rows, width), lambda i: (layer(i), 0, 0)),
                      block((1, rows, width), lambda i: (i, 0, 0)),
                      plane, plane, s_plane, s_plane, edge, edge, s_edge, s_edge],
            out_specs=own,
        ),
        out_shape=jax.ShapeDtypeStruct(field.shape, jnp.float32),
        input_output_aliases={1: 0},
        compiler_params=pltpu.CompilerParams(vmem_limit_bytes=VMEM_LIMIT),
    )(position, field, stiffness, totals, low, high, s_low, s_high,
      before, after, s_before, s_after)


def per_device(
    displacement,
    stiffness,
    node_list,
    active_count,
    wear_class,
    pressure,
    slip_speed,
    rate_table,
    tile_owner,
    node_cell,
):
    rows, width = displacement.shape[2:]
    position = jnp.stack(
        [lax.axis_index("tan"), (lax.axis_index("depth") == 0).astype(jnp.int32)]
    ).astype(jnp.int32)

    row_first, row_last = pack_rows(displacement, stiffness)
    wear = archard(wear_class, pressure, slip_speed, rate_table)
    other = swap_halves(wear)
    before, after = shift_both(row_last, row_first, "tan")
    face_first, face_last = pack_faces(displacement, stiffness, row_first)
    face_first, face_last, other, before, after = lax.optimization_barrier(
        (face_first, face_last, other, before, after)
    )
    low, high = shift_both(face_last, face_first, "depth")
    wear = gather_wear(wear, other)
    surface = paint(position, tile_owner, active_count, wear, node_list,
                    node_cell.reshape(-1, 128), rows, width, wear_class.shape[0])

    first, totals, before_2, after_2 = relax_layers(
        position, displacement, stiffness, before, after, before, after, surface,
        (row_first, row_last),
    )
    first, send_last, edge_first, edge_last = finish_first(
        position, 1, first, stiffness, totals, high, None
    )
    first, send_first, edge_first, edge_last = finish_first(
        position, 0, first, stiffness, totals, low, (edge_first, edge_last)
    )
    low_2, high_2 = shift_both(send_last, send_first, "depth")
    edge_before, edge_after = shift_both(edge_last, edge_first, "tan")
    result, totals = relax_layers(
        position, first, stiffness, before_2, after_2, before, after, None
    )
    return finish_second(position, result, stiffness, totals, low_2, high_2, low, high,
                         edge_before, edge_after, before, after)


def solution(mesh):
    in_specs = (
        P(None, "depth", "tan", None),
        P("depth", "tan", None),
        P(),
        P(),
        P("tan", None),
        P("tan", None),
        P("tan", None),
        P(),
        P(),
        P(),
    )
    out_specs = P(None, "depth", "tan", None)
    return jax.shard_map(
        per_device, mesh=mesh, in_specs=in_specs, out_specs=out_specs, check_vma=False
    )
```

```python
import functools

import jax
import jax.numpy as jnp
from jax import lax
from jax.experimental import pallas as pl
from jax.experimental.pallas import tpu as pltpu
from jax.sharding import PartitionSpec as P

wear_step = 0.6
hardness = 4.0
GROUP = 8
VMEM_LIMIT = 48 * 1024 * 1024


def shift_both(last, first, axis):
    size = lax.axis_size(axis)
    up = [(i, i + 1) for i in range(size - 1)]
    down = [(j, i) for i, j in up]
    return lax.ppermute(last, axis, up), lax.ppermute(first, axis, down)


def wear_kernel(rates_ref, class_ref, contact_ref, sliding_ref, wear_ref):
    ids = class_ref[...]
    rate = jnp.zeros(ids.shape, jnp.float32)
    for k in range(rates_ref.shape[0]):
        rate = jnp.where(ids == k, rates_ref[k], rate)
    product = contact_ref[...] * sliding_ref[...]
    wear_ref[...] = wear_step * rate * product / (1.0 + product / hardness)


def archard(class_ids, contact, sliding, rates):
    near = pl.BlockSpec(memory_space=pltpu.VMEM)
    return pl.pallas_call(
        wear_kernel,
        name="archard",
        in_specs=[pl.BlockSpec(memory_space=pltpu.SMEM), near, near, near],
        out_specs=near,
        out_shape=jax.ShapeDtypeStruct(contact.shape, jnp.float32),
    )(rates, class_ids, contact, sliding)


def rows_kernel(f_top, s_top, f_bottom, s_bottom, first_ref, last_ref):
    for l in range(f_top.shape[1]):
        for k in range(2):
            first_ref[4 * k + 3, l : l + 1, :] = s_top[l, k : k + 1, :]
            last_ref[4 * k + 3, l : l + 1, :] = s_bottom[l, 7 - k : 8 - k, :]
            for c in range(3):
                first_ref[4 * k + c, l : l + 1, :] = f_top[c, l, k : k + 1, :]
                last_ref[4 * k + c, l : l + 1, :] = f_bottom[c, l, 7 - k : 8 - k, :]


def pack_rows(field, stiffness):
    _, layers, rows, width = field.shape
    bottom = rows // 8 - 1
    f_spec = lambda at: pl.BlockSpec((3, layers, 8, width), lambda i: (0, 0, at, 0))
    s_spec = lambda at: pl.BlockSpec((layers, 8, width), lambda i: (0, at, 0))
    out = jax.ShapeDtypeStruct((8, layers, width), jnp.float32)
    out_spec = pl.BlockSpec((8, layers, width), lambda i: (0, 0, 0))
    return pl.pallas_call(
        rows_kernel,
        name="pack_rows",
        grid=(1,),
        in_specs=[f_spec(0), s_spec(0), f_spec(bottom), s_spec(bottom)],
        out_specs=[out_spec, out_spec],
        out_shape=[out, out],
        compiler_params=pltpu.CompilerParams(vmem_limit_bytes=VMEM_LIMIT),
    )(field, stiffness, field, stiffness)


def faces_kernel(field_ref, stiff_ref, first_ref, last_ref):
    step = pl.program_id(0)

    def put(to):
        to[0:3] = field_ref[:, 0]
        to[3:4] = stiff_ref[...]

    pl.when(step == 0)(lambda: put(last_ref))
    pl.when(step == 1)(lambda: put(first_ref))


def pack_faces(field, stiffness):
    _, layers, rows, width = field.shape
    face = jax.ShapeDtypeStruct((4, rows, width), jnp.float32)
    layer = lambda i: (1 - i) * (layers - 1)
    whole = pl.BlockSpec((4, rows, width), lambda i: (0, 0, 0))
    return pl.pallas_call(
        faces_kernel,
        name="pack_faces",
        grid=(2,),
        in_specs=[
            pl.BlockSpec((3, 1, rows, width), lambda i: (0, layer(i), 0, 0)),
            pl.BlockSpec((1, rows, width), lambda i: (layer(i), 0, 0)),
        ],
        out_specs=[whole, whole],
        out_shape=[face, face],
        compiler_params=pltpu.CompilerParams(vmem_limit_bytes=VMEM_LIMIT),
    )(field, stiffness)


def swap_halves(wear):
    size = lax.axis_size("tan")
    return lax.ppermute(wear, "tan", [(i, i ^ 2) for i in range(size)])


def gather_wear(wear, other):
    size = lax.axis_size("tan")
    both = jnp.concatenate([wear, other], axis=0)
    groups = [[i for i in range(size) if (i // 2) % 2 == half] for half in range(2)]
    return lax.all_gather(both, "tan", axis=0, axis_index_groups=groups, tiled=True)


def three_parts(value):
    high = value.astype(jnp.bfloat16).astype(jnp.float32)
    rest = value - high
    middle = rest.astype(jnp.bfloat16).astype(jnp.float32)
    return high, middle, rest - middle


def paint_kernel(
    shard_tiles, where_ref, owner_ref, count_ref, wear_ref, list_ref, table_ref, out_ref,
    own_ref, side_ref, acc_ref, edge_ref,
):
    slots = wear_ref.shape[1]
    ntile = wear_ref.shape[0]
    rows_table = table_ref.shape[0] // ntile
    tile_len = rows_table * 128
    width = out_ref.shape[1]
    rows = out_ref.shape[0] - 16
    me = where_ref[0]
    on_top = where_ref[1]
    out_ref[...] = jnp.zeros_like(out_ref)

    @pl.when(on_top == 1)
    def _():
        acc_ref[...] = jnp.zeros_like(acc_ref)
        edge_ref[...] = jnp.zeros_like(edge_ref)

        def collect(i, carry):
            n_own, n_side = carry
            offset = owner_ref[i] - me
            own_ref[n_own] = i
            side_ref[n_side] = i
            n_own = n_own + jnp.where(offset == 0, 1, 0)
            n_side = n_side + jnp.where(offset * offset == 1, 1, 0)
            return n_own, n_side

        n_own, n_side = lax.fori_loop(
            0, ntile, collect, (jnp.int32(0), jnp.int32(0)), unroll=8
        )

        lane = lax.broadcasted_iota(jnp.int32, (1, slots), 1)
        table_row = lax.broadcasted_iota(jnp.int32, (rows_table, slots), 0)
        block = width // 8
        fine = lax.broadcasted_iota(jnp.int32, (block, slots), 0)
        coarse = lax.broadcasted_iota(jnp.int32, (rows * 8, slots), 0)
        fine_edge = lax.broadcasted_iota(jnp.int32, (128, slots), 0)
        edge_blocks = width // 128
        coarse_edge = lax.broadcasted_iota(jnp.int32, (2 * edge_blocks, slots), 0)

        def entry(tiles_ref, position, total):
            i = tiles_ref[jnp.minimum(position, total - 1)]
            live = jnp.where(position < total, count_ref[i], 0)
            local = list_ref[pl.ds(i, 1), :] - i * tile_len
            table = table_ref[pl.ds(pl.multiple_of(i * rows_table, 8), rows_table), :]
            column = jnp.broadcast_to(local & 127, (rows_table, slots))
            picked = jnp.take_along_axis(table, column, axis=1)
            cell = jnp.sum(
                jnp.where(table_row == (local >> 7), picked, 0), axis=0, keepdims=True
            )
            shard = i // shard_tiles
            half = jnp.where((shard // 2) % 2 == (me // 2) % 2, 0, 1)
            place = (shard // 4) * 4 + (shard % 2) * 2 + half
            at = place * shard_tiles + i % shard_tiles
            wear = jnp.where(lane < live, wear_ref[pl.ds(at, 1), :], 0.0)
            return i, cell, wear

        def one_hot(mask, value):
            return jnp.where(mask, value, 0.0).astype(jnp.bfloat16)

        def add(into_ref, parts, hot):
            total = into_ref[...]
            for part in parts:
                total = total + lax.dot_general(
                    jnp.concatenate(part, axis=1), hot, (((1,), (1,)), ((), ())),
                    preferred_element_type=jnp.float32,
                )
            into_ref[...] = total

        def own_group(g, carry):
            parts = ([], [], [])
            hots = []
            for j in range(GROUP):
                _, cell, wear = entry(own_ref, g * GROUP + j, n_own)
                col = cell % width
                a_index = (col // block) * rows + cell // width
                hots.append(one_hot(fine == col % block, 1.0))
                mask = coarse == a_index
                for part, value in zip(parts, three_parts(wear)):
                    part.append(one_hot(mask, value))
            add(acc_ref, parts, jnp.concatenate(hots, axis=1))
            return carry

        def side_group(g, carry):
            parts = ([], [], [])
            hots = []
            for j in range(GROUP):
                i, cell, wear = entry(side_ref, g * GROUP + j, n_side)
                below = owner_ref[i] > me
                col = cell % width
                wanted = jnp.where(below, 0, rows - 1)
                shift = jnp.where(below, edge_blocks, 0)
                a_index = jnp.where(cell // width == wanted, col // 128 + shift, -1)
                hots.append(one_hot(fine_edge == col % 128, 1.0))
                mask = coarse_edge == a_index
                for part, value in zip(parts, three_parts(wear)):
                    part.append(one_hot(mask, value))
            add(edge_ref, parts, jnp.concatenate(hots, axis=1))
            return carry

        lax.fori_loop(0, (n_own + GROUP - 1) // GROUP, own_group, 0)
        lax.fori_loop(0, (n_side + GROUP - 1) // GROUP, side_group, 0)
        for j in range(8):
            out_ref[8 : 8 + rows, j * block : (j + 1) * block] = acc_ref[
                j * rows : (j + 1) * rows, :
            ]
        for j in range(edge_blocks):
            out_ref[7:8, j * 128 : (j + 1) * 128] = edge_ref[j : j + 1, :]
            out_ref[8 + rows : 9 + rows, j * 128 : (j + 1) * 128] = edge_ref[
                edge_blocks + j : edge_blocks + j + 1, :
            ]


def paint(position, owner, counts, wear, lists, table, rows, width, shard_tiles):
    ntile, slots = lists.shape
    whole = lambda shape: pl.BlockSpec(shape, lambda i, *_: (0,) * len(shape))
    return pl.pallas_call(
        functools.partial(paint_kernel, shard_tiles),
        name="paint_band",
        grid_spec=pltpu.PrefetchScalarGridSpec(
            num_scalar_prefetch=3,
            grid=(1,),
            in_specs=[whole(wear.shape), whole(lists.shape), whole(table.shape)],
            out_specs=whole((rows + 16, width)),
            scratch_shapes=[
                pltpu.SMEM((ntile + 1,), jnp.int32),
                pltpu.SMEM((ntile + 1,), jnp.int32),
                pltpu.VMEM((rows * 8, width // 8), jnp.float32),
                pltpu.VMEM((2 * width // 128, 128), jnp.float32),
            ],
        ),
        out_shape=jax.ShapeDtypeStruct((rows + 16, width), jnp.float32),
        compiler_params=pltpu.CompilerParams(vmem_limit_bytes=VMEM_LIMIT),
    )(position, owner, counts, wear, lists, table)


def relax_tile(load, beside, has_high, has_low):
    centers = {}

    def neighbours(c):
        here = load(c, 0)
        centers[c] = here
        width = here.shape[1]
        lane = lax.broadcasted_iota(jnp.int32, here.shape, 1)
        yield load(c, 1)
        yield load(c, -1)
        yield from beside(c, here)
        yield jnp.where(lane == width - 1, 0.0, pltpu.roll(here, width - 1, 1))
        yield jnp.where(lane == 0, 0.0, pltpu.roll(here, 1, 1))

    around = list(neighbours(3))
    weights = [centers[3] + s for s in around]
    weights[0] = weights[0] * has_high
    weights[1] = weights[1] * has_low
    total = weights[0]
    for w in weights[1:]:
        total = total + w
    sums = []
    for c in range(3):
        acc = None
        for w, f in zip(weights, neighbours(c)):
            acc = w * f if acc is None else acc + w * f
        sums.append(acc)
    return sums, total, centers


def relax_outside(out, near, s_near, far, inside, surface, at, layer):
    def load(c, side):
        here = s_near[0] if c == 3 else near[c]
        if c == 0:
            here = here + jnp.where(layer == 0, surface[at : at + 1, :], 0.0)
        return here if side == 0 else pltpu.roll(here, 7 if side == 1 else 1, 0)

    sums, total, _ = relax_tile(load, lambda c, here: (far[c], inside[c]), 1.0, 1.0)
    inverse = 1.0 / total
    between = jnp.logical_and(layer > 0, layer < out.shape[1] - 1)
    kept = jnp.logical_and(between, s_near[0] > 0.0)
    for c in range(3):
        out[c] = jnp.where(kept, sums[c] * inverse, 0.0)


def layer_kernel(first_sweep, *refs):
    (where_ref, low, mid, high, s_low, s_mid, s_high, before, after, s_before,
     s_after) = refs[:11]
    rest = list(refs[11:])
    surface = rest.pop(0) if first_sweep else None
    if first_sweep:
        face_first, face_last = rest[:2]
        out = rest[6]
        extra = rest[2:6] + rest[7:]
    else:
        out, totals = rest
    layer = pl.program_id(0)
    last = pl.num_programs(0) - 1
    ntiles = mid.shape[2] // 8
    f_refs = {-1: low, 0: mid, 1: high}
    s_refs = {-1: s_low, 0: s_mid, 1: s_high}
    outermost = jnp.logical_or(layer == 0, layer == last)
    row = lax.broadcasted_iota(jnp.int32, (8, 1), 0)
    if first_sweep:

        @pl.when(layer == 0)
        def _():
            far_before, far_after, own_first, own_last, out_before, out_after = extra
            relax_outside(out_before, before, s_before, far_before, own_first, surface, 7, row)
            relax_outside(out_after, after, s_after, far_after, own_last, surface,
                          8 + 8 * ntiles, row)

    has_low = jnp.where(layer == 0, 0.0, 1.0)
    has_high = jnp.where(layer == last, 0.0, 1.0)
    scale = jnp.where(layer == 1, 1.0, 0.0)
    pinned = jnp.logical_and(layer == 0, where_ref[1] == 1)

    def sweep():
        for t in range(ntiles):
            at = slice(8 * t, 8 * t + 8)

            def load(c, side):
                if c == 3:
                    return s_refs[side][0, at, :]
                value = f_refs[side][c, 0, at, :]
                if first_sweep and c == 0 and side < 0:
                    value = value + scale * surface[8 * t + 8 : 8 * t + 16, :]
                return value

            def beside(inside, row, f_edge, s_edge):
                def get(c):
                    if c == 3:
                        if inside:
                            return s_mid[0, row : row + 1, :]
                        return s_edge[0, pl.ds(layer, 1), :]
                    if inside:
                        return mid[c, 0, row : row + 1, :]
                    return f_edge[c, pl.ds(layer, 1), :]
                return get

            above = beside(t > 0, 8 * t - 1, before, s_before)
            below = beside(t < ntiles - 1, 8 * t + 8, after, s_after)

            def rolled(c, here):
                yield jnp.where(row == 7, below(c), pltpu.roll(here, 7, 0))
                yield jnp.where(row == 0, above(c), pltpu.roll(here, 1, 0))

            sums, total, centers = relax_tile(load, rolled, has_high, has_low)
            inverse = 1.0 / total
            if not first_sweep:
                inverse = jnp.where(outermost, 1.0, inverse)
            outs = [part * inverse for part in sums]
            if not first_sweep:
                outs[0] = jnp.where(pinned, centers[0], outs[0])
                totals[0, at, :] = total
            for c in range(3):
                out[c, 0, at, :] = outs[c]

    if not first_sweep:
        sweep()
        return
    pl.when(jnp.logical_not(outermost))(sweep)

    @pl.when(layer == last)
    def _():
        out[:, 0] = face_last[...]

    @pl.when(layer == 0)
    def _():
        out[1:3, 0] = face_first[1:3]
        held = mid[0, 0] + surface[8 : 8 + 8 * ntiles, :]
        out[0, 0] = jnp.where(where_ref[1] == 1, held, face_first[0])


def relax_layers(position, field, stiffness, before, after, s_before, s_after, surface=None,
                 faces=(), own=()):
    _, layers, rows, width = field.shape
    first_sweep = surface is not None
    whole = lambda shape: pl.BlockSpec(shape, lambda i, *_: (0,) * len(shape))
    at = lambda i, k: jnp.clip(i + k, 0, layers - 1)
    f_spec = lambda k: pl.BlockSpec((3, 1, rows, width), lambda i, *_: (0, at(i, k), 0, 0))
    s_spec = lambda k: pl.BlockSpec((1, rows, width), lambda i, *_: (at(i, k), 0, 0))
    f_edge = whole((3, layers, width))
    s_edge = pl.BlockSpec((1, layers, width), lambda i, *_: (3, 0, 0))
    sides = (-1, 0, 1)
    args = [field] * 3 + [stiffness] * 3 + [before, after, s_before, s_after]
    in_specs = [f_spec(k) for k in sides] + [s_spec(k) for k in sides]
    in_specs += [f_edge, f_edge, s_edge, s_edge]
    out_shape = [jax.ShapeDtypeStruct(field.shape, jnp.float32)]
    out_specs = [f_spec(0)]
    if not first_sweep:
        out_shape.append(jax.ShapeDtypeStruct((2, rows, width), jnp.float32))
        out_specs.append(
            pl.BlockSpec((1, rows, width), lambda i, *_: (jnp.minimum(i, 1), 0, 0)))
    else:
        args += [surface, *faces, before, after, *own]
        in_specs += [whole(surface.shape)] + [whole((3, rows, width))] * 2
        near = pl.BlockSpec((4, layers, width), lambda i, *_: (0, 0, 0))
        far = pl.BlockSpec((4, layers, width), lambda i, *_: (1, 0, 0))
        in_specs += [far, far, near, near]
        out_shape += [jax.ShapeDtypeStruct((3, layers, width), jnp.float32)] * 2
        out_specs += [f_edge] * 2
    return pl.pallas_call(
        functools.partial(layer_kernel, first_sweep),
        name="relax_layers_first" if first_sweep else "relax_layers_second",
        grid_spec=pltpu.PrefetchScalarGridSpec(
            num_scalar_prefetch=1, grid=(layers,), in_specs=in_specs, out_specs=out_specs
        ),
        out_shape=out_shape,
        compiler_params=pltpu.CompilerParams(vmem_limit_bytes=VMEM_LIMIT),
    )(position, *args)


def face_sums_kernel(here, inside, s_here, s_inside, sums, totals):
    ntiles = here.shape[2] // 8
    row = lax.broadcasted_iota(jnp.int32, (8, 1), 0)
    for t in range(ntiles):
        at = slice(8 * t, 8 * t + 8)

        def load(c, side):
            if side == 0:
                return s_here[0, at, :] if c == 3 else here[c, 0, at, :]
            return s_inside[0, at, :] if c == 3 else inside[c, 0, at, :]

        def beside(c, tile):
            def take(k, missing, own):
                if missing:
                    return -s_here[0, own : own + 1, :] if c == 3 else 0.0
                return s_here[0, k : k + 1, :] if c == 3 else here[c, 0, k : k + 1, :]

            below = take(8 * t + 8, t == ntiles - 1, 8 * t + 7)
            above = take(8 * t - 1, t == 0, 8 * t)
            yield jnp.where(row == 7, below, pltpu.roll(tile, 7, 0))
            yield jnp.where(row == 0, above, pltpu.roll(tile, 1, 0))

        parts, total, _ = relax_tile(load, beside, 1.0, 0.0)
        for c in range(3):
            sums[c, 0, at, :] = parts[c]
        totals[0, at, :] = total


def face_sums(field, stiffness):
    _, layers, rows, width = field.shape
    outer = lambda i: i * (layers - 1)
    inner = lambda i: 1 + i * (layers - 3)
    f_spec = lambda at: pl.BlockSpec((3, 1, rows, width), lambda i: (0, at(i), 0, 0))
    s_spec = lambda at: pl.BlockSpec((1, rows, width), lambda i: (at(i), 0, 0))
    itself = lambda i: i
    return pl.pallas_call(
        face_sums_kernel,
        name="face_sums",
        grid=(2,),
        in_specs=[f_spec(outer), f_spec(inner), s_spec(outer), s_spec(inner)],
        out_specs=[f_spec(itself), s_spec(itself)],
        out_shape=[jax.ShapeDtypeStruct((3, 2, rows, width), jnp.float32),
                   jax.ShapeDtypeStruct((2, rows, width), jnp.float32)],
        compiler_params=pltpu.CompilerParams(vmem_limit_bytes=VMEM_LIMIT),
    )(field, field, stiffness, stiffness)


def finish_first_kernel(sums, s_here, totals, low, high, s_low, s_high, before, after,
                        s_before, s_after, send_first, send_last, first_row, last_row):
    ntiles = sums.shape[2] // 8
    row = lax.broadcasted_iota(jnp.int32, (8, 1), 0)

    def one(face, outer, s_outer, send):
        layer = face * (s_before.shape[1] - 1)
        for t in range(ntiles):
            at = slice(8 * t, 8 * t + 8)
            here = s_here[0, at, :]
            weight = here + s_outer[0, at, :]
            total = totals[0, at, :] + weight
            values = [sums[c, 0, at, :] + weight * outer[c, at, :] for c in range(3)]
            for wanted, k, f_edge, s_edge in ((0, 0, before, s_before),
                                              (ntiles - 1, 7, after, s_after)):
                if t == wanted:
                    side = jnp.where(row == k, here + s_edge[0, layer : layer + 1, :], 0.0)
                    total = total + side
                    for c in range(3):
                        values[c] = values[c] + side * f_edge[c, layer : layer + 1, :]
            inverse = 1.0 / total
            for c in range(3):
                value = values[c] * inverse
                send[c, at, :] = value
                k = 2 * c + face
                if t == 0:
                    first_row[k : k + 1, :] = value[0:1]
                if t == ntiles - 1:
                    last_row[k : k + 1, :] = value[7:8]

    step = pl.program_id(0)

    @pl.when(step == 0)
    def _():
        first_row[...] = jnp.zeros_like(first_row)
        last_row[...] = jnp.zeros_like(last_row)
        one(0, low, s_low, send_first)

    pl.when(step == 1)(lambda: one(1, high, s_high, send_last))


def finish_first(sums, stiffness, totals, low, high, before, after):
    layers = stiffness.shape[0]
    rows, width = sums.shape[2:]
    block = lambda shape, at: pl.BlockSpec(shape, lambda i: at(i))
    plane = block((3, rows, width), lambda i: (0, 0, 0))
    s_plane = block((1, rows, width), lambda i: (3, 0, 0))
    edge = block((8, width), lambda i: (0, 0))
    f_edge = block((3, layers, width), lambda i: (0, 0, 0))
    s_edge = block((1, layers, width), lambda i: (3, 0, 0))
    face_shape = jax.ShapeDtypeStruct((3, rows, width), jnp.float32)
    edge_shape = jax.ShapeDtypeStruct((8, width), jnp.float32)
    return pl.pallas_call(
        finish_first_kernel,
        name="finish_first",
        grid=(2,),
        in_specs=[block((3, 1, rows, width), lambda i: (0, i, 0, 0)),
                  block((1, rows, width), lambda i: (i * (layers - 1), 0, 0)),
                  block((1, rows, width), lambda i: (i, 0, 0)),
                  plane, plane, s_plane, s_plane, f_edge, f_edge, s_edge, s_edge],
        out_specs=[plane, plane, edge, edge],
        out_shape=[face_shape, face_shape, edge_shape, edge_shape],
        compiler_params=pltpu.CompilerParams(vmem_limit_bytes=VMEM_LIMIT),
    )(sums, stiffness, totals, low, high, low, high, before, after, before, after)


def finish_second_kernel(where_ref, sums, s_here, totals, low, high, s_low, s_high,
                         before, after, s_before, s_after, out):
    ntiles = sums.shape[2] // 8
    pinned = where_ref[1] == 1
    row = lax.broadcasted_iota(jnp.int32, (8, 1), 0)

    def one(face, outer, s_outer):
        layer = face * (s_before.shape[1] - 1)
        for t in range(ntiles):
            at = slice(8 * t, 8 * t + 8)
            here = s_here[0, at, :]
            weight = here + s_outer[0, at, :]
            inverse = 1.0 / (totals[0, at, :] + weight)
            for c in range(3):
                so_far = sums[c, 0, at, :]
                value = so_far + weight * outer[c, at, :]
                k = 2 * c + face
                if t == 0:
                    side = here + s_before[0, layer : layer + 1, :]
                    value = value + jnp.where(row == 0, side * before[k : k + 1, :], 0.0)
                if t == ntiles - 1:
                    side = here + s_after[0, layer : layer + 1, :]
                    value = value + jnp.where(row == 7, side * after[k : k + 1, :], 0.0)
                value = value * inverse
                if face == 0 and c == 0:
                    value = jnp.where(pinned, so_far, value)
                out[c, 0, at, :] = value

    step = pl.program_id(0)
    pl.when(step == 0)(lambda: one(0, low, s_low))
    pl.when(step == 1)(lambda: one(1, high, s_high))


def finish_second(position, field, stiffness, totals, low, high, s_low, s_high,
                  before, after, s_before, s_after):
    _, layers, rows, width = field.shape
    block = lambda shape, at: pl.BlockSpec(shape, lambda i, *_: at(i))
    layer = lambda i: i * (layers - 1)
    plane = block((3, rows, width), lambda i: (0, 0, 0))
    s_plane = block((1, rows, width), lambda i: (3, 0, 0))
    own = block((3, 1, rows, width), lambda i: (0, layer(i), 0, 0))
    edge = block((8, width), lambda i: (0, 0))
    s_edge = block((1, layers, width), lambda i: (3, 0, 0))
    return pl.pallas_call(
        finish_second_kernel,
        name="finish_second",
        grid_spec=pltpu.PrefetchScalarGridSpec(
            num_scalar_prefetch=1, grid=(2,),
            in_specs=[own, block((1, rows, width), lambda i: (layer(i), 0, 0)),
                      block((1, rows, width), lambda i: (i, 0, 0)),
                      plane, plane, s_plane, s_plane, edge, edge, s_edge, s_edge],
            out_specs=own,
        ),
        out_shape=jax.ShapeDtypeStruct(field.shape, jnp.float32),
        input_output_aliases={1: 0},
        compiler_params=pltpu.CompilerParams(vmem_limit_bytes=VMEM_LIMIT),
    )(position, field, stiffness, totals, low, high, s_low, s_high,
      before, after, s_before, s_after)


def per_device(
    displacement,
    stiffness,
    node_list,
    active_count,
    wear_class,
    pressure,
    slip_speed,
    rate_table,
    tile_owner,
    node_cell,
):
    rows, width = displacement.shape[2:]
    position = jnp.stack(
        [lax.axis_index("tan"), (lax.axis_index("depth") == 0).astype(jnp.int32)]
    ).astype(jnp.int32)

    face_first, face_last = pack_faces(displacement, stiffness)
    low, high = shift_both(face_last, face_first, "depth")
    row_first, row_last = pack_rows(displacement, stiffness)
    before, after = shift_both(row_last, row_first, "tan")
    wear = archard(wear_class, pressure, slip_speed, rate_table)
    wear = gather_wear(wear, swap_halves(wear))
    surface = paint(position, tile_owner, active_count, wear, node_list,
                    node_cell.reshape(-1, 128), rows, width, wear_class.shape[0])
    sums, totals = face_sums(displacement, stiffness)

    low, high, surface = lax.optimization_barrier((low, high, surface))
    face_first, face_last, edge_first, edge_last = finish_first(
        sums, stiffness, totals, low, high, before, after
    )
    low_2, high_2 = shift_both(face_last, face_first, "depth")
    edge_before, edge_after = shift_both(edge_last, edge_first, "tan")
    first, before_2, after_2 = relax_layers(
        position, displacement, stiffness, before, after, before, after, surface,
        (face_first, face_last), (row_first, row_last),
    )
    result, totals = relax_layers(
        position, first, stiffness, before_2, after_2, before, after
    )
    return finish_second(position, result, stiffness, totals, low_2, high_2, low, high,
                         edge_before, edge_after, before, after)


def solution(mesh):
    in_specs = (
        P(None, "depth", "tan", None),
        P("depth", "tan", None),
        P(),
        P(),
        P("tan", None),
        P("tan", None),
        P("tan", None),
        P(),
        P(),
        P(),
    )
    out_specs = P(None, "depth", "tan", None)
    return jax.shard_map(
        per_device, mesh=mesh, in_specs=in_specs, out_specs=out_specs, check_vma=False
    )
```

```python
import functools

import jax
import jax.numpy as jnp
from jax import lax
from jax.experimental import pallas as pl
from jax.experimental.pallas import tpu as pltpu
from jax.sharding import PartitionSpec as P

wear_step = 0.6
hardness = 4.0
GROUP = 8
VMEM_LIMIT = 48 * 1024 * 1024


def shift_both(last, first, axis):
    size = lax.axis_size(axis)
    up = [(i, i + 1) for i in range(size - 1)]
    down = [(j, i) for i, j in up]
    return lax.ppermute(last, axis, up), lax.ppermute(first, axis, down)


def wear_kernel(rates_ref, class_ref, contact_ref, sliding_ref, wear_ref):
    ids = class_ref[...]
    rate = jnp.zeros(ids.shape, jnp.float32)
    for k in range(rates_ref.shape[0]):
        rate = jnp.where(ids == k, rates_ref[k], rate)
    product = contact_ref[...] * sliding_ref[...]
    wear_ref[...] = wear_step * rate * product / (1.0 + product / hardness)


def archard(class_ids, contact, sliding, rates):
    near = pl.BlockSpec(memory_space=pltpu.VMEM)
    return pl.pallas_call(
        wear_kernel,
        name="archard",
        in_specs=[pl.BlockSpec(memory_space=pltpu.SMEM), near, near, near],
        out_specs=near,
        out_shape=jax.ShapeDtypeStruct(contact.shape, jnp.float32),
    )(rates, class_ids, contact, sliding)


def rows_kernel(f_top, s_top, f_bottom, s_bottom, first_ref, last_ref):
    for l in range(f_top.shape[1]):
        for k in range(2):
            first_ref[4 * k + 3, l : l + 1, :] = s_top[l, k : k + 1, :]
            last_ref[4 * k + 3, l : l + 1, :] = s_bottom[l, 7 - k : 8 - k, :]
            for c in range(3):
                first_ref[4 * k + c, l : l + 1, :] = f_top[c, l, k : k + 1, :]
                last_ref[4 * k + c, l : l + 1, :] = f_bottom[c, l, 7 - k : 8 - k, :]


def pack_rows(field, stiffness):
    _, layers, rows, width = field.shape
    bottom = rows // 8 - 1
    f_spec = lambda at: pl.BlockSpec((3, layers, 8, width), lambda i: (0, 0, at, 0))
    s_spec = lambda at: pl.BlockSpec((layers, 8, width), lambda i: (0, at, 0))
    out = jax.ShapeDtypeStruct((8, layers, width), jnp.float32)
    out_spec = pl.BlockSpec((8, layers, width), lambda i: (0, 0, 0))
    return pl.pallas_call(
        rows_kernel,
        name="pack_rows",
        grid=(1,),
        in_specs=[f_spec(0), s_spec(0), f_spec(bottom), s_spec(bottom)],
        out_specs=[out_spec, out_spec],
        out_shape=[out, out],
        compiler_params=pltpu.CompilerParams(vmem_limit_bytes=VMEM_LIMIT),
    )(field, stiffness, field, stiffness)


def faces_kernel(field_ref, stiff_ref, first_ref, last_ref):
    step = pl.program_id(0)

    def put(to):
        to[0:3] = field_ref[:, 0]
        to[3:4] = stiff_ref[...]

    pl.when(step == 0)(lambda: put(last_ref))
    pl.when(step == 1)(lambda: put(first_ref))


def pack_faces(field, stiffness):
    _, layers, rows, width = field.shape
    face = jax.ShapeDtypeStruct((4, rows, width), jnp.float32)
    layer = lambda i: (1 - i) * (layers - 1)
    whole = pl.BlockSpec((4, rows, width), lambda i: (0, 0, 0))
    return pl.pallas_call(
        faces_kernel,
        name="pack_faces",
        grid=(2,),
        in_specs=[
            pl.BlockSpec((3, 1, rows, width), lambda i: (0, layer(i), 0, 0)),
            pl.BlockSpec((1, rows, width), lambda i: (layer(i), 0, 0)),
        ],
        out_specs=[whole, whole],
        out_shape=[face, face],
        compiler_params=pltpu.CompilerParams(vmem_limit_bytes=VMEM_LIMIT),
    )(field, stiffness)


def gather_wear(wear):
    size = lax.axis_size("tan")
    groups = [[i for i in range(size) if (i // 2) % 2 == half] for half in range(2)]
    own = lax.all_gather(wear, "tan", axis=0, axis_index_groups=groups, tiled=True)
    return own, lax.ppermute(own, "tan", [(i, i ^ 2) for i in range(size)])


def three_parts(value):
    high = value.astype(jnp.bfloat16).astype(jnp.float32)
    rest = value - high
    middle = rest.astype(jnp.bfloat16).astype(jnp.float32)
    return high, middle, rest - middle


def paint_kernel(
    shard_tiles, where_ref, owner_ref, count_ref, wear_ref, list_ref, table_ref, out_ref,
    own_ref, side_ref, acc_ref, edge_ref,
):
    slots = wear_ref.shape[1]
    ntile = wear_ref.shape[0]
    rows_table = table_ref.shape[0] // ntile
    tile_len = rows_table * 128
    width = out_ref.shape[1]
    rows = out_ref.shape[0] - 16
    me = where_ref[0]
    on_top = where_ref[1]
    out_ref[...] = jnp.zeros_like(out_ref)

    @pl.when(on_top == 1)
    def _():
        acc_ref[...] = jnp.zeros_like(acc_ref)
        edge_ref[...] = jnp.zeros_like(edge_ref)

        def collect(i, carry):
            n_own, n_side = carry
            offset = owner_ref[i] - me
            own_ref[n_own] = i
            side_ref[n_side] = i
            n_own = n_own + jnp.where(offset == 0, 1, 0)
            n_side = n_side + jnp.where(offset * offset == 1, 1, 0)
            return n_own, n_side

        n_own, n_side = lax.fori_loop(
            0, ntile, collect, (jnp.int32(0), jnp.int32(0)), unroll=8
        )

        lane = lax.broadcasted_iota(jnp.int32, (1, slots), 1)
        table_row = lax.broadcasted_iota(jnp.int32, (rows_table, slots), 0)
        block = width // 8
        fine = lax.broadcasted_iota(jnp.int32, (block, slots), 0)
        coarse = lax.broadcasted_iota(jnp.int32, (rows * 8, slots), 0)
        fine_edge = lax.broadcasted_iota(jnp.int32, (128, slots), 0)
        edge_blocks = width // 128
        coarse_edge = lax.broadcasted_iota(jnp.int32, (2 * edge_blocks, slots), 0)

        def entry(tiles_ref, position, total):
            i = tiles_ref[jnp.minimum(position, total - 1)]
            live = jnp.where(position < total, count_ref[i], 0)
            local = list_ref[pl.ds(i, 1), :] - i * tile_len
            table = table_ref[pl.ds(pl.multiple_of(i * rows_table, 8), rows_table), :]
            column = jnp.broadcast_to(local & 127, (rows_table, slots))
            picked = jnp.take_along_axis(table, column, axis=1)
            cell = jnp.sum(
                jnp.where(table_row == (local >> 7), picked, 0), axis=0, keepdims=True
            )
            shard = i // shard_tiles
            half = jnp.where((shard // 2) % 2 == (me // 2) % 2, 0, 1)
            place = half * (ntile // shard_tiles // 2) + (shard // 4) * 2 + shard % 2
            at = place * shard_tiles + i % shard_tiles
            wear = jnp.where(lane < live, wear_ref[pl.ds(at, 1), :], 0.0)
            return i, cell, wear

        def one_hot(mask, value):
            return jnp.where(mask, value, 0.0).astype(jnp.bfloat16)

        def add(into_ref, parts, hot):
            total = into_ref[...]
            for part in parts:
                total = total + lax.dot_general(
                    jnp.concatenate(part, axis=1), hot, (((1,), (1,)), ((), ())),
                    preferred_element_type=jnp.float32,
                )
            into_ref[...] = total

        def own_group(g, carry):
            parts = ([], [], [])
            hots = []
            for j in range(GROUP):
                _, cell, wear = entry(own_ref, g * GROUP + j, n_own)
                col = cell % width
                a_index = (col // block) * rows + cell // width
                hots.append(one_hot(fine == col % block, 1.0))
                mask = coarse == a_index
                for part, value in zip(parts, three_parts(wear)):
                    part.append(one_hot(mask, value))
            add(acc_ref, parts, jnp.concatenate(hots, axis=1))
            return carry

        def side_group(g, carry):
            parts = ([], [], [])
            hots = []
            for j in range(GROUP):
                i, cell, wear = entry(side_ref, g * GROUP + j, n_side)
                below = owner_ref[i] > me
                col = cell % width
                wanted = jnp.where(below, 0, rows - 1)
                shift = jnp.where(below, edge_blocks, 0)
                a_index = jnp.where(cell // width == wanted, col // 128 + shift, -1)
                hots.append(one_hot(fine_edge == col % 128, 1.0))
                mask = coarse_edge == a_index
                for part, value in zip(parts, three_parts(wear)):
                    part.append(one_hot(mask, value))
            add(edge_ref, parts, jnp.concatenate(hots, axis=1))
            return carry

        lax.fori_loop(0, (n_own + GROUP - 1) // GROUP, own_group, 0)
        lax.fori_loop(0, (n_side + GROUP - 1) // GROUP, side_group, 0)
        for j in range(8):
            out_ref[8 : 8 + rows, j * block : (j + 1) * block] = acc_ref[
                j * rows : (j + 1) * rows, :
            ]
        for j in range(edge_blocks):
            out_ref[7:8, j * 128 : (j + 1) * 128] = edge_ref[j : j + 1, :]
            out_ref[8 + rows : 9 + rows, j * 128 : (j + 1) * 128] = edge_ref[
                edge_blocks + j : edge_blocks + j + 1, :
            ]


def paint(position, owner, counts, wear, lists, table, rows, width, shard_tiles):
    ntile, slots = lists.shape
    whole = lambda shape: pl.BlockSpec(shape, lambda i, *_: (0,) * len(shape))
    return pl.pallas_call(
        functools.partial(paint_kernel, shard_tiles),
        name="paint_band",
        grid_spec=pltpu.PrefetchScalarGridSpec(
            num_scalar_prefetch=3,
            grid=(1,),
            in_specs=[whole(wear.shape), whole(lists.shape), whole(table.shape)],
            out_specs=whole((rows + 16, width)),
            scratch_shapes=[
                pltpu.SMEM((ntile + 1,), jnp.int32),
                pltpu.SMEM((ntile + 1,), jnp.int32),
                pltpu.VMEM((rows * 8, width // 8), jnp.float32),
                pltpu.VMEM((2 * width // 128, 128), jnp.float32),
            ],
        ),
        out_shape=jax.ShapeDtypeStruct((rows + 16, width), jnp.float32),
        compiler_params=pltpu.CompilerParams(vmem_limit_bytes=VMEM_LIMIT),
    )(position, owner, counts, wear, lists, table)


def relax_tile(load, beside, has_high, has_low):
    centers = {}

    def neighbours(c):
        here = load(c, 0)
        centers[c] = here
        width = here.shape[1]
        lane = lax.broadcasted_iota(jnp.int32, here.shape, 1)
        yield load(c, 1)
        yield load(c, -1)
        yield from beside(c, here)
        yield jnp.where(lane == width - 1, 0.0, pltpu.roll(here, width - 1, 1))
        yield jnp.where(lane == 0, 0.0, pltpu.roll(here, 1, 1))

    around = list(neighbours(3))
    weights = [centers[3] + s for s in around]
    weights[0] = weights[0] * has_high
    weights[1] = weights[1] * has_low
    total = weights[0]
    for w in weights[1:]:
        total = total + w
    sums = []
    for c in range(3):
        acc = None
        for w, f in zip(weights, neighbours(c)):
            acc = w * f if acc is None else acc + w * f
        sums.append(acc)
    return sums, total, centers


def relax_outside(out, near, s_near, far, inside, surface, at, layer):
    def load(c, side):
        here = s_near[0] if c == 3 else near[c]
        if c == 0:
            here = here + jnp.where(layer == 0, surface[at : at + 1, :], 0.0)
        return here if side == 0 else pltpu.roll(here, 7 if side == 1 else 1, 0)

    sums, total, _ = relax_tile(load, lambda c, here: (far[c], inside[c]), 1.0, 1.0)
    inverse = 1.0 / total
    between = jnp.logical_and(layer > 0, layer < out.shape[1] - 1)
    kept = jnp.logical_and(between, s_near[0] > 0.0)
    for c in range(3):
        out[c] = jnp.where(kept, sums[c] * inverse, 0.0)


def layer_kernel(first_sweep, *refs):
    where_ref, f_in, s_in, before, after, s_before, s_after = refs[:7]
    rest = list(refs[7:-2])
    f_kept, s_kept = refs[-2:]
    surface = rest.pop(0) if first_sweep else None
    if first_sweep:
        face_first, face_last = rest[:2]
        out = rest[6]
        extra = rest[2:6] + rest[7:]
    else:
        out, totals = rest
    step = pl.program_id(0)
    layer = step - 1
    last = pl.num_programs(0) - 2
    slot = step % 2
    ntiles = f_in.shape[2] // 8
    mid, s_mid = f_kept.at[1 - slot], s_kept.at[1 - slot]
    f_refs = {-1: f_kept.at[slot], 0: mid, 1: f_in.at[:, 0]}
    s_refs = {-1: s_kept.at[slot], 0: s_mid, 1: s_in.at[0]}
    outermost = jnp.logical_or(layer == 0, layer == last)
    row = lax.broadcasted_iota(jnp.int32, (8, 1), 0)

    @pl.when(step == 0)
    def _():
        f_kept[1] = f_in[:, 0]
        s_kept[1] = s_in[0]
        if first_sweep:
            far_before, far_after, own_first, own_last, out_before, out_after = extra
            relax_outside(out_before, before, s_before, far_before, own_first, surface, 7, row)
            relax_outside(out_after, after, s_after, far_after, own_last, surface,
                          8 + 8 * ntiles, row)

    has_low = jnp.where(layer == 0, 0.0, 1.0)
    has_high = jnp.where(layer == last, 0.0, 1.0)
    scale = jnp.where(layer == 1, 1.0, 0.0)
    pinned = jnp.logical_and(layer == 0, where_ref[1] == 1)

    def sweep():
        for t in range(ntiles):
            at = slice(8 * t, 8 * t + 8)

            def load(c, side):
                if c == 3:
                    return s_refs[side][at, :]
                value = f_refs[side][c, at, :]
                if first_sweep and c == 0 and side < 0:
                    value = value + scale * surface[8 * t + 8 : 8 * t + 16, :]
                return value

            def beside(inside, row, f_edge, s_edge):
                def get(c):
                    if c == 3:
                        if inside:
                            return s_mid[row : row + 1, :]
                        return s_edge[0, pl.ds(layer, 1), :]
                    if inside:
                        return mid[c, row : row + 1, :]
                    return f_edge[c, pl.ds(layer, 1), :]
                return get

            above = beside(t > 0, 8 * t - 1, before, s_before)
            below = beside(t < ntiles - 1, 8 * t + 8, after, s_after)

            def rolled(c, here):
                yield jnp.where(row == 7, below(c), pltpu.roll(here, 7, 0))
                yield jnp.where(row == 0, above(c), pltpu.roll(here, 1, 0))

            sums, total, centers = relax_tile(load, rolled, has_high, has_low)
            inverse = 1.0 / total
            if not first_sweep:
                inverse = jnp.where(outermost, 1.0, inverse)
            outs = [part * inverse for part in sums]
            if not first_sweep:
                outs[0] = jnp.where(pinned, centers[0], outs[0])
                totals[0, at, :] = total
            for c in range(3):
                out[c, 0, at, :] = outs[c]

    if first_sweep:
        inner = jnp.logical_and(layer > 0, layer < last)
        pl.when(inner)(sweep)

        @pl.when(layer == last)
        def _():
            out[:, 0] = face_last[...]

        @pl.when(layer == 0)
        def _():
            out[1:3, 0] = face_first[1:3]
            held = mid[0] + surface[8 : 8 + 8 * ntiles, :]
            out[0, 0] = jnp.where(where_ref[1] == 1, held, face_first[0])
    else:
        pl.when(layer >= 0)(sweep)

    f_kept[slot] = f_in[:, 0]
    s_kept[slot] = s_in[0]


def relax_layers(position, field, stiffness, before, after, s_before, s_after, surface=None,
                 faces=(), own=()):
    _, layers, rows, width = field.shape
    first_sweep = surface is not None
    whole = lambda shape: pl.BlockSpec(shape, lambda i, *_: (0,) * len(shape))
    came = lambda k: jnp.minimum(k, layers - 1)
    swept = lambda k: jnp.maximum(k - 1, 0)
    f_spec = lambda at: pl.BlockSpec((3, 1, rows, width), lambda k, *_: (0, at(k), 0, 0))
    f_edge = whole((3, layers, width))
    s_edge = pl.BlockSpec((1, layers, width), lambda k, *_: (3, 0, 0))
    args = [field, stiffness, before, after, s_before, s_after]
    in_specs = [f_spec(came), pl.BlockSpec((1, rows, width), lambda k, *_: (came(k), 0, 0))]
    in_specs += [f_edge, f_edge, s_edge, s_edge]
    out_shape = [jax.ShapeDtypeStruct(field.shape, jnp.float32)]
    out_specs = [f_spec(swept)]
    if not first_sweep:
        out_shape.append(jax.ShapeDtypeStruct((2, rows, width), jnp.float32))
        out_specs.append(
            pl.BlockSpec((1, rows, width), lambda k, *_: (jnp.minimum(swept(k), 1), 0, 0)))
    else:
        args += [surface, *faces, before, after, *own]
        in_specs += [whole(surface.shape)] + [whole((3, rows, width))] * 2
        near = pl.BlockSpec((4, layers, width), lambda i, *_: (0, 0, 0))
        far = pl.BlockSpec((4, layers, width), lambda i, *_: (1, 0, 0))
        in_specs += [far, far, near, near]
        out_shape += [jax.ShapeDtypeStruct((3, layers, width), jnp.float32)] * 2
        out_specs += [f_edge] * 2
    return pl.pallas_call(
        functools.partial(layer_kernel, first_sweep),
        name="relax_layers_first" if first_sweep else "relax_layers_second",
        grid_spec=pltpu.PrefetchScalarGridSpec(
            num_scalar_prefetch=1, grid=(layers + 1,), in_specs=in_specs, out_specs=out_specs,
            scratch_shapes=[pltpu.VMEM((2, 3, rows, width), jnp.float32),
                            pltpu.VMEM((2, rows, width), jnp.float32)],
        ),
        out_shape=out_shape,
        compiler_params=pltpu.CompilerParams(vmem_limit_bytes=VMEM_LIMIT),
    )(position, *args)


def face_sums_kernel(here, inside, s_here, s_inside, sums, totals):
    ntiles = here.shape[2] // 8
    row = lax.broadcasted_iota(jnp.int32, (8, 1), 0)
    for t in range(ntiles):
        at = slice(8 * t, 8 * t + 8)

        def load(c, side):
            if side == 0:
                return s_here[0, at, :] if c == 3 else here[c, 0, at, :]
            return s_inside[0, at, :] if c == 3 else inside[c, 0, at, :]

        def beside(c, tile):
            def take(k, missing, own):
                if missing:
                    return -s_here[0, own : own + 1, :] if c == 3 else 0.0
                return s_here[0, k : k + 1, :] if c == 3 else here[c, 0, k : k + 1, :]

            below = take(8 * t + 8, t == ntiles - 1, 8 * t + 7)
            above = take(8 * t - 1, t == 0, 8 * t)
            yield jnp.where(row == 7, below, pltpu.roll(tile, 7, 0))
            yield jnp.where(row == 0, above, pltpu.roll(tile, 1, 0))

        parts, total, _ = relax_tile(load, beside, 1.0, 0.0)
        for c in range(3):
            sums[c, 0, at, :] = parts[c]
        totals[0, at, :] = total


def face_sums(field, stiffness):
    _, layers, rows, width = field.shape
    outer = lambda i: i * (layers - 1)
    inner = lambda i: 1 + i * (layers - 3)
    f_spec = lambda at: pl.BlockSpec((3, 1, rows, width), lambda i: (0, at(i), 0, 0))
    s_spec = lambda at: pl.BlockSpec((1, rows, width), lambda i: (at(i), 0, 0))
    itself = lambda i: i
    return pl.pallas_call(
        face_sums_kernel,
        name="face_sums",
        grid=(2,),
        in_specs=[f_spec(outer), f_spec(inner), s_spec(outer), s_spec(inner)],
        out_specs=[f_spec(itself), s_spec(itself)],
        out_shape=[jax.ShapeDtypeStruct((3, 2, rows, width), jnp.float32),
                   jax.ShapeDtypeStruct((2, rows, width), jnp.float32)],
        compiler_params=pltpu.CompilerParams(vmem_limit_bytes=VMEM_LIMIT),
    )(field, field, stiffness, stiffness)


def finish_first_kernel(sums, s_here, totals, low, high, s_low, s_high, before, after,
                        s_before, s_after, send_first, send_last, first_row, last_row):
    ntiles = sums.shape[2] // 8
    row = lax.broadcasted_iota(jnp.int32, (8, 1), 0)

    def one(face, outer, s_outer, send):
        layer = face * (s_before.shape[1] - 1)
        for t in range(ntiles):
            at = slice(8 * t, 8 * t + 8)
            here = s_here[0, at, :]
            weight = here + s_outer[0, at, :]
            total = totals[0, at, :] + weight
            values = [sums[c, 0, at, :] + weight * outer[c, at, :] for c in range(3)]
            for wanted, k, f_edge, s_edge in ((0, 0, before, s_before),
                                              (ntiles - 1, 7, after, s_after)):
                if t == wanted:
                    side = jnp.where(row == k, here + s_edge[0, layer : layer + 1, :], 0.0)
                    total = total + side
                    for c in range(3):
                        values[c] = values[c] + side * f_edge[c, layer : layer + 1, :]
            inverse = 1.0 / total
            for c in range(3):
                value = values[c] * inverse
                send[c, at, :] = value
                k = 2 * c + face
                if t == 0:
                    first_row[k : k + 1, :] = value[0:1]
                if t == ntiles - 1:
                    last_row[k : k + 1, :] = value[7:8]

    step = pl.program_id(0)

    @pl.when(step == 0)
    def _():
        first_row[...] = jnp.zeros_like(first_row)
        last_row[...] = jnp.zeros_like(last_row)
        one(0, low, s_low, send_first)

    pl.when(step == 1)(lambda: one(1, high, s_high, send_last))


def finish_first(sums, stiffness, totals, low, high, before, after):
    layers = stiffness.shape[0]
    rows, width = sums.shape[2:]
    block = lambda shape, at: pl.BlockSpec(shape, lambda i: at(i))
    plane = block((3, rows, width), lambda i: (0, 0, 0))
    s_plane = block((1, rows, width), lambda i: (3, 0, 0))
    edge = block((8, width), lambda i: (0, 0))
    f_edge = block((3, layers, width), lambda i: (0, 0, 0))
    s_edge = block((1, layers, width), lambda i: (3, 0, 0))
    face_shape = jax.ShapeDtypeStruct((3, rows, width), jnp.float32)
    edge_shape = jax.ShapeDtypeStruct((8, width), jnp.float32)
    return pl.pallas_call(
        finish_first_kernel,
        name="finish_first",
        grid=(2,),
        in_specs=[block((3, 1, rows, width), lambda i: (0, i, 0, 0)),
                  block((1, rows, width), lambda i: (i * (layers - 1), 0, 0)),
                  block((1, rows, width), lambda i: (i, 0, 0)),
                  plane, plane, s_plane, s_plane, f_edge, f_edge, s_edge, s_edge],
        out_specs=[plane, plane, edge, edge],
        out_shape=[face_shape, face_shape, edge_shape, edge_shape],
        compiler_params=pltpu.CompilerParams(vmem_limit_bytes=VMEM_LIMIT),
    )(sums, stiffness, totals, low, high, low, high, before, after, before, after)


def finish_second_kernel(where_ref, sums, s_here, totals, low, high, s_low, s_high,
                         before, after, s_before, s_after, out):
    ntiles = sums.shape[2] // 8
    pinned = where_ref[1] == 1
    row = lax.broadcasted_iota(jnp.int32, (8, 1), 0)

    def one(face, outer, s_outer):
        layer = face * (s_before.shape[1] - 1)
        for t in range(ntiles):
            at = slice(8 * t, 8 * t + 8)
            here = s_here[0, at, :]
            weight = here + s_outer[0, at, :]
            inverse = 1.0 / (totals[0, at, :] + weight)
            for c in range(3):
                so_far = sums[c, 0, at, :]
                value = so_far + weight * outer[c, at, :]
                k = 2 * c + face
                if t == 0:
                    side = here + s_before[0, layer : layer + 1, :]
                    value = value + jnp.where(row == 0, side * before[k : k + 1, :], 0.0)
                if t == ntiles - 1:
                    side = here + s_after[0, layer : layer + 1, :]
                    value = value + jnp.where(row == 7, side * after[k : k + 1, :], 0.0)
                value = value * inverse
                if face == 0 and c == 0:
                    value = jnp.where(pinned, so_far, value)
                out[c, 0, at, :] = value

    step = pl.program_id(0)
    pl.when(step == 0)(lambda: one(0, low, s_low))
    pl.when(step == 1)(lambda: one(1, high, s_high))


def finish_second(position, field, stiffness, totals, low, high, s_low, s_high,
                  before, after, s_before, s_after):
    _, layers, rows, width = field.shape
    block = lambda shape, at: pl.BlockSpec(shape, lambda i, *_: at(i))
    layer = lambda i: i * (layers - 1)
    plane = block((3, rows, width), lambda i: (0, 0, 0))
    s_plane = block((1, rows, width), lambda i: (3, 0, 0))
    own = block((3, 1, rows, width), lambda i: (0, layer(i), 0, 0))
    edge = block((8, width), lambda i: (0, 0))
    s_edge = block((1, layers, width), lambda i: (3, 0, 0))
    return pl.pallas_call(
        finish_second_kernel,
        name="finish_second",
        grid_spec=pltpu.PrefetchScalarGridSpec(
            num_scalar_prefetch=1, grid=(2,),
            in_specs=[own, block((1, rows, width), lambda i: (layer(i), 0, 0)),
                      block((1, rows, width), lambda i: (i, 0, 0)),
                      plane, plane, s_plane, s_plane, edge, edge, s_edge, s_edge],
            out_specs=own,
        ),
        out_shape=jax.ShapeDtypeStruct(field.shape, jnp.float32),
        input_output_aliases={1: 0},
        compiler_params=pltpu.CompilerParams(vmem_limit_bytes=VMEM_LIMIT),
    )(position, field, stiffness, totals, low, high, s_low, s_high,
      before, after, s_before, s_after)


def per_device(
    displacement,
    stiffness,
    node_list,
    active_count,
    wear_class,
    pressure,
    slip_speed,
    rate_table,
    tile_owner,
    node_cell,
):
    rows, width = displacement.shape[2:]
    position = jnp.stack(
        [lax.axis_index("tan"), (lax.axis_index("depth") == 0).astype(jnp.int32)]
    ).astype(jnp.int32)

    face_first, face_last = pack_faces(displacement, stiffness)
    low, high = shift_both(face_last, face_first, "depth")
    row_first, row_last = pack_rows(displacement, stiffness)
    before, after = shift_both(row_last, row_first, "tan")
    wear = archard(wear_class, pressure, slip_speed, rate_table)
    wear = gather_wear(wear)
    sums, totals = face_sums(displacement, stiffness)
    low, high, wear = lax.optimization_barrier((low, high, wear))
    face_first, face_last, edge_first, edge_last = finish_first(
        sums, stiffness, totals, low, high, before, after
    )
    low_2, high_2 = shift_both(face_last, face_first, "depth")
    edge_before, edge_after = shift_both(edge_last, edge_first, "tan")
    surface = paint(position, tile_owner, active_count, jnp.concatenate(wear), node_list,
                    node_cell.reshape(-1, 128), rows, width, wear_class.shape[0])
    first, before_2, after_2 = relax_layers(
        position, displacement, stiffness, before, after, before, after, surface,
        (face_first, face_last), (row_first, row_last),
    )
    result, totals = relax_layers(
        position, first, stiffness, before_2, after_2, before, after
    )
    return finish_second(position, result, stiffness, totals, low_2, high_2, low, high,
                         edge_before, edge_after, before, after)


def solution(mesh):
    in_specs = (
        P(None, "depth", "tan", None),
        P("depth", "tan", None),
        P(),
        P(),
        P("tan", None),
        P("tan", None),
        P("tan", None),
        P(),
        P(),
        P(),
    )
    out_specs = P(None, "depth", "tan", None)
    return jax.shard_map(
        per_device, mesh=mesh, in_specs=in_specs, out_specs=out_specs, check_vma=False
    )
```

```python
import functools

import jax
import jax.numpy as jnp
from jax import lax
from jax.experimental import pallas as pl
from jax.experimental.pallas import tpu as pltpu
from jax.sharding import PartitionSpec as P

wear_step = 0.6
hardness = 4.0
GROUP = 8
VMEM_LIMIT = 48 * 1024 * 1024


def shift_both(last, first, axis):
    size = lax.axis_size(axis)
    up = [(i, i + 1) for i in range(size - 1)]
    down = [(j, i) for i, j in up]
    return lax.ppermute(last, axis, up), lax.ppermute(first, axis, down)


def wear_kernel(rates_ref, class_ref, contact_ref, sliding_ref, wear_ref):
    ids = class_ref[...]
    rate = jnp.zeros(ids.shape, jnp.float32)
    for k in range(rates_ref.shape[0]):
        rate = jnp.where(ids == k, rates_ref[k], rate)
    product = contact_ref[...] * sliding_ref[...]
    wear_ref[...] = wear_step * rate * product / (1.0 + product / hardness)


def archard(class_ids, contact, sliding, rates):
    near = pl.BlockSpec(memory_space=pltpu.VMEM)
    return pl.pallas_call(
        wear_kernel,
        name="archard",
        in_specs=[pl.BlockSpec(memory_space=pltpu.SMEM), near, near, near],
        out_specs=near,
        out_shape=jax.ShapeDtypeStruct(contact.shape, jnp.float32),
    )(rates, class_ids, contact, sliding)


def rows_kernel(f_top, s_top, f_bottom, s_bottom, first_ref, last_ref):
    for l in range(f_top.shape[1]):
        for k in range(2):
            first_ref[4 * k + 3, l : l + 1, :] = s_top[l, k : k + 1, :]
            last_ref[4 * k + 3, l : l + 1, :] = s_bottom[l, 7 - k : 8 - k, :]
            for c in range(3):
                first_ref[4 * k + c, l : l + 1, :] = f_top[c, l, k : k + 1, :]
                last_ref[4 * k + c, l : l + 1, :] = f_bottom[c, l, 7 - k : 8 - k, :]


def pack_rows(field, stiffness):
    _, layers, rows, width = field.shape
    bottom = rows // 8 - 1
    f_spec = lambda at: pl.BlockSpec((3, layers, 8, width), lambda i: (0, 0, at, 0))
    s_spec = lambda at: pl.BlockSpec((layers, 8, width), lambda i: (0, at, 0))
    out = jax.ShapeDtypeStruct((8, layers, width), jnp.float32)
    out_spec = pl.BlockSpec((8, layers, width), lambda i: (0, 0, 0))
    return pl.pallas_call(
        rows_kernel,
        name="pack_rows",
        grid=(1,),
        in_specs=[f_spec(0), s_spec(0), f_spec(bottom), s_spec(bottom)],
        out_specs=[out_spec, out_spec],
        out_shape=[out, out],
        compiler_params=pltpu.CompilerParams(vmem_limit_bytes=VMEM_LIMIT),
    )(field, stiffness, field, stiffness)


def faces_kernel(field_ref, stiff_ref, after_ref, first_ref, last_ref):
    step = pl.program_id(0)

    def put(to):
        to[0:3] = field_ref[:, 0]
        to[3:4] = stiff_ref[...]

    pl.when(step == 0)(lambda: put(last_ref))
    pl.when(step == 1)(lambda: put(first_ref))


def pack_faces(field, stiffness, earlier):
    _, layers, rows, width = field.shape
    face = jax.ShapeDtypeStruct((4, rows, width), jnp.float32)
    layer = lambda i: (1 - i) * (layers - 1)
    whole = pl.BlockSpec((4, rows, width), lambda i: (0, 0, 0))
    return pl.pallas_call(
        faces_kernel,
        name="pack_faces",
        grid=(2,),
        in_specs=[
            pl.BlockSpec((3, 1, rows, width), lambda i: (0, layer(i), 0, 0)),
            pl.BlockSpec((1, rows, width), lambda i: (layer(i), 0, 0)),
            pl.BlockSpec(memory_space=pl.ANY),
        ],
        out_specs=[whole, whole],
        out_shape=[face, face],
        compiler_params=pltpu.CompilerParams(vmem_limit_bytes=VMEM_LIMIT),
    )(field, stiffness, earlier)


def swap_halves(wear):
    size = lax.axis_size("tan")
    return lax.ppermute(wear, "tan", [(i, i ^ 2) for i in range(size)])


def gather_wear(wear, other):
    size = lax.axis_size("tan")
    both = jnp.concatenate([wear, other], axis=0)
    groups = [[i for i in range(size) if (i // 2) % 2 == half] for half in range(2)]
    return lax.all_gather(both, "tan", axis=0, axis_index_groups=groups, tiled=True)


def three_parts(value):
    high = value.astype(jnp.bfloat16).astype(jnp.float32)
    rest = value - high
    middle = rest.astype(jnp.bfloat16).astype(jnp.float32)
    return high, middle, rest - middle


def paint_kernel(
    shard_tiles, where_ref, owner_ref, count_ref, wear_ref, list_ref, table_ref, out_ref,
    own_ref, side_ref, acc_ref, edge_ref,
):
    slots = wear_ref.shape[1]
    ntile = wear_ref.shape[0]
    rows_table = table_ref.shape[0] // ntile
    tile_len = rows_table * 128
    width = out_ref.shape[1]
    rows = out_ref.shape[0] - 16
    me = where_ref[0]
    on_top = where_ref[1]
    out_ref[...] = jnp.zeros_like(out_ref)

    @pl.when(on_top == 1)
    def _():
        acc_ref[...] = jnp.zeros_like(acc_ref)
        edge_ref[...] = jnp.zeros_like(edge_ref)

        def collect(i, carry):
            n_own, n_side = carry
            offset = owner_ref[i] - me
            own_ref[n_own] = i
            side_ref[n_side] = i
            n_own = n_own + jnp.where(offset == 0, 1, 0)
            n_side = n_side + jnp.where(offset * offset == 1, 1, 0)
            return n_own, n_side

        n_own, n_side = lax.fori_loop(
            0, ntile, collect, (jnp.int32(0), jnp.int32(0)), unroll=8
        )

        lane = lax.broadcasted_iota(jnp.int32, (1, slots), 1)
        table_row = lax.broadcasted_iota(jnp.int32, (rows_table, slots), 0)
        block = width // 8
        fine = lax.broadcasted_iota(jnp.int32, (block, slots), 0)
        coarse = lax.broadcasted_iota(jnp.int32, (rows * 8, slots), 0)
        fine_edge = lax.broadcasted_iota(jnp.int32, (128, slots), 0)
        edge_blocks = width // 128
        coarse_edge = lax.broadcasted_iota(jnp.int32, (2 * edge_blocks, slots), 0)

        def entry(tiles_ref, position, total):
            i = tiles_ref[jnp.minimum(position, total - 1)]
            live = jnp.where(position < total, count_ref[i], 0)
            local = list_ref[pl.ds(i, 1), :] - i * tile_len
            table = table_ref[pl.ds(pl.multiple_of(i * rows_table, 8), rows_table), :]
            column = jnp.broadcast_to(local & 127, (rows_table, slots))
            picked = jnp.take_along_axis(table, column, axis=1)
            cell = jnp.sum(
                jnp.where(table_row == (local >> 7), picked, 0), axis=0, keepdims=True
            )
            shard = i // shard_tiles
            half = jnp.where((shard // 2) % 2 == (me // 2) % 2, 0, 1)
            place = (shard // 4) * 4 + (shard % 2) * 2 + half
            at = place * shard_tiles + i % shard_tiles
            wear = jnp.where(lane < live, wear_ref[pl.ds(at, 1), :], 0.0)
            return i, cell, wear

        def one_hot(mask, value):
            return jnp.where(mask, value, 0.0).astype(jnp.bfloat16)

        def add(into_ref, parts, hot):
            total = into_ref[...]
            for part in parts:
                total = total + lax.dot_general(
                    jnp.concatenate(part, axis=1), hot, (((1,), (1,)), ((), ())),
                    preferred_element_type=jnp.float32,
                )
            into_ref[...] = total

        def own_group(g, carry):
            parts = ([], [], [])
            hots = []
            for j in range(GROUP):
                _, cell, wear = entry(own_ref, g * GROUP + j, n_own)
                col = cell % width
                a_index = (col // block) * rows + cell // width
                hots.append(one_hot(fine == col % block, 1.0))
                mask = coarse == a_index
                for part, value in zip(parts, three_parts(wear)):
                    part.append(one_hot(mask, value))
            add(acc_ref, parts, jnp.concatenate(hots, axis=1))
            return carry

        def side_group(g, carry):
            parts = ([], [], [])
            hots = []
            for j in range(GROUP):
                i, cell, wear = entry(side_ref, g * GROUP + j, n_side)
                below = owner_ref[i] > me
                col = cell % width
                wanted = jnp.where(below, 0, rows - 1)
                shift = jnp.where(below, edge_blocks, 0)
                a_index = jnp.where(cell // width == wanted, col // 128 + shift, -1)
                hots.append(one_hot(fine_edge == col % 128, 1.0))
                mask = coarse_edge == a_index
                for part, value in zip(parts, three_parts(wear)):
                    part.append(one_hot(mask, value))
            add(edge_ref, parts, jnp.concatenate(hots, axis=1))
            return carry

        lax.fori_loop(0, (n_own + GROUP - 1) // GROUP, own_group, 0)
        lax.fori_loop(0, (n_side + GROUP - 1) // GROUP, side_group, 0)
        for j in range(8):
            out_ref[8 : 8 + rows, j * block : (j + 1) * block] = acc_ref[
                j * rows : (j + 1) * rows, :
            ]
        for j in range(edge_blocks):
            out_ref[7:8, j * 128 : (j + 1) * 128] = edge_ref[j : j + 1, :]
            out_ref[8 + rows : 9 + rows, j * 128 : (j + 1) * 128] = edge_ref[
                edge_blocks + j : edge_blocks + j + 1, :
            ]


def paint(position, owner, counts, wear, lists, table, rows, width, shard_tiles):
    ntile, slots = lists.shape
    whole = lambda shape: pl.BlockSpec(shape, lambda i, *_: (0,) * len(shape))
    return pl.pallas_call(
        functools.partial(paint_kernel, shard_tiles),
        name="paint_band",
        grid_spec=pltpu.PrefetchScalarGridSpec(
            num_scalar_prefetch=3,
            grid=(1,),
            in_specs=[whole(wear.shape), whole(lists.shape), whole(table.shape)],
            out_specs=whole((rows + 16, width)),
            scratch_shapes=[
                pltpu.SMEM((ntile + 1,), jnp.int32),
                pltpu.SMEM((ntile + 1,), jnp.int32),
                pltpu.VMEM((rows * 8, width // 8), jnp.float32),
                pltpu.VMEM((2 * width // 128, 128), jnp.float32),
            ],
        ),
        out_shape=jax.ShapeDtypeStruct((rows + 16, width), jnp.float32),
        compiler_params=pltpu.CompilerParams(vmem_limit_bytes=VMEM_LIMIT),
    )(position, owner, counts, wear, lists, table)


def relax_tile(load, beside, has_high, has_low):
    centers = {}

    def neighbours(c):
        here = load(c, 0)
        centers[c] = here
        width = here.shape[1]
        lane = lax.broadcasted_iota(jnp.int32, here.shape, 1)
        yield load(c, 1)
        yield load(c, -1)
        yield from beside(c, here)
        yield jnp.where(lane == width - 1, 0.0, pltpu.roll(here, width - 1, 1))
        yield jnp.where(lane == 0, 0.0, pltpu.roll(here, 1, 1))

    around = list(neighbours(3))
    weights = [centers[3] + s for s in around]
    weights[0] = weights[0] * has_high
    weights[1] = weights[1] * has_low
    total = weights[0]
    for w in weights[1:]:
        total = total + w
    sums = []
    for c in range(3):
        acc = None
        for w, f in zip(weights, neighbours(c)):
            acc = w * f if acc is None else acc + w * f
        sums.append(acc)
    return sums, total, centers


def relax_outside(out, near, s_near, far, inside, surface, at, layer):
    def load(c, side):
        here = s_near[0] if c == 3 else near[c]
        if c == 0:
            here = here + jnp.where(layer == 0, surface[at : at + 1, :], 0.0)
        return here if side == 0 else pltpu.roll(here, 7 if side == 1 else 1, 0)

    sums, total, _ = relax_tile(load, lambda c, here: (far[c], inside[c]), 1.0, 1.0)
    inverse = 1.0 / total
    between = jnp.logical_and(layer > 0, layer < out.shape[1] - 1)
    kept = jnp.logical_and(between, s_near[0] > 0.0)
    for c in range(3):
        out[c] = jnp.where(kept, sums[c] * inverse, 0.0)


def layer_kernel(first_sweep, *refs):
    where_ref, f_in, s_in, before, after, s_before, s_after = refs[:7]
    rest = list(refs[7:-2])
    f_kept, s_kept = refs[-2:]
    surface = rest.pop(0) if first_sweep else None
    extra = rest[:4] + rest[6:]
    out, totals = rest[4:6] if first_sweep else rest
    step = pl.program_id(0)
    layer = step - 1
    last = pl.num_programs(0) - 2
    slot = step % 2
    ntiles = f_in.shape[2] // 8
    mid, s_mid = f_kept.at[1 - slot], s_kept.at[1 - slot]
    f_refs = {-1: f_kept.at[slot], 0: mid, 1: f_in.at[:, 0]}
    s_refs = {-1: s_kept.at[slot], 0: s_mid, 1: s_in.at[0]}
    outermost = jnp.logical_or(layer == 0, layer == last)
    row = lax.broadcasted_iota(jnp.int32, (8, 1), 0)

    @pl.when(step == 0)
    def _():
        f_kept[1] = f_in[:, 0]
        s_kept[1] = s_in[0]
        if first_sweep:
            far_before, far_after, own_first, own_last, out_before, out_after = extra
            relax_outside(out_before, before, s_before, far_before, own_first, surface, 7, row)
            relax_outside(out_after, after, s_after, far_after, own_last, surface,
                          8 + 8 * ntiles, row)

    has_low = jnp.where(layer == 0, 0.0, 1.0)
    has_high = jnp.where(layer == last, 0.0, 1.0)
    scales = {0: jnp.where(layer == 0, 1.0, 0.0), -1: jnp.where(layer == 1, 1.0, 0.0)}
    pinned = jnp.logical_and(layer == 0, where_ref[1] == 1)

    @pl.when(layer >= 0)
    def _():
        for t in range(ntiles):
            at = slice(8 * t, 8 * t + 8)

            def load(c, side):
                if c == 3:
                    return s_refs[side][at, :]
                value = f_refs[side][c, at, :]
                if first_sweep and c == 0 and side <= 0:
                    value = value + scales[side] * surface[8 * t + 8 : 8 * t + 16, :]
                return value

            def beside(inside, row, f_edge, s_edge):
                def get(c):
                    if c == 3:
                        if inside:
                            return s_mid[row : row + 1, :]
                        return s_edge[0, pl.ds(layer, 1), :]
                    value = mid[c, row : row + 1, :] if inside else f_edge[c, pl.ds(layer, 1), :]
                    if first_sweep and c == 0:
                        value = value + scales[0] * surface[row + 8 : row + 9, :]
                    return value
                return get

            above = beside(t > 0, 8 * t - 1, before, s_before)
            below = beside(t < ntiles - 1, 8 * t + 8, after, s_after)

            def rolled(c, here):
                yield jnp.where(row == 7, below(c), pltpu.roll(here, 7, 0))
                yield jnp.where(row == 0, above(c), pltpu.roll(here, 1, 0))

            sums, total, centers = relax_tile(load, rolled, has_high, has_low)
            inverse = jnp.where(outermost, 1.0, 1.0 / total)
            outs = [part * inverse for part in sums]
            outs[0] = jnp.where(pinned, centers[0], outs[0])
            for c in range(3):
                out[c, 0, at, :] = outs[c]

            totals[0, at, :] = total

    f_kept[slot] = f_in[:, 0]
    s_kept[slot] = s_in[0]


def relax_layers(position, field, stiffness, before, after, s_before, s_after, surface,
                 own=()):
    _, layers, rows, width = field.shape
    first_sweep = surface is not None
    whole = lambda shape: pl.BlockSpec(shape, lambda i, *_: (0,) * len(shape))
    came = lambda k: jnp.minimum(k, layers - 1)
    swept = lambda k: jnp.maximum(k - 1, 0)
    f_spec = lambda at: pl.BlockSpec((3, 1, rows, width), lambda k, *_: (0, at(k), 0, 0))
    f_edge = whole((3, layers, width))
    s_edge = pl.BlockSpec((1, layers, width), lambda k, *_: (3, 0, 0))
    args = [field, stiffness, before, after, s_before, s_after]
    in_specs = [f_spec(came), pl.BlockSpec((1, rows, width), lambda k, *_: (came(k), 0, 0))]
    in_specs += [f_edge, f_edge, s_edge, s_edge]
    out_shape = [jax.ShapeDtypeStruct(field.shape, jnp.float32),
                 jax.ShapeDtypeStruct((2, rows, width), jnp.float32)]
    out_specs = [f_spec(swept),
                 pl.BlockSpec((1, rows, width), lambda k, *_: (jnp.minimum(swept(k), 1), 0, 0))]
    if first_sweep:
        args.append(surface)
        in_specs.append(whole(surface.shape))
        args += [before, after, *own]
        near = pl.BlockSpec((4, layers, width), lambda i, *_: (0, 0, 0))
        far = pl.BlockSpec((4, layers, width), lambda i, *_: (1, 0, 0))
        in_specs += [far, far, near, near]
        out_shape += [jax.ShapeDtypeStruct((3, layers, width), jnp.float32)] * 2
        out_specs += [f_edge] * 2
    return pl.pallas_call(
        functools.partial(layer_kernel, first_sweep),
        name="relax_layers_first" if first_sweep else "relax_layers_second",
        grid_spec=pltpu.PrefetchScalarGridSpec(
            num_scalar_prefetch=1, grid=(layers + 1,), in_specs=in_specs, out_specs=out_specs,
            scratch_shapes=[pltpu.VMEM((2, 3, rows, width), jnp.float32),
                            pltpu.VMEM((2, rows, width), jnp.float32)],
        ),
        out_shape=out_shape,
        compiler_params=pltpu.CompilerParams(vmem_limit_bytes=VMEM_LIMIT),
    )(position, *args)


def finish_first_kernel(where_ref, sums, s_here, totals, low, high, s_low, s_high,
                        out, send_first, send_last, first_row, last_row):
    ntiles = sums.shape[2] // 8
    pinned = where_ref[1] == 1

    def one(face, outer, s_outer, send):
        for t in range(ntiles):
            at = slice(8 * t, 8 * t + 8)
            weight = s_here[0, at, :] + s_outer[0, at, :]
            inverse = 1.0 / (totals[0, at, :] + weight)
            for c in range(3):
                so_far = sums[c, 0, at, :]
                value = (so_far + weight * outer[c, at, :]) * inverse
                if face == 0 and c == 0:
                    value = jnp.where(pinned, so_far, value)
                out[c, 0, at, :] = value
                send[c, at, :] = value
                k = 2 * c + face
                if t == 0:
                    first_row[k : k + 1, :] = value[0:1]
                if t == ntiles - 1:
                    last_row[k : k + 1, :] = value[7:8]

    step = pl.program_id(0)

    @pl.when(step == 0)
    def _():
        first_row[...] = jnp.zeros_like(first_row)
        last_row[...] = jnp.zeros_like(last_row)
        one(0, low, s_low, send_first)

    pl.when(step == 1)(lambda: one(1, high, s_high, send_last))


def finish_first(position, field, stiffness, totals, low, high):
    _, layers, rows, width = field.shape
    block = lambda shape, at: pl.BlockSpec(shape, lambda i, *_: at(i))
    layer = lambda i: i * (layers - 1)
    plane = block((3, rows, width), lambda i: (0, 0, 0))
    s_plane = block((1, rows, width), lambda i: (3, 0, 0))
    own = block((3, 1, rows, width), lambda i: (0, layer(i), 0, 0))
    edge = block((8, width), lambda i: (0, 0))
    face_shape = jax.ShapeDtypeStruct((3, rows, width), jnp.float32)
    edge_shape = jax.ShapeDtypeStruct((8, width), jnp.float32)
    return pl.pallas_call(
        finish_first_kernel,
        name="finish_first",
        grid_spec=pltpu.PrefetchScalarGridSpec(
            num_scalar_prefetch=1, grid=(2,),
            in_specs=[own, block((1, rows, width), lambda i: (layer(i), 0, 0)),
                      block((1, rows, width), lambda i: (i, 0, 0)),
                      plane, plane, s_plane, s_plane],
            out_specs=[own, plane, plane, edge, edge],
        ),
        out_shape=[jax.ShapeDtypeStruct(field.shape, jnp.float32),
                   face_shape, face_shape, edge_shape, edge_shape],
        input_output_aliases={1: 0},
        compiler_params=pltpu.CompilerParams(vmem_limit_bytes=VMEM_LIMIT),
    )(position, field, stiffness, totals, low, high, low, high)


def finish_second_kernel(where_ref, sums, s_here, totals, low, high, s_low, s_high,
                         before, after, s_before, s_after, out):
    ntiles = sums.shape[2] // 8
    pinned = where_ref[1] == 1
    row = lax.broadcasted_iota(jnp.int32, (8, 1), 0)

    def one(face, outer, s_outer):
        layer = face * (s_before.shape[1] - 1)
        for t in range(ntiles):
            at = slice(8 * t, 8 * t + 8)
            here = s_here[0, at, :]
            weight = here + s_outer[0, at, :]
            inverse = 1.0 / (totals[0, at, :] + weight)
            for c in range(3):
                so_far = sums[c, 0, at, :]
                value = so_far + weight * outer[c, at, :]
                k = 2 * c + face
                if t == 0:
                    side = here + s_before[0, layer : layer + 1, :]
                    value = value + jnp.where(row == 0, side * before[k : k + 1, :], 0.0)
                if t == ntiles - 1:
                    side = here + s_after[0, layer : layer + 1, :]
                    value = value + jnp.where(row == 7, side * after[k : k + 1, :], 0.0)
                value = value * inverse
                if face == 0 and c == 0:
                    value = jnp.where(pinned, so_far, value)
                out[c, 0, at, :] = value

    step = pl.program_id(0)
    pl.when(step == 0)(lambda: one(0, low, s_low))
    pl.when(step == 1)(lambda: one(1, high, s_high))


def finish_second(position, field, stiffness, totals, low, high, s_low, s_high,
                  before, after, s_before, s_after):
    _, layers, rows, width = field.shape
    block = lambda shape, at: pl.BlockSpec(shape, lambda i, *_: at(i))
    layer = lambda i: i * (layers - 1)
    plane = block((3, rows, width), lambda i: (0, 0, 0))
    s_plane = block((1, rows, width), lambda i: (3, 0, 0))
    own = block((3, 1, rows, width), lambda i: (0, layer(i), 0, 0))
    edge = block((8, width), lambda i: (0, 0))
    s_edge = block((1, layers, width), lambda i: (3, 0, 0))
    return pl.pallas_call(
        finish_second_kernel,
        name="finish_second",
        grid_spec=pltpu.PrefetchScalarGridSpec(
            num_scalar_prefetch=1, grid=(2,),
            in_specs=[own, block((1, rows, width), lambda i: (layer(i), 0, 0)),
                      block((1, rows, width), lambda i: (i, 0, 0)),
                      plane, plane, s_plane, s_plane, edge, edge, s_edge, s_edge],
            out_specs=own,
        ),
        out_shape=jax.ShapeDtypeStruct(field.shape, jnp.float32),
        input_output_aliases={1: 0},
        compiler_params=pltpu.CompilerParams(vmem_limit_bytes=VMEM_LIMIT),
    )(position, field, stiffness, totals, low, high, s_low, s_high,
      before, after, s_before, s_after)


def per_device(
    displacement,
    stiffness,
    node_list,
    active_count,
    wear_class,
    pressure,
    slip_speed,
    rate_table,
    tile_owner,
    node_cell,
):
    rows, width = displacement.shape[2:]
    position = jnp.stack(
        [lax.axis_index("tan"), (lax.axis_index("depth") == 0).astype(jnp.int32)]
    ).astype(jnp.int32)

    row_first, row_last = pack_rows(displacement, stiffness)
    wear = archard(wear_class, pressure, slip_speed, rate_table)
    other = swap_halves(wear)
    before, after = shift_both(row_last, row_first, "tan")
    face_first, face_last = pack_faces(displacement, stiffness, row_first)
    face_first, face_last, other, before, after = lax.optimization_barrier(
        (face_first, face_last, other, before, after)
    )
    low, high = shift_both(face_last, face_first, "depth")
    wear = gather_wear(wear, other)
    surface = paint(position, tile_owner, active_count, wear, node_list,
                    node_cell.reshape(-1, 128), rows, width, wear_class.shape[0])

    first, totals, before_2, after_2 = relax_layers(
        position, displacement, stiffness, before, after, before, after, surface,
        (row_first, row_last),
    )
    first, send_first, send_last, edge_first, edge_last = finish_first(
        position, first, stiffness, totals, low, high
    )
    low_2, high_2 = shift_both(send_last, send_first, "depth")
    edge_before, edge_after = shift_both(edge_last, edge_first, "tan")
    result, totals = relax_layers(
        position, first, stiffness, before_2, after_2, before, after, None
    )
    return finish_second(position, result, stiffness, totals, low_2, high_2, low, high,
                         edge_before, edge_after, before, after)


def solution(mesh):
    in_specs = (
        P(None, "depth", "tan", None),
        P("depth", "tan", None),
        P(),
        P(),
        P("tan", None),
        P("tan", None),
        P("tan", None),
        P(),
        P(),
        P(),
    )
    out_specs = P(None, "depth", "tan", None)
    return jax.shard_map(
        per_device, mesh=mesh, in_specs=in_specs, out_specs=out_specs, check_vma=False
    )
```

```python
import functools

import jax
import jax.numpy as jnp
from jax import lax
from jax.experimental import pallas as pl
from jax.experimental.pallas import tpu as pltpu
from jax.sharding import PartitionSpec as P

wear_step = 0.6
hardness = 4.0
GROUP = 8
VMEM_LIMIT = 48 * 1024 * 1024


def shift_both(last, first, axis):
    size = lax.axis_size(axis)
    up = [(i, i + 1) for i in range(size - 1)]
    down = [(j, i) for i, j in up]
    return lax.ppermute(last, axis, up), lax.ppermute(first, axis, down)


def wear_kernel(rates_ref, class_ref, contact_ref, sliding_ref, wear_ref):
    ids = class_ref[...]
    rate = jnp.zeros(ids.shape, jnp.float32)
    for k in range(rates_ref.shape[0]):
        rate = jnp.where(ids == k, rates_ref[k], rate)
    product = contact_ref[...] * sliding_ref[...]
    wear_ref[...] = wear_step * rate * product / (1.0 + product / hardness)


def archard(class_ids, contact, sliding, rates):
    near = pl.BlockSpec(memory_space=pltpu.VMEM)
    return pl.pallas_call(
        wear_kernel,
        name="archard",
        in_specs=[pl.BlockSpec(memory_space=pltpu.SMEM), near, near, near],
        out_specs=near,
        out_shape=jax.ShapeDtypeStruct(contact.shape, jnp.float32),
    )(rates, class_ids, contact, sliding)


def rows_kernel(f_top, s_top, f_bottom, s_bottom, first_ref, last_ref):
    for l in range(f_top.shape[1]):
        for k in range(2):
            first_ref[4 * k + 3, l : l + 1, :] = s_top[l, k : k + 1, :]
            last_ref[4 * k + 3, l : l + 1, :] = s_bottom[l, 7 - k : 8 - k, :]
            for c in range(3):
                first_ref[4 * k + c, l : l + 1, :] = f_top[c, l, k : k + 1, :]
                last_ref[4 * k + c, l : l + 1, :] = f_bottom[c, l, 7 - k : 8 - k, :]


def pack_rows(field, stiffness):
    _, layers, rows, width = field.shape
    bottom = rows // 8 - 1
    f_spec = lambda at: pl.BlockSpec((3, layers, 8, width), lambda i: (0, 0, at, 0))
    s_spec = lambda at: pl.BlockSpec((layers, 8, width), lambda i: (0, at, 0))
    out = jax.ShapeDtypeStruct((8, layers, width), jnp.float32)
    out_spec = pl.BlockSpec((8, layers, width), lambda i: (0, 0, 0))
    return pl.pallas_call(
        rows_kernel,
        name="pack_rows",
        grid=(1,),
        in_specs=[f_spec(0), s_spec(0), f_spec(bottom), s_spec(bottom)],
        out_specs=[out_spec, out_spec],
        out_shape=[out, out],
        compiler_params=pltpu.CompilerParams(vmem_limit_bytes=VMEM_LIMIT),
    )(field, stiffness, field, stiffness)


def faces_kernel(field_ref, stiff_ref, first_ref, last_ref):
    step = pl.program_id(0)

    def put(to):
        to[0:3] = field_ref[:, 0]
        to[3:4] = stiff_ref[...]

    pl.when(step == 0)(lambda: put(last_ref))
    pl.when(step == 1)(lambda: put(first_ref))


def pack_faces(field, stiffness):
    _, layers, rows, width = field.shape
    face = jax.ShapeDtypeStruct((4, rows, width), jnp.float32)
    layer = lambda i: (1 - i) * (layers - 1)
    whole = pl.BlockSpec((4, rows, width), lambda i: (0, 0, 0))
    return pl.pallas_call(
        faces_kernel,
        name="pack_faces",
        grid=(2,),
        in_specs=[
            pl.BlockSpec((3, 1, rows, width), lambda i: (0, layer(i), 0, 0)),
            pl.BlockSpec((1, rows, width), lambda i: (layer(i), 0, 0)),
        ],
        out_specs=[whole, whole],
        out_shape=[face, face],
        compiler_params=pltpu.CompilerParams(vmem_limit_bytes=VMEM_LIMIT),
    )(field, stiffness)


def gather_wear(wear):
    size = lax.axis_size("tan")
    groups = [[i for i in range(size) if (i // 2) % 2 == half] for half in range(2)]
    own = lax.all_gather(wear, "tan", axis=0, axis_index_groups=groups, tiled=True)
    return own, lax.ppermute(own, "tan", [(i, i ^ 2) for i in range(size)])


def three_parts(value):
    high = value.astype(jnp.bfloat16).astype(jnp.float32)
    rest = value - high
    middle = rest.astype(jnp.bfloat16).astype(jnp.float32)
    return high, middle, rest - middle


def paint_kernel(
    shard_tiles, half, where_ref, owner_ref, count_ref, wear_ref, list_ref, table_ref,
    *refs,
):
    out_ref, own_ref, side_ref, acc_ref, edge_ref = refs[-5:]
    ntile, slots = list_ref.shape
    rows_table = table_ref.shape[0] // ntile
    tile_len = rows_table * 128
    width = out_ref.shape[1]
    rows = out_ref.shape[0] - 16
    me = where_ref[0]
    on_top = where_ref[1]
    out_ref[...] = jnp.zeros_like(out_ref) if half == 0 else refs[0][...]

    @pl.when(on_top == 1)
    def _():
        acc_ref[...] = jnp.zeros_like(acc_ref)
        edge_ref[...] = jnp.zeros_like(edge_ref)

        def collect(i, carry):
            n_own, n_side = carry
            same = ((i // (2 * shard_tiles)) ^ (me // 2)) & 1
            offset = jnp.where(same == half, owner_ref[i] - me, 2)
            own_ref[n_own] = i
            side_ref[n_side] = i
            n_own = n_own + jnp.where(offset == 0, 1, 0)
            n_side = n_side + jnp.where(offset * offset == 1, 1, 0)
            return n_own, n_side

        n_own, n_side = lax.fori_loop(
            0, ntile, collect, (jnp.int32(0), jnp.int32(0)), unroll=8
        )

        lane = lax.broadcasted_iota(jnp.int32, (1, slots), 1)
        table_row = lax.broadcasted_iota(jnp.int32, (rows_table, slots), 0)
        block = width // 8
        fine = lax.broadcasted_iota(jnp.int32, (block, slots), 0)
        coarse = lax.broadcasted_iota(jnp.int32, (rows * 8, slots), 0)
        fine_edge = lax.broadcasted_iota(jnp.int32, (128, slots), 0)
        edge_blocks = width // 128
        coarse_edge = lax.broadcasted_iota(jnp.int32, (2 * edge_blocks, slots), 0)

        def entry(tiles_ref, position, total):
            i = tiles_ref[jnp.minimum(position, total - 1)]
            live = jnp.where(position < total, count_ref[i], 0)
            local = list_ref[pl.ds(i, 1), :] - i * tile_len
            table = table_ref[pl.ds(pl.multiple_of(i * rows_table, 8), rows_table), :]
            column = jnp.broadcast_to(local & 127, (rows_table, slots))
            picked = jnp.take_along_axis(table, column, axis=1)
            cell = jnp.sum(
                jnp.where(table_row == (local >> 7), picked, 0), axis=0, keepdims=True
            )
            shard = i // shard_tiles
            place = (shard // 4) * 2 + shard % 2
            at = place * shard_tiles + i % shard_tiles
            wear = jnp.where(lane < live, wear_ref[pl.ds(at, 1), :], 0.0)
            return i, cell, wear

        def one_hot(mask, value):
            return jnp.where(mask, value, 0.0).astype(jnp.bfloat16)

        def add(into_ref, parts, hot):
            total = into_ref[...]
            for part in parts:
                total = total + lax.dot_general(
                    jnp.concatenate(part, axis=1), hot, (((1,), (1,)), ((), ())),
                    preferred_element_type=jnp.float32,
                )
            into_ref[...] = total

        def own_group(g, carry):
            parts = ([], [], [])
            hots = []
            for j in range(GROUP):
                _, cell, wear = entry(own_ref, g * GROUP + j, n_own)
                col = cell % width
                a_index = (col // block) * rows + cell // width
                hots.append(one_hot(fine == col % block, 1.0))
                mask = coarse == a_index
                for part, value in zip(parts, three_parts(wear)):
                    part.append(one_hot(mask, value))
            add(acc_ref, parts, jnp.concatenate(hots, axis=1))
            return carry

        def side_group(g, carry):
            parts = ([], [], [])
            hots = []
            for j in range(GROUP):
                i, cell, wear = entry(side_ref, g * GROUP + j, n_side)
                below = owner_ref[i] > me
                col = cell % width
                wanted = jnp.where(below, 0, rows - 1)
                shift = jnp.where(below, edge_blocks, 0)
                a_index = jnp.where(cell // width == wanted, col // 128 + shift, -1)
                hots.append(one_hot(fine_edge == col % 128, 1.0))
                mask = coarse_edge == a_index
                for part, value in zip(parts, three_parts(wear)):
                    part.append(one_hot(mask, value))
            add(edge_ref, parts, jnp.concatenate(hots, axis=1))
            return carry

        lax.fori_loop(0, (n_own + GROUP - 1) // GROUP, own_group, 0)
        lax.fori_loop(0, (n_side + GROUP - 1) // GROUP, side_group, 0)
        for j in range(8):
            out_ref[8 : 8 + rows, j * block : (j + 1) * block] += acc_ref[
                j * rows : (j + 1) * rows, :
            ]
        for j in range(edge_blocks):
            out_ref[7:8, j * 128 : (j + 1) * 128] += edge_ref[j : j + 1, :]
            out_ref[8 + rows : 9 + rows, j * 128 : (j + 1) * 128] += edge_ref[
                edge_blocks + j : edge_blocks + j + 1, :
            ]


def paint(position, owner, counts, wear, lists, table, rows, width, shard_tiles, base=None):
    ntile, slots = lists.shape
    args = [wear, lists, table] + ([] if base is None else [base])
    whole = lambda shape: pl.BlockSpec(shape, lambda i, *_: (0,) * len(shape))
    return pl.pallas_call(
        functools.partial(paint_kernel, shard_tiles, 0 if base is None else 1),
        name="paint_band",
        grid_spec=pltpu.PrefetchScalarGridSpec(
            num_scalar_prefetch=3,
            grid=(1,),
            in_specs=[whole(a.shape) for a in args],
            out_specs=whole((rows + 16, width)),
            scratch_shapes=[
                pltpu.SMEM((ntile + 1,), jnp.int32),
                pltpu.SMEM((ntile + 1,), jnp.int32),
                pltpu.VMEM((rows * 8, width // 8), jnp.float32),
                pltpu.VMEM((2 * width // 128, 128), jnp.float32),
            ],
        ),
        out_shape=jax.ShapeDtypeStruct((rows + 16, width), jnp.float32),
        compiler_params=pltpu.CompilerParams(vmem_limit_bytes=VMEM_LIMIT),
    )(position, owner, counts, *args)


def relax_tile(load, beside, has_high, has_low):
    centers = {}

    def neighbours(c):
        here = load(c, 0)
        centers[c] = here
        width = here.shape[1]
        lane = lax.broadcasted_iota(jnp.int32, (here.shape[0], 128), 1)
        yield load(c, 1)
        yield load(c, -1)
        yield from beside(c, here)
        right = pltpu.roll(here, width - 1, 1)
        end = jnp.where(lane == 127, 0.0, right[:, width - 128 :])
        yield jnp.concatenate([right[:, : width - 128], end], axis=1)
        left = pltpu.roll(here, 1, 1)
        end = jnp.where(lane == 0, 0.0, left[:, :128])
        yield jnp.concatenate([end, left[:, 128:]], axis=1)

    around = list(neighbours(3))
    weights = [centers[3] + s for s in around]
    if has_high is not None:
        weights[0] = weights[0] * has_high
    if has_low is not None:
        weights[1] = weights[1] * has_low
    total = weights[0]
    for w in weights[1:]:
        total = total + w
    sums = []
    for c in range(3):
        acc = None
        for w, f in zip(weights, neighbours(c)):
            acc = w * f if acc is None else acc + w * f
        sums.append(acc)
    return sums, total, centers


def relax_outside(out, near, s_near, far, inside, surface, at, layer):
    def load(c, side):
        here = s_near[0] if c == 3 else near[c]
        if c == 0:
            here = here + jnp.where(layer == 0, surface[at : at + 1, :], 0.0)
        return here if side == 0 else pltpu.roll(here, 7 if side == 1 else 1, 0)

    sums, total, _ = relax_tile(load, lambda c, here: (far[c], inside[c]), None, None)
    inverse = 1.0 / total
    between = jnp.logical_and(layer > 0, layer < out.shape[1] - 1)
    kept = jnp.logical_and(between, s_near[0] > 0.0)
    for c in range(3):
        out[c] = jnp.where(kept, sums[c] * inverse, 0.0)


def layer_kernel(first_sweep, *refs):
    where_ref, f_in, s_in, before, after, s_before, s_after = refs[:7]
    rest = list(refs[7:-2])
    f_kept, s_kept = refs[-2:]
    surface = rest.pop(0) if first_sweep else None
    if first_sweep:
        face_first, face_last = rest[:2]
        out = rest[6]
        extra = rest[2:6] + rest[7:]
    else:
        out, totals = rest
    step = pl.program_id(0)
    layer = step - 1
    last = pl.num_programs(0) - 2
    slot = step % 2
    ntiles = f_in.shape[2] // 8
    mid, s_mid = f_kept.at[1 - slot], s_kept.at[1 - slot]
    f_refs = {-1: f_kept.at[slot], 0: mid, 1: f_in.at[:, 0]}
    s_refs = {-1: s_kept.at[slot], 0: s_mid, 1: s_in.at[0]}
    outermost = jnp.logical_or(layer == 0, layer == last)
    row = lax.broadcasted_iota(jnp.int32, (8, 1), 0)

    @pl.when(step == 0)
    def _():
        f_kept[1] = f_in[:, 0]
        s_kept[1] = s_in[0]
        if first_sweep:
            far_before, far_after, own_first, own_last, out_before, out_after = extra
            relax_outside(out_before, before, s_before, far_before, own_first, surface, 7, row)
            relax_outside(out_after, after, s_after, far_after, own_last, surface,
                          8 + 8 * ntiles, row)

    has_low = None if first_sweep else jnp.where(layer == 0, 0.0, 1.0)
    has_high = None if first_sweep else jnp.where(layer == last, 0.0, 1.0)
    scale = jnp.where(layer == 1, 1.0, 0.0)
    pinned = jnp.logical_and(layer == 0, where_ref[1] == 1)

    def sweep():
        for t in range(ntiles):
            at = slice(8 * t, 8 * t + 8)

            def load(c, side):
                if c == 3:
                    return s_refs[side][at, :]
                value = f_refs[side][c, at, :]
                if first_sweep and c == 0 and side < 0:
                    value = value + scale * surface[8 * t + 8 : 8 * t + 16, :]
                return value

            def beside(inside, row, f_edge, s_edge):
                def get(c):
                    if c == 3:
                        if inside:
                            return s_mid[row : row + 1, :]
                        return s_edge[0, pl.ds(layer, 1), :]
                    if inside:
                        return mid[c, row : row + 1, :]
                    return f_edge[c, pl.ds(layer, 1), :]
                return get

            above = beside(t > 0, 8 * t - 1, before, s_before)
            below = beside(t < ntiles - 1, 8 * t + 8, after, s_after)

            def rolled(c, here):
                yield jnp.where(row == 7, below(c), pltpu.roll(here, 7, 0))
                yield jnp.where(row == 0, above(c), pltpu.roll(here, 1, 0))

            sums, total, centers = relax_tile(load, rolled, has_high, has_low)
            inverse = 1.0 / total
            if not first_sweep:
                inverse = jnp.where(outermost, 1.0, inverse)
            outs = [part * inverse for part in sums]
            if not first_sweep:
                outs[0] = jnp.where(pinned, centers[0], outs[0])
                totals[0, at, :] = total
            for c in range(3):
                out[c, 0, at, :] = outs[c]

    if first_sweep:
        inner = jnp.logical_and(layer > 0, layer < last)
        pl.when(inner)(sweep)

        @pl.when(layer == last)
        def _():
            out[:, 0] = face_last[...]

        @pl.when(layer == 0)
        def _():
            out[1:3, 0] = face_first[1:3]
            held = mid[0] + surface[8 : 8 + 8 * ntiles, :]
            out[0, 0] = jnp.where(where_ref[1] == 1, held, face_first[0])
    else:
        pl.when(layer >= 0)(sweep)

    f_kept[slot] = f_in[:, 0]
    s_kept[slot] = s_in[0]


def relax_layers(position, field, stiffness, before, after, s_before, s_after, surface=None,
                 faces=(), own=()):
    _, layers, rows, width = field.shape
    first_sweep = surface is not None
    whole = lambda shape: pl.BlockSpec(shape, lambda i, *_: (0,) * len(shape))
    came = lambda k: jnp.minimum(k, layers - 1)
    swept = lambda k: jnp.maximum(k - 1, 0)
    f_spec = lambda at: pl.BlockSpec((3, 1, rows, width), lambda k, *_: (0, at(k), 0, 0))
    f_edge = whole((3, layers, width))
    s_edge = pl.BlockSpec((1, layers, width), lambda k, *_: (3, 0, 0))
    args = [field, stiffness, before, after, s_before, s_after]
    in_specs = [f_spec(came), pl.BlockSpec((1, rows, width), lambda k, *_: (came(k), 0, 0))]
    in_specs += [f_edge, f_edge, s_edge, s_edge]
    out_shape = [jax.ShapeDtypeStruct(field.shape, jnp.float32)]
    out_specs = [f_spec(swept)]
    if not first_sweep:
        out_shape.append(jax.ShapeDtypeStruct((2, rows, width), jnp.float32))
        out_specs.append(
            pl.BlockSpec((1, rows, width), lambda k, *_: (jnp.minimum(swept(k), 1), 0, 0)))
    else:
        args += [surface, *faces, before, after, *own]
        in_specs += [whole(surface.shape)] + [whole((3, rows, width))] * 2
        near = pl.BlockSpec((4, layers, width), lambda i, *_: (0, 0, 0))
        far = pl.BlockSpec((4, layers, width), lambda i, *_: (1, 0, 0))
        in_specs += [far, far, near, near]
        out_shape += [jax.ShapeDtypeStruct((3, layers, width), jnp.float32)] * 2
        out_specs += [f_edge] * 2
    return pl.pallas_call(
        functools.partial(layer_kernel, first_sweep),
        name="relax_layers_first" if first_sweep else "relax_layers_second",
        grid_spec=pltpu.PrefetchScalarGridSpec(
            num_scalar_prefetch=1, grid=(layers + 1,), in_specs=in_specs, out_specs=out_specs,
            scratch_shapes=[pltpu.VMEM((2, 3, rows, width), jnp.float32),
                            pltpu.VMEM((2, rows, width), jnp.float32)],
        ),
        out_shape=out_shape,
        compiler_params=pltpu.CompilerParams(vmem_limit_bytes=VMEM_LIMIT),
    )(position, *args)


def face_sums_kernel(here, inside, s_here, s_inside, sums, totals):
    ntiles = here.shape[2] // 8
    row = lax.broadcasted_iota(jnp.int32, (8, 1), 0)
    for t in range(ntiles):
        at = slice(8 * t, 8 * t + 8)

        def load(c, side):
            if side == 0:
                return s_here[0, at, :] if c == 3 else here[c, 0, at, :]
            return s_inside[0, at, :] if c == 3 else inside[c, 0, at, :]

        def beside(c, tile):
            def take(k, missing, own):
                if missing:
                    return -s_here[0, own : own + 1, :] if c == 3 else 0.0
                return s_here[0, k : k + 1, :] if c == 3 else here[c, 0, k : k + 1, :]

            below = take(8 * t + 8, t == ntiles - 1, 8 * t + 7)
            above = take(8 * t - 1, t == 0, 8 * t)
            yield jnp.where(row == 7, below, pltpu.roll(tile, 7, 0))
            yield jnp.where(row == 0, above, pltpu.roll(tile, 1, 0))

        parts, total, _ = relax_tile(load, beside, None, 0.0)
        for c in range(3):
            sums[c, 0, at, :] = parts[c]
        totals[0, at, :] = total


def face_sums(field, stiffness):
    _, layers, rows, width = field.shape
    outer = lambda i: i * (layers - 1)
    inner = lambda i: 1 + i * (layers - 3)
    f_spec = lambda at: pl.BlockSpec((3, 1, rows, width), lambda i: (0, at(i), 0, 0))
    s_spec = lambda at: pl.BlockSpec((1, rows, width), lambda i: (at(i), 0, 0))
    itself = lambda i: i
    return pl.pallas_call(
        face_sums_kernel,
        name="face_sums",
        grid=(2,),
        in_specs=[f_spec(outer), f_spec(inner), s_spec(outer), s_spec(inner)],
        out_specs=[f_spec(itself), s_spec(itself)],
        out_shape=[jax.ShapeDtypeStruct((3, 2, rows, width), jnp.float32),
                   jax.ShapeDtypeStruct((2, rows, width), jnp.float32)],
        compiler_params=pltpu.CompilerParams(vmem_limit_bytes=VMEM_LIMIT),
    )(field, field, stiffness, stiffness)


def finish_first_kernel(sums, s_here, totals, low, high, s_low, s_high, before, after,
                        s_before, s_after, send_first, send_last, first_row, last_row):
    ntiles = sums.shape[2] // 8
    row = lax.broadcasted_iota(jnp.int32, (8, 1), 0)

    def one(face, outer, s_outer, send):
        layer = face * (s_before.shape[1] - 1)
        for t in range(ntiles):
            at = slice(8 * t, 8 * t + 8)
            here = s_here[0, at, :]
            weight = here + s_outer[0, at, :]
            total = totals[0, at, :] + weight
            values = [sums[c, 0, at, :] + weight * outer[c, at, :] for c in range(3)]
            for wanted, k, f_edge, s_edge in ((0, 0, before, s_before),
                                              (ntiles - 1, 7, after, s_after)):
                if t == wanted:
                    side = jnp.where(row == k, here + s_edge[0, layer : layer + 1, :], 0.0)
                    total = total + side
                    for c in range(3):
                        values[c] = values[c] + side * f_edge[c, layer : layer + 1, :]
            inverse = 1.0 / total
            for c in range(3):
                value = values[c] * inverse
                send[c, at, :] = value
                k = 2 * c + face
                if t == 0:
                    first_row[k : k + 1, :] = value[0:1]
                if t == ntiles - 1:
                    last_row[k : k + 1, :] = value[7:8]

    step = pl.program_id(0)

    @pl.when(step == 0)
    def _():
        first_row[...] = jnp.zeros_like(first_row)
        last_row[...] = jnp.zeros_like(last_row)
        one(0, low, s_low, send_first)

    pl.when(step == 1)(lambda: one(1, high, s_high, send_last))


def finish_first(sums, stiffness, totals, low, high, before, after):
    layers = stiffness.shape[0]
    rows, width = sums.shape[2:]
    block = lambda shape, at: pl.BlockSpec(shape, lambda i: at(i))
    plane = block((3, rows, width), lambda i: (0, 0, 0))
    s_plane = block((1, rows, width), lambda i: (3, 0, 0))
    edge = block((8, width), lambda i: (0, 0))
    f_edge = block((3, layers, width), lambda i: (0, 0, 0))
    s_edge = block((1, layers, width), lambda i: (3, 0, 0))
    face_shape = jax.ShapeDtypeStruct((3, rows, width), jnp.float32)
    edge_shape = jax.ShapeDtypeStruct((8, width), jnp.float32)
    return pl.pallas_call(
        finish_first_kernel,
        name="finish_first",
        grid=(2,),
        in_specs=[block((3, 1, rows, width), lambda i: (0, i, 0, 0)),
                  block((1, rows, width), lambda i: (i * (layers - 1), 0, 0)),
                  block((1, rows, width), lambda i: (i, 0, 0)),
                  plane, plane, s_plane, s_plane, f_edge, f_edge, s_edge, s_edge],
        out_specs=[plane, plane, edge, edge],
        out_shape=[face_shape, face_shape, edge_shape, edge_shape],
        compiler_params=pltpu.CompilerParams(vmem_limit_bytes=VMEM_LIMIT),
    )(sums, stiffness, totals, low, high, low, high, before, after, before, after)


def finish_second_kernel(where_ref, sums, s_here, totals, low, high, s_low, s_high,
                         before, after, s_before, s_after, out):
    ntiles = sums.shape[2] // 8
    pinned = where_ref[1] == 1
    row = lax.broadcasted_iota(jnp.int32, (8, 1), 0)

    def one(face, outer, s_outer):
        layer = face * (s_before.shape[1] - 1)
        for t in range(ntiles):
            at = slice(8 * t, 8 * t + 8)
            here = s_here[0, at, :]
            weight = here + s_outer[0, at, :]
            inverse = 1.0 / (totals[0, at, :] + weight)
            for c in range(3):
                so_far = sums[c, 0, at, :]
                value = so_far + weight * outer[c, at, :]
                k = 2 * c + face
                if t == 0:
                    side = here + s_before[0, layer : layer + 1, :]
                    value = value + jnp.where(row == 0, side * before[k : k + 1, :], 0.0)
                if t == ntiles - 1:
                    side = here + s_after[0, layer : layer + 1, :]
                    value = value + jnp.where(row == 7, side * after[k : k + 1, :], 0.0)
                value = value * inverse
                if face == 0 and c == 0:
                    value = jnp.where(pinned, so_far, value)
                out[c, 0, at, :] = value

    step = pl.program_id(0)
    pl.when(step == 0)(lambda: one(0, low, s_low))
    pl.when(step == 1)(lambda: one(1, high, s_high))


def finish_second(position, field, stiffness, totals, low, high, s_low, s_high,
                  before, after, s_before, s_after):
    _, layers, rows, width = field.shape
    block = lambda shape, at: pl.BlockSpec(shape, lambda i, *_: at(i))
    layer = lambda i: i * (layers - 1)
    plane = block((3, rows, width), lambda i: (0, 0, 0))
    s_plane = block((1, rows, width), lambda i: (3, 0, 0))
    own = block((3, 1, rows, width), lambda i: (0, layer(i), 0, 0))
    edge = block((8, width), lambda i: (0, 0))
    s_edge = block((1, layers, width), lambda i: (3, 0, 0))
    return pl.pallas_call(
        finish_second_kernel,
        name="finish_second",
        grid_spec=pltpu.PrefetchScalarGridSpec(
            num_scalar_prefetch=1, grid=(2,),
            in_specs=[own, block((1, rows, width), lambda i: (layer(i), 0, 0)),
                      block((1, rows, width), lambda i: (i, 0, 0)),
                      plane, plane, s_plane, s_plane, edge, edge, s_edge, s_edge],
            out_specs=own,
        ),
        out_shape=jax.ShapeDtypeStruct(field.shape, jnp.float32),
        input_output_aliases={1: 0},
        compiler_params=pltpu.CompilerParams(vmem_limit_bytes=VMEM_LIMIT),
    )(position, field, stiffness, totals, low, high, s_low, s_high,
      before, after, s_before, s_after)


def per_device(
    displacement,
    stiffness,
    node_list,
    active_count,
    wear_class,
    pressure,
    slip_speed,
    rate_table,
    tile_owner,
    node_cell,
):
    rows, width = displacement.shape[2:]
    position = jnp.stack(
        [lax.axis_index("tan"), (lax.axis_index("depth") == 0).astype(jnp.int32)]
    ).astype(jnp.int32)

    face_first, face_last = pack_faces(displacement, stiffness)
    low, high = shift_both(face_last, face_first, "depth")
    row_first, row_last = pack_rows(displacement, stiffness)
    before, after = shift_both(row_last, row_first, "tan")
    wear = archard(wear_class, pressure, slip_speed, rate_table)
    own, other = gather_wear(wear)
    table = node_cell.reshape(-1, 128)
    tiles_here = wear_class.shape[0]
    surface = paint(position, tile_owner, active_count, own, node_list, table,
                    rows, width, tiles_here)
    sums, totals = face_sums(displacement, stiffness)
    low, high, other, surface = lax.optimization_barrier((low, high, other, surface))
    face_first, face_last, edge_first, edge_last = finish_first(
        sums, stiffness, totals, low, high, before, after
    )
    low_2, high_2 = shift_both(face_last, face_first, "depth")
    surface = paint(position, tile_owner, active_count, other, node_list, table,
                    rows, width, tiles_here, surface)
    first, before_2, after_2 = relax_layers(
        position, displacement, stiffness, before, after, before, after, surface,
        (face_first, face_last), (row_first, row_last),
    )
    edge_first, edge_last, before_2 = lax.optimization_barrier(
        (edge_first, edge_last, before_2)
    )
    edge_before, edge_after = shift_both(edge_last, edge_first, "tan")
    result, totals = relax_layers(
        position, first, stiffness, before_2, after_2, before, after
    )
    return finish_second(position, result, stiffness, totals, low_2, high_2, low, high,
                         edge_before, edge_after, before, after)


def solution(mesh):
    in_specs = (
        P(None, "depth", "tan", None),
        P("depth", "tan", None),
        P(),
        P(),
        P("tan", None),
        P("tan", None),
        P("tan", None),
        P(),
        P(),
        P(),
    )
    out_specs = P(None, "depth", "tan", None)
    return jax.shard_map(
        per_device, mesh=mesh, in_specs=in_specs, out_specs=out_specs, check_vma=False
    )
```

```python
import functools

import jax
import jax.numpy as jnp
from jax import lax
from jax.experimental import pallas as pl
from jax.experimental.pallas import tpu as pltpu
from jax.sharding import PartitionSpec as P

wear_step = 0.6
hardness = 4.0
GROUP = 8
VMEM_LIMIT = 48 * 1024 * 1024


def shift_both(last, first, axis):
    size = lax.axis_size(axis)
    up = [(i, i + 1) for i in range(size - 1)]
    down = [(j, i) for i, j in up]
    return lax.ppermute(last, axis, up), lax.ppermute(first, axis, down)


def wear_kernel(rates_ref, class_ref, contact_ref, sliding_ref, wear_ref):
    ids = class_ref[...]
    rate = jnp.zeros(ids.shape, jnp.float32)
    for k in range(rates_ref.shape[0]):
        rate = jnp.where(ids == k, rates_ref[k], rate)
    product = contact_ref[...] * sliding_ref[...]
    wear_ref[...] = wear_step * rate * product / (1.0 + product / hardness)


def archard(class_ids, contact, sliding, rates):
    near = pl.BlockSpec(memory_space=pltpu.VMEM)
    return pl.pallas_call(
        wear_kernel,
        name="archard",
        in_specs=[pl.BlockSpec(memory_space=pltpu.SMEM), near, near, near],
        out_specs=near,
        out_shape=jax.ShapeDtypeStruct(contact.shape, jnp.float32),
    )(rates, class_ids, contact, sliding)


def rows_kernel(f_top, s_top, f_bottom, s_bottom, first_ref, last_ref):
    for l in range(f_top.shape[1]):
        for k in range(2):
            first_ref[4 * k + 3, l : l + 1, :] = s_top[l, k : k + 1, :]
            last_ref[4 * k + 3, l : l + 1, :] = s_bottom[l, 7 - k : 8 - k, :]
            for c in range(3):
                first_ref[4 * k + c, l : l + 1, :] = f_top[c, l, k : k + 1, :]
                last_ref[4 * k + c, l : l + 1, :] = f_bottom[c, l, 7 - k : 8 - k, :]


def pack_rows(field, stiffness):
    _, layers, rows, width = field.shape
    bottom = rows // 8 - 1
    f_spec = lambda at: pl.BlockSpec((3, layers, 8, width), lambda i: (0, 0, at, 0))
    s_spec = lambda at: pl.BlockSpec((layers, 8, width), lambda i: (0, at, 0))
    out = jax.ShapeDtypeStruct((8, layers, width), jnp.float32)
    out_spec = pl.BlockSpec((8, layers, width), lambda i: (0, 0, 0))
    return pl.pallas_call(
        rows_kernel,
        name="pack_rows",
        grid=(1,),
        in_specs=[f_spec(0), s_spec(0), f_spec(bottom), s_spec(bottom)],
        out_specs=[out_spec, out_spec],
        out_shape=[out, out],
        compiler_params=pltpu.CompilerParams(vmem_limit_bytes=VMEM_LIMIT),
    )(field, stiffness, field, stiffness)


def faces_kernel(field_ref, stiff_ref, first_ref, last_ref):
    step = pl.program_id(0)

    def put(to):
        to[0:3] = field_ref[:, 0]
        to[3:4] = stiff_ref[...]

    pl.when(step == 0)(lambda: put(last_ref))
    pl.when(step == 1)(lambda: put(first_ref))


def pack_faces(field, stiffness):
    _, layers, rows, width = field.shape
    face = jax.ShapeDtypeStruct((4, rows, width), jnp.float32)
    layer = lambda i: (1 - i) * (layers - 1)
    whole = pl.BlockSpec((4, rows, width), lambda i: (0, 0, 0))
    return pl.pallas_call(
        faces_kernel,
        name="pack_faces",
        grid=(2,),
        in_specs=[
            pl.BlockSpec((3, 1, rows, width), lambda i: (0, layer(i), 0, 0)),
            pl.BlockSpec((1, rows, width), lambda i: (layer(i), 0, 0)),
        ],
        out_specs=[whole, whole],
        out_shape=[face, face],
        compiler_params=pltpu.CompilerParams(vmem_limit_bytes=VMEM_LIMIT),
    )(field, stiffness)


def gather_wear(wear):
    size = lax.axis_size("tan")
    groups = [[i for i in range(size) if (i // 2) % 2 == half] for half in range(2)]
    own = lax.all_gather(wear, "tan", axis=0, axis_index_groups=groups, tiled=True)
    return own, lax.ppermute(own, "tan", [(i, i ^ 2) for i in range(size)])


def three_parts(value):
    high = value.astype(jnp.bfloat16).astype(jnp.float32)
    rest = value - high
    middle = rest.astype(jnp.bfloat16).astype(jnp.float32)
    return high, middle, rest - middle


def collect_kernel(shard_tiles, where_ref, owner_ref, out_ref):
    ntile = owner_ref.shape[0]
    room = out_ref.shape[0] // 4
    me = where_ref[0]
    for k in range(4):
        out_ref[(k + 1) * room - 1] = 0

    @pl.when(where_ref[1] == 1)
    def _():
        def step(i, ends):
            offset = owner_ref[i] - me
            other = ((i // (2 * shard_tiles)) ^ (me // 2)) & 1
            kind = jnp.where(offset == 0, 0, jnp.where(offset * offset == 1, 1, 8)) + 2 * other
            for end in ends:
                out_ref[end] = i
            return tuple(end + jnp.where(kind == k, 1, 0) for k, end in enumerate(ends))

        starts = tuple(jnp.int32(k * room) for k in range(4))
        ends = lax.fori_loop(0, ntile, step, starts, unroll=8)
        for k in range(4):
            out_ref[(k + 1) * room - 1] = ends[k] - k * room


def collect(position, owner, shard_tiles):
    return pl.pallas_call(
        functools.partial(collect_kernel, shard_tiles),
        name="collect_tiles",
        in_specs=[pl.BlockSpec(memory_space=pltpu.SMEM)] * 2,
        out_specs=pl.BlockSpec(memory_space=pltpu.SMEM),
        out_shape=jax.ShapeDtypeStruct((4 * (owner.shape[0] + 128),), jnp.int32),
    )(position, owner)


def paint_kernel(
    shard_tiles, half, where_ref, owner_ref, count_ref, tiles_ref, wear_ref, list_ref,
    table_ref,
    *refs,
):
    out_ref, acc_ref, edge_ref = refs[-3:]
    room = tiles_ref.shape[0] // 4
    ntile, slots = list_ref.shape
    rows_table = table_ref.shape[0] // ntile
    tile_len = rows_table * 128
    width = out_ref.shape[1]
    rows = out_ref.shape[0] - 16
    me = where_ref[0]
    on_top = where_ref[1]
    out_ref[...] = jnp.zeros_like(out_ref) if half == 0 else refs[0][...]

    @pl.when(on_top == 1)
    def _():
        acc_ref[...] = jnp.zeros_like(acc_ref)
        edge_ref[...] = jnp.zeros_like(edge_ref)

        n_own = tiles_ref[(2 * half + 1) * room - 1]
        n_side = tiles_ref[(2 * half + 2) * room - 1]
        lane = lax.broadcasted_iota(jnp.int32, (1, slots), 1)
        table_row = lax.broadcasted_iota(jnp.int32, (rows_table, slots), 0)
        block = width // 8
        fine = lax.broadcasted_iota(jnp.int32, (block, slots), 0)
        coarse = lax.broadcasted_iota(jnp.int32, (rows * 8, slots), 0)
        fine_edge = lax.broadcasted_iota(jnp.int32, (128, slots), 0)
        edge_blocks = width // 128
        coarse_edge = lax.broadcasted_iota(jnp.int32, (2 * edge_blocks, slots), 0)

        def entry(kind, position, total):
            i = tiles_ref[(2 * half + kind) * room + jnp.minimum(position, total - 1)]
            live = jnp.where(position < total, count_ref[i], 0)
            local = list_ref[pl.ds(i, 1), :] - i * tile_len
            table = table_ref[pl.ds(pl.multiple_of(i * rows_table, 8), rows_table), :]
            column = jnp.broadcast_to(local & 127, (rows_table, slots))
            picked = jnp.take_along_axis(table, column, axis=1)
            cell = jnp.sum(
                jnp.where(table_row == (local >> 7), picked, 0), axis=0, keepdims=True
            )
            shard = i // shard_tiles
            place = (shard // 4) * 2 + shard % 2
            at = place * shard_tiles + i % shard_tiles
            wear = jnp.where(lane < live, wear_ref[pl.ds(at, 1), :], 0.0)
            return i, cell, wear

        def one_hot(mask, value):
            return jnp.where(mask, value, 0.0).astype(jnp.bfloat16)

        def add(into_ref, parts, hot):
            total = into_ref[...]
            for part in parts:
                total = total + lax.dot_general(
                    jnp.concatenate(part, axis=1), hot, (((1,), (1,)), ((), ())),
                    preferred_element_type=jnp.float32,
                )
            into_ref[...] = total

        def own_group(g, carry):
            parts = ([], [], [])
            hots = []
            for j in range(GROUP):
                _, cell, wear = entry(0, g * GROUP + j, n_own)
                col = cell % width
                a_index = (col // block) * rows + cell // width
                hots.append(one_hot(fine == col % block, 1.0))
                mask = coarse == a_index
                for part, value in zip(parts, three_parts(wear)):
                    part.append(one_hot(mask, value))
            add(acc_ref, parts, jnp.concatenate(hots, axis=1))
            return carry

        def side_group(g, carry):
            parts = ([], [], [])
            hots = []
            for j in range(GROUP):
                i, cell, wear = entry(1, g * GROUP + j, n_side)
                below = owner_ref[i] > me
                col = cell % width
                wanted = jnp.where(below, 0, rows - 1)
                shift = jnp.where(below, edge_blocks, 0)
                a_index = jnp.where(cell // width == wanted, col // 128 + shift, -1)
                hots.append(one_hot(fine_edge == col % 128, 1.0))
                mask = coarse_edge == a_index
                for part, value in zip(parts, three_parts(wear)):
                    part.append(one_hot(mask, value))
            add(edge_ref, parts, jnp.concatenate(hots, axis=1))
            return carry

        lax.fori_loop(0, (n_own + GROUP - 1) // GROUP, own_group, 0)
        lax.fori_loop(0, (n_side + GROUP - 1) // GROUP, side_group, 0)
        for j in range(8):
            out_ref[8 : 8 + rows, j * block : (j + 1) * block] += acc_ref[
                j * rows : (j + 1) * rows, :
            ]
        for j in range(edge_blocks):
            out_ref[7:8, j * 128 : (j + 1) * 128] += edge_ref[j : j + 1, :]
            out_ref[8 + rows : 9 + rows, j * 128 : (j + 1) * 128] += edge_ref[
                edge_blocks + j : edge_blocks + j + 1, :
            ]


def paint(position, owner, counts, tiles, wear, lists, table, rows, width, shard_tiles, base=None):
    args = [wear, lists, table] + ([] if base is None else [base])
    whole = lambda shape: pl.BlockSpec(shape, lambda i, *_: (0,) * len(shape))
    return pl.pallas_call(
        functools.partial(paint_kernel, shard_tiles, 0 if base is None else 1),
        name="paint_band",
        grid_spec=pltpu.PrefetchScalarGridSpec(
            num_scalar_prefetch=4,
            grid=(1,),
            in_specs=[whole(a.shape) for a in args],
            out_specs=whole((rows + 16, width)),
            scratch_shapes=[
                pltpu.VMEM((rows * 8, width // 8), jnp.float32),
                pltpu.VMEM((2 * width // 128, 128), jnp.float32),
            ],
        ),
        out_shape=jax.ShapeDtypeStruct((rows + 16, width), jnp.float32),
        compiler_params=pltpu.CompilerParams(vmem_limit_bytes=VMEM_LIMIT),
    )(position, owner, counts, tiles, *args)


def relax_tile(load, beside, has_high, has_low):
    centers = {}

    def neighbours(c):
        here = load(c, 0)
        centers[c] = here
        width = here.shape[1]
        lane = lax.broadcasted_iota(jnp.int32, (here.shape[0], 128), 1)
        yield load(c, 1)
        yield load(c, -1)
        yield from beside(c, here)
        right = pltpu.roll(here, width - 1, 1)
        end = jnp.where(lane == 127, 0.0, right[:, width - 128 :])
        yield jnp.concatenate([right[:, : width - 128], end], axis=1)
        left = pltpu.roll(here, 1, 1)
        end = jnp.where(lane == 0, 0.0, left[:, :128])
        yield jnp.concatenate([end, left[:, 128:]], axis=1)

    around = list(neighbours(3))
    weights = [centers[3] + s for s in around]
    if has_high is not None:
        weights[0] = weights[0] * has_high
    if has_low is not None:
        weights[1] = weights[1] * has_low
    total = weights[0]
    for w in weights[1:]:
        total = total + w
    sums = []
    for c in range(3):
        acc = None
        for w, f in zip(weights, neighbours(c)):
            acc = w * f if acc is None else acc + w * f
        sums.append(acc)
    return sums, total, centers


def relax_outside(out, near, s_near, far, inside, surface, at, layer):
    def load(c, side):
        here = s_near[0] if c == 3 else near[c]
        if c == 0:
            here = here + jnp.where(layer == 0, surface[at : at + 1, :], 0.0)
        return here if side == 0 else pltpu.roll(here, 7 if side == 1 else 1, 0)

    sums, total, _ = relax_tile(load, lambda c, here: (far[c], inside[c]), None, None)
    inverse = 1.0 / total
    between = jnp.logical_and(layer > 0, layer < out.shape[1] - 1)
    kept = jnp.logical_and(between, s_near[0] > 0.0)
    for c in range(3):
        out[c] = jnp.where(kept, sums[c] * inverse, 0.0)


def layer_kernel(first_sweep, *refs):
    where_ref, f_in, s_in, before, after, s_before, s_after = refs[:7]
    rest = list(refs[7:-2])
    f_kept, s_kept = refs[-2:]
    surface = rest.pop(0) if first_sweep else None
    if first_sweep:
        face_first, face_last = rest[:2]
        out = rest[6]
        extra = rest[2:6] + rest[7:]
    else:
        out, totals = rest
    step = pl.program_id(0)
    layer = step - 1
    last = pl.num_programs(0) - 2
    slot = step % 2
    ntiles = f_in.shape[2] // 8
    mid, s_mid = f_kept.at[1 - slot], s_kept.at[1 - slot]
    f_refs = {-1: f_kept.at[slot], 0: mid, 1: f_in.at[:, 0]}
    s_refs = {-1: s_kept.at[slot], 0: s_mid, 1: s_in.at[0]}
    outermost = jnp.logical_or(layer == 0, layer == last)
    row = lax.broadcasted_iota(jnp.int32, (8, 1), 0)

    @pl.when(step == 0)
    def _():
        f_kept[1] = f_in[:, 0]
        s_kept[1] = s_in[0]
        if first_sweep:
            far_before, far_after, own_first, own_last, out_before, out_after = extra
            relax_outside(out_before, before, s_before, far_before, own_first, surface, 7, row)
            relax_outside(out_after, after, s_after, far_after, own_last, surface,
                          8 + 8 * ntiles, row)

    has_low = None if first_sweep else jnp.where(layer == 0, 0.0, 1.0)
    has_high = None if first_sweep else jnp.where(layer == last, 0.0, 1.0)
    scale = jnp.where(layer == 1, 1.0, 0.0)
    pinned = jnp.logical_and(layer == 0, where_ref[1] == 1)

    def sweep():
        for t in range(ntiles):
            at = slice(8 * t, 8 * t + 8)

            def load(c, side):
                if c == 3:
                    return s_refs[side][at, :]
                value = f_refs[side][c, at, :]
                if first_sweep and c == 0 and side < 0:
                    value = value + scale * surface[8 * t + 8 : 8 * t + 16, :]
                return value

            def beside(inside, row, f_edge, s_edge):
                def get(c):
                    if c == 3:
                        if inside:
                            return s_mid[row : row + 1, :]
                        return s_edge[0, pl.ds(layer, 1), :]
                    if inside:
                        return mid[c, row : row + 1, :]
                    return f_edge[c, pl.ds(layer, 1), :]
                return get

            above = beside(t > 0, 8 * t - 1, before, s_before)
            below = beside(t < ntiles - 1, 8 * t + 8, after, s_after)

            def rolled(c, here):
                yield jnp.where(row == 7, below(c), pltpu.roll(here, 7, 0))
                yield jnp.where(row == 0, above(c), pltpu.roll(here, 1, 0))

            sums, total, centers = relax_tile(load, rolled, has_high, has_low)
            inverse = 1.0 / total
            if not first_sweep:
                inverse = jnp.where(outermost, 1.0, inverse)
            outs = [part * inverse for part in sums]
            if not first_sweep:
                outs[0] = jnp.where(pinned, centers[0], outs[0])
                totals[0, at, :] = total
            for c in range(3):
                out[c, 0, at, :] = outs[c]

    if first_sweep:
        inner = jnp.logical_and(layer > 0, layer < last)
        pl.when(inner)(sweep)

        @pl.when(layer == last)
        def _():
            out[:, 0] = face_last[...]

        @pl.when(layer == 0)
        def _():
            out[1:3, 0] = face_first[1:3]
            held = mid[0] + surface[8 : 8 + 8 * ntiles, :]
            out[0, 0] = jnp.where(where_ref[1] == 1, held, face_first[0])
    else:
        pl.when(layer >= 0)(sweep)

    f_kept[slot] = f_in[:, 0]
    s_kept[slot] = s_in[0]


def relax_layers(position, field, stiffness, before, after, s_before, s_after, surface=None,
                 faces=(), own=()):
    _, layers, rows, width = field.shape
    first_sweep = surface is not None
    whole = lambda shape: pl.BlockSpec(shape, lambda i, *_: (0,) * len(shape))
    came = lambda k: jnp.minimum(k, layers - 1)
    swept = lambda k: jnp.maximum(k - 1, 0)
    f_spec = lambda at: pl.BlockSpec((3, 1, rows, width), lambda k, *_: (0, at(k), 0, 0))
    f_edge = whole((3, layers, width))
    s_edge = pl.BlockSpec((1, layers, width), lambda k, *_: (3, 0, 0))
    args = [field, stiffness, before, after, s_before, s_after]
    in_specs = [f_spec(came), pl.BlockSpec((1, rows, width), lambda k, *_: (came(k), 0, 0))]
    in_specs += [f_edge, f_edge, s_edge, s_edge]
    out_shape = [jax.ShapeDtypeStruct(field.shape, jnp.float32)]
    out_specs = [f_spec(swept)]
    if not first_sweep:
        out_shape.append(jax.ShapeDtypeStruct((2, rows, width), jnp.float32))
        out_specs.append(
            pl.BlockSpec((1, rows, width), lambda k, *_: (jnp.minimum(swept(k), 1), 0, 0)))
    else:
        args += [surface, *faces, before, after, *own]
        in_specs += [whole(surface.shape)] + [whole((3, rows, width))] * 2
        near = pl.BlockSpec((4, layers, width), lambda i, *_: (0, 0, 0))
        far = pl.BlockSpec((4, layers, width), lambda i, *_: (1, 0, 0))
        in_specs += [far, far, near, near]
        out_shape += [jax.ShapeDtypeStruct((3, layers, width), jnp.float32)] * 2
        out_specs += [f_edge] * 2
    return pl.pallas_call(
        functools.partial(layer_kernel, first_sweep),
        name="relax_layers_first" if first_sweep else "relax_layers_second",
        grid_spec=pltpu.PrefetchScalarGridSpec(
            num_scalar_prefetch=1, grid=(layers + 1,), in_specs=in_specs, out_specs=out_specs,
            scratch_shapes=[pltpu.VMEM((2, 3, rows, width), jnp.float32),
                            pltpu.VMEM((2, rows, width), jnp.float32)],
        ),
        out_shape=out_shape,
        compiler_params=pltpu.CompilerParams(vmem_limit_bytes=VMEM_LIMIT),
    )(position, *args)


def face_sums_kernel(here, inside, s_here, s_inside, sums, totals):
    ntiles = here.shape[2] // 8
    row = lax.broadcasted_iota(jnp.int32, (8, 1), 0)
    for t in range(ntiles):
        at = slice(8 * t, 8 * t + 8)

        def load(c, side):
            if side == 0:
                return s_here[0, at, :] if c == 3 else here[c, 0, at, :]
            return s_inside[0, at, :] if c == 3 else inside[c, 0, at, :]

        def beside(c, tile):
            def take(k, missing, own):
                if missing:
                    return -s_here[0, own : own + 1, :] if c == 3 else 0.0
                return s_here[0, k : k + 1, :] if c == 3 else here[c, 0, k : k + 1, :]

            below = take(8 * t + 8, t == ntiles - 1, 8 * t + 7)
            above = take(8 * t - 1, t == 0, 8 * t)
            yield jnp.where(row == 7, below, pltpu.roll(tile, 7, 0))
            yield jnp.where(row == 0, above, pltpu.roll(tile, 1, 0))

        parts, total, _ = relax_tile(load, beside, None, 0.0)
        for c in range(3):
            sums[c, 0, at, :] = parts[c]
        totals[0, at, :] = total


def face_sums(field, stiffness):
    _, layers, rows, width = field.shape
    outer = lambda i: i * (layers - 1)
    inner = lambda i: 1 + i * (layers - 3)
    f_spec = lambda at: pl.BlockSpec((3, 1, rows, width), lambda i: (0, at(i), 0, 0))
    s_spec = lambda at: pl.BlockSpec((1, rows, width), lambda i: (at(i), 0, 0))
    itself = lambda i: i
    return pl.pallas_call(
        face_sums_kernel,
        name="face_sums",
        grid=(2,),
        in_specs=[f_spec(outer), f_spec(inner), s_spec(outer), s_spec(inner)],
        out_specs=[f_spec(itself), s_spec(itself)],
        out_shape=[jax.ShapeDtypeStruct((3, 2, rows, width), jnp.float32),
                   jax.ShapeDtypeStruct((2, rows, width), jnp.float32)],
        compiler_params=pltpu.CompilerParams(vmem_limit_bytes=VMEM_LIMIT),
    )(field, field, stiffness, stiffness)


def finish_first_kernel(sums, s_here, totals, low, high, s_low, s_high, before, after,
                        s_before, s_after, send_first, send_last, first_row, last_row):
    ntiles = sums.shape[2] // 8
    row = lax.broadcasted_iota(jnp.int32, (8, 1), 0)

    def one(face, outer, s_outer, send):
        layer = face * (s_before.shape[1] - 1)
        for t in range(ntiles):
            at = slice(8 * t, 8 * t + 8)
            here = s_here[0, at, :]
            weight = here + s_outer[0, at, :]
            total = totals[0, at, :] + weight
            values = [sums[c, 0, at, :] + weight * outer[c, at, :] for c in range(3)]
            for wanted, k, f_edge, s_edge in ((0, 0, before, s_before),
                                              (ntiles - 1, 7, after, s_after)):
                if t == wanted:
                    side = jnp.where(row == k, here + s_edge[0, layer : layer + 1, :], 0.0)
                    total = total + side
                    for c in range(3):
                        values[c] = values[c] + side * f_edge[c, layer : layer + 1, :]
            inverse = 1.0 / total
            for c in range(3):
                value = values[c] * inverse
                send[c, at, :] = value
                k = 2 * c + face
                if t == 0:
                    first_row[k : k + 1, :] = value[0:1]
                if t == ntiles - 1:
                    last_row[k : k + 1, :] = value[7:8]

    step = pl.program_id(0)

    @pl.when(step == 0)
    def _():
        first_row[...] = jnp.zeros_like(first_row)
        last_row[...] = jnp.zeros_like(last_row)
        one(0, low, s_low, send_first)

    pl.when(step == 1)(lambda: one(1, high, s_high, send_last))


def finish_first(sums, stiffness, totals, low, high, before, after):
    layers = stiffness.shape[0]
    rows, width = sums.shape[2:]
    block = lambda shape, at: pl.BlockSpec(shape, lambda i: at(i))
    plane = block((3, rows, width), lambda i: (0, 0, 0))
    s_plane = block((1, rows, width), lambda i: (3, 0, 0))
    edge = block((8, width), lambda i: (0, 0))
    f_edge = block((3, layers, width), lambda i: (0, 0, 0))
    s_edge = block((1, layers, width), lambda i: (3, 0, 0))
    face_shape = jax.ShapeDtypeStruct((3, rows, width), jnp.float32)
    edge_shape = jax.ShapeDtypeStruct((8, width), jnp.float32)
    return pl.pallas_call(
        finish_first_kernel,
        name="finish_first",
        grid=(2,),
        in_specs=[block((3, 1, rows, width), lambda i: (0, i, 0, 0)),
                  block((1, rows, width), lambda i: (i * (layers - 1), 0, 0)),
                  block((1, rows, width), lambda i: (i, 0, 0)),
                  plane, plane, s_plane, s_plane, f_edge, f_edge, s_edge, s_edge],
        out_specs=[plane, plane, edge, edge],
        out_shape=[face_shape, face_shape, edge_shape, edge_shape],
        compiler_params=pltpu.CompilerParams(vmem_limit_bytes=VMEM_LIMIT),
    )(sums, stiffness, totals, low, high, low, high, before, after, before, after)


def finish_second_kernel(where_ref, sums, s_here, totals, low, high, s_low, s_high,
                         before, after, s_before, s_after, out):
    ntiles = sums.shape[2] // 8
    pinned = where_ref[1] == 1
    row = lax.broadcasted_iota(jnp.int32, (8, 1), 0)

    def one(face, outer, s_outer):
        layer = face * (s_before.shape[1] - 1)
        for t in range(ntiles):
            at = slice(8 * t, 8 * t + 8)
            here = s_here[0, at, :]
            weight = here + s_outer[0, at, :]
            inverse = 1.0 / (totals[0, at, :] + weight)
            for c in range(3):
                so_far = sums[c, 0, at, :]
                value = so_far + weight * outer[c, at, :]
                k = 2 * c + face
                if t == 0:
                    side = here + s_before[0, layer : layer + 1, :]
                    value = value + jnp.where(row == 0, side * before[k : k + 1, :], 0.0)
                if t == ntiles - 1:
                    side = here + s_after[0, layer : layer + 1, :]
                    value = value + jnp.where(row == 7, side * after[k : k + 1, :], 0.0)
                value = value * inverse
                if face == 0 and c == 0:
                    value = jnp.where(pinned, so_far, value)
                out[c, 0, at, :] = value

    step = pl.program_id(0)
    pl.when(step == 0)(lambda: one(0, low, s_low))
    pl.when(step == 1)(lambda: one(1, high, s_high))


def finish_second(position, field, stiffness, totals, low, high, s_low, s_high,
                  before, after, s_before, s_after):
    _, layers, rows, width = field.shape
    block = lambda shape, at: pl.BlockSpec(shape, lambda i, *_: at(i))
    layer = lambda i: i * (layers - 1)
    plane = block((3, rows, width), lambda i: (0, 0, 0))
    s_plane = block((1, rows, width), lambda i: (3, 0, 0))
    own = block((3, 1, rows, width), lambda i: (0, layer(i), 0, 0))
    edge = block((8, width), lambda i: (0, 0))
    s_edge = block((1, layers, width), lambda i: (3, 0, 0))
    return pl.pallas_call(
        finish_second_kernel,
        name="finish_second",
        grid_spec=pltpu.PrefetchScalarGridSpec(
            num_scalar_prefetch=1, grid=(2,),
            in_specs=[own, block((1, rows, width), lambda i: (layer(i), 0, 0)),
                      block((1, rows, width), lambda i: (i, 0, 0)),
                      plane, plane, s_plane, s_plane, edge, edge, s_edge, s_edge],
            out_specs=own,
        ),
        out_shape=jax.ShapeDtypeStruct(field.shape, jnp.float32),
        input_output_aliases={1: 0},
        compiler_params=pltpu.CompilerParams(vmem_limit_bytes=VMEM_LIMIT),
    )(position, field, stiffness, totals, low, high, s_low, s_high,
      before, after, s_before, s_after)


def per_device(
    displacement,
    stiffness,
    node_list,
    active_count,
    wear_class,
    pressure,
    slip_speed,
    rate_table,
    tile_owner,
    node_cell,
):
    rows, width = displacement.shape[2:]
    position = jnp.stack(
        [lax.axis_index("tan"), (lax.axis_index("depth") == 0).astype(jnp.int32)]
    ).astype(jnp.int32)

    face_first, face_last = pack_faces(displacement, stiffness)
    low, high = shift_both(face_last, face_first, "depth")
    row_first, row_last = pack_rows(displacement, stiffness)
    before, after = shift_both(row_last, row_first, "tan")
    wear = archard(wear_class, pressure, slip_speed, rate_table)
    own, other = gather_wear(wear)
    table = node_cell.reshape(-1, 128)
    tiles_here = wear_class.shape[0]
    tiles = collect(position, tile_owner, tiles_here)
    surface = paint(position, tile_owner, active_count, tiles, own, node_list, table,
                    rows, width, tiles_here)
    sums, totals = face_sums(displacement, stiffness)
    low, high, other, surface = lax.optimization_barrier((low, high, other, surface))
    face_first, face_last, edge_first, edge_last = finish_first(
        sums, stiffness, totals, low, high, before, after
    )
    low_2, high_2 = shift_both(face_last, face_first, "depth")
    surface = paint(position, tile_owner, active_count, tiles, other, node_list, table,
                    rows, width, tiles_here, surface)
    first, before_2, after_2 = relax_layers(
        position, displacement, stiffness, before, after, before, after, surface,
        (face_first, face_last), (row_first, row_last),
    )
    edge_first, edge_last, before_2 = lax.optimization_barrier(
        (edge_first, edge_last, before_2)
    )
    edge_before, edge_after = shift_both(edge_last, edge_first, "tan")
    result, totals = relax_layers(
        position, first, stiffness, before_2, after_2, before, after
    )
    return finish_second(position, result, stiffness, totals, low_2, high_2, low, high,
                         edge_before, edge_after, before, after)


def solution(mesh):
    in_specs = (
        P(None, "depth", "tan", None),
        P("depth", "tan", None),
        P(),
        P(),
        P("tan", None),
        P("tan", None),
        P("tan", None),
        P(),
        P(),
        P(),
    )
    out_specs = P(None, "depth", "tan", None)
    return jax.shard_map(
        per_device, mesh=mesh, in_specs=in_specs, out_specs=out_specs, check_vma=False
    )
```

```python
import functools

import jax
import jax.numpy as jnp
from jax import lax
from jax.experimental import pallas as pl
from jax.experimental.pallas import tpu as pltpu
from jax.sharding import PartitionSpec as P

wear_step = 0.6
hardness = 4.0
GROUP = 8
VMEM_LIMIT = 48 * 1024 * 1024


def shift_both(last, first, axis):
    size = lax.axis_size(axis)
    up = [(i, i + 1) for i in range(size - 1)]
    down = [(j, i) for i, j in up]
    return lax.ppermute(last, axis, up), lax.ppermute(first, axis, down)


def wear_kernel(rates_ref, class_ref, contact_ref, sliding_ref, wear_ref):
    ids = class_ref[...]
    rate = jnp.zeros(ids.shape, jnp.float32)
    for k in range(rates_ref.shape[0]):
        rate = jnp.where(ids == k, rates_ref[k], rate)
    product = contact_ref[...] * sliding_ref[...]
    wear_ref[...] = wear_step * rate * product / (1.0 + product / hardness)


def archard(class_ids, contact, sliding, rates):
    near = pl.BlockSpec(memory_space=pltpu.VMEM)
    return pl.pallas_call(
        wear_kernel,
        name="archard",
        in_specs=[pl.BlockSpec(memory_space=pltpu.SMEM), near, near, near],
        out_specs=near,
        out_shape=jax.ShapeDtypeStruct(contact.shape, jnp.float32),
    )(rates, class_ids, contact, sliding)


def rows_kernel(f_top, s_top, f_bottom, s_bottom, first_ref, last_ref):
    for l in range(f_top.shape[1]):
        for k in range(2):
            first_ref[4 * k + 3, l : l + 1, :] = s_top[l, k : k + 1, :]
            last_ref[4 * k + 3, l : l + 1, :] = s_bottom[l, 7 - k : 8 - k, :]
            for c in range(3):
                first_ref[4 * k + c, l : l + 1, :] = f_top[c, l, k : k + 1, :]
                last_ref[4 * k + c, l : l + 1, :] = f_bottom[c, l, 7 - k : 8 - k, :]


def pack_rows(field, stiffness):
    _, layers, rows, width = field.shape
    bottom = rows // 8 - 1
    f_spec = lambda at: pl.BlockSpec((3, layers, 8, width), lambda i: (0, 0, at, 0))
    s_spec = lambda at: pl.BlockSpec((layers, 8, width), lambda i: (0, at, 0))
    out = jax.ShapeDtypeStruct((8, layers, width), jnp.float32)
    out_spec = pl.BlockSpec((8, layers, width), lambda i: (0, 0, 0))
    return pl.pallas_call(
        rows_kernel,
        name="pack_rows",
        grid=(1,),
        in_specs=[f_spec(0), s_spec(0), f_spec(bottom), s_spec(bottom)],
        out_specs=[out_spec, out_spec],
        out_shape=[out, out],
        compiler_params=pltpu.CompilerParams(vmem_limit_bytes=VMEM_LIMIT),
    )(field, stiffness, field, stiffness)


def faces_kernel(field_ref, stiff_ref, first_ref, last_ref, sems):
    layers = field_ref.shape[1]
    copies = []
    for k, (to, layer) in enumerate(((last_ref, layers - 1), (first_ref, 0))):
        copies.append(pltpu.make_async_copy(
            field_ref.at[:, layer], to.at[pl.ds(0, 3)], sems.at[2 * k]))
        copies.append(pltpu.make_async_copy(
            stiff_ref.at[pl.ds(layer, 1)], to.at[pl.ds(3, 1)], sems.at[2 * k + 1]))
    for copy in copies:
        copy.start()
    for copy in copies:
        copy.wait()


def pack_faces(field, stiffness):
    _, _, rows, width = field.shape
    face = jax.ShapeDtypeStruct((4, rows, width), jnp.float32)
    far = pl.BlockSpec(memory_space=pltpu.HBM)
    near = pl.BlockSpec(memory_space=pltpu.VMEM)
    return pl.pallas_call(
        faces_kernel,
        name="pack_faces",
        in_specs=[far, far],
        out_specs=[near, near],
        out_shape=[face, face],
        scratch_shapes=[pltpu.SemaphoreType.DMA((4,))],
        compiler_params=pltpu.CompilerParams(vmem_limit_bytes=VMEM_LIMIT),
    )(field, stiffness)


def gather_wear(wear):
    size = lax.axis_size("tan")
    groups = [[i for i in range(size) if (i // 2) % 2 == half] for half in range(2)]
    own = lax.all_gather(wear, "tan", axis=0, axis_index_groups=groups, tiled=True)
    return own, lax.ppermute(own, "tan", [(i, i ^ 2) for i in range(size)])


def three_parts(value):
    high = value.astype(jnp.bfloat16).astype(jnp.float32)
    rest = value - high
    middle = rest.astype(jnp.bfloat16).astype(jnp.float32)
    return high, middle, rest - middle


def collect_kernel(shard_tiles, where_ref, owner_ref, out_ref):
    ntile = owner_ref.shape[0]
    room = out_ref.shape[0] // 4
    me = where_ref[0]
    for k in range(4):
        out_ref[(k + 1) * room - 1] = 0

    @pl.when(where_ref[1] == 1)
    def _():
        def step(i, ends):
            offset = owner_ref[i] - me
            other = ((i // (2 * shard_tiles)) ^ (me // 2)) & 1
            kind = jnp.where(offset == 0, 0, jnp.where(offset * offset == 1, 1, 8)) + 2 * other
            for end in ends:
                out_ref[end] = i
            return tuple(end + jnp.where(kind == k, 1, 0) for k, end in enumerate(ends))

        starts = tuple(jnp.int32(k * room) for k in range(4))
        ends = lax.fori_loop(0, ntile, step, starts, unroll=8)
        for k in range(4):
            out_ref[(k + 1) * room - 1] = ends[k] - k * room


def collect(position, owner, shard_tiles):
    return pl.pallas_call(
        functools.partial(collect_kernel, shard_tiles),
        name="collect_tiles",
        in_specs=[pl.BlockSpec(memory_space=pltpu.SMEM)] * 2,
        out_specs=pl.BlockSpec(memory_space=pltpu.SMEM),
        out_shape=jax.ShapeDtypeStruct((4 * (owner.shape[0] + 128),), jnp.int32),
    )(position, owner)


def paint_kernel(
    shard_tiles, half, where_ref, owner_ref, count_ref, tiles_ref, wear_ref, list_ref,
    table_ref,
    *refs,
):
    out_ref, acc_ref, edge_ref = refs[-3:]
    room = tiles_ref.shape[0] // 4
    ntile, slots = list_ref.shape
    rows_table = table_ref.shape[0] // ntile
    tile_len = rows_table * 128
    width = out_ref.shape[1]
    rows = out_ref.shape[0] - 16
    me = where_ref[0]
    on_top = where_ref[1]
    out_ref[...] = jnp.zeros_like(out_ref) if half == 0 else refs[0][...]

    @pl.when(on_top == 1)
    def _():
        acc_ref[...] = jnp.zeros_like(acc_ref)
        edge_ref[...] = jnp.zeros_like(edge_ref)

        n_own = tiles_ref[(2 * half + 1) * room - 1]
        n_side = tiles_ref[(2 * half + 2) * room - 1]
        lane = lax.broadcasted_iota(jnp.int32, (1, slots), 1)
        table_row = lax.broadcasted_iota(jnp.int32, (rows_table, slots), 0)
        block = width // 8
        fine = lax.broadcasted_iota(jnp.int32, (block, slots), 0)
        coarse = lax.broadcasted_iota(jnp.int32, (rows * 8, slots), 0)
        fine_edge = lax.broadcasted_iota(jnp.int32, (128, slots), 0)
        edge_blocks = width // 128
        coarse_edge = lax.broadcasted_iota(jnp.int32, (2 * edge_blocks, slots), 0)

        def entry(kind, position, total):
            i = tiles_ref[(2 * half + kind) * room + jnp.minimum(position, total - 1)]
            live = jnp.where(position < total, count_ref[i], 0)
            local = list_ref[pl.ds(i, 1), :] - i * tile_len
            table = table_ref[pl.ds(pl.multiple_of(i * rows_table, 8), rows_table), :]
            column = jnp.broadcast_to(local & 127, (rows_table, slots))
            picked = jnp.take_along_axis(table, column, axis=1)
            cell = jnp.sum(
                jnp.where(table_row == (local >> 7), picked, 0), axis=0, keepdims=True
            )
            shard = i // shard_tiles
            place = (shard // 4) * 2 + shard % 2
            at = place * shard_tiles + i % shard_tiles
            wear = jnp.where(lane < live, wear_ref[pl.ds(at, 1), :], 0.0)
            return i, cell, wear

        def one_hot(mask, value):
            return jnp.where(mask, value, 0.0).astype(jnp.bfloat16)

        def add(into_ref, parts, hot):
            total = into_ref[...]
            for part in parts:
                total = total + lax.dot_general(
                    jnp.concatenate(part, axis=1), hot, (((1,), (1,)), ((), ())),
                    preferred_element_type=jnp.float32,
                )
            into_ref[...] = total

        def own_group(g, carry):
            parts = ([], [], [])
            hots = []
            for j in range(GROUP):
                _, cell, wear = entry(0, g * GROUP + j, n_own)
                col = cell % width
                a_index = (col // block) * rows + cell // width
                hots.append(one_hot(fine == col % block, 1.0))
                mask = coarse == a_index
                for part, value in zip(parts, three_parts(wear)):
                    part.append(one_hot(mask, value))
            add(acc_ref, parts, jnp.concatenate(hots, axis=1))
            return carry

        def side_group(g, carry):
            parts = ([], [], [])
            hots = []
            for j in range(GROUP):
                i, cell, wear = entry(1, g * GROUP + j, n_side)
                below = owner_ref[i] > me
                col = cell % width
                wanted = jnp.where(below, 0, rows - 1)
                shift = jnp.where(below, edge_blocks, 0)
                a_index = jnp.where(cell // width == wanted, col // 128 + shift, -1)
                hots.append(one_hot(fine_edge == col % 128, 1.0))
                mask = coarse_edge == a_index
                for part, value in zip(parts, three_parts(wear)):
                    part.append(one_hot(mask, value))
            add(edge_ref, parts, jnp.concatenate(hots, axis=1))
            return carry

        lax.fori_loop(0, (n_own + GROUP - 1) // GROUP, own_group, 0)
        lax.fori_loop(0, (n_side + GROUP - 1) // GROUP, side_group, 0)
        for j in range(8):
            out_ref[8 : 8 + rows, j * block : (j + 1) * block] += acc_ref[
                j * rows : (j + 1) * rows, :
            ]
        for j in range(edge_blocks):
            out_ref[7:8, j * 128 : (j + 1) * 128] += edge_ref[j : j + 1, :]
            out_ref[8 + rows : 9 + rows, j * 128 : (j + 1) * 128] += edge_ref[
                edge_blocks + j : edge_blocks + j + 1, :
            ]


def paint(position, owner, counts, tiles, wear, lists, table, rows, width, shard_tiles, base=None):
    args = [wear, lists, table] + ([] if base is None else [base])
    return pl.pallas_call(
        functools.partial(paint_kernel, shard_tiles, 0 if base is None else 1),
        name="paint_band",
        in_specs=[pl.BlockSpec(memory_space=pltpu.SMEM)] * 4
        + [pl.BlockSpec(memory_space=pltpu.VMEM)] * len(args),
        out_specs=pl.BlockSpec(memory_space=pltpu.VMEM),
        scratch_shapes=[
            pltpu.VMEM((rows * 8, width // 8), jnp.float32),
            pltpu.VMEM((2 * width // 128, 128), jnp.float32),
        ],
        out_shape=jax.ShapeDtypeStruct((rows + 16, width), jnp.float32),
        compiler_params=pltpu.CompilerParams(vmem_limit_bytes=VMEM_LIMIT),
    )(position, owner, counts, tiles, *args)


def relax_tile(load, beside, has_high, has_low):
    centers = {}

    def neighbours(c):
        here = load(c, 0)
        centers[c] = here
        width = here.shape[1]
        lane = lax.broadcasted_iota(jnp.int32, (here.shape[0], 128), 1)
        yield load(c, 1)
        yield load(c, -1)
        yield from beside(c, here)
        right = pltpu.roll(here, width - 1, 1)
        end = jnp.where(lane == 127, 0.0, right[:, width - 128 :])
        yield jnp.concatenate([right[:, : width - 128], end], axis=1)
        left = pltpu.roll(here, 1, 1)
        end = jnp.where(lane == 0, 0.0, left[:, :128])
        yield jnp.concatenate([end, left[:, 128:]], axis=1)

    around = list(neighbours(3))
    weights = [centers[3] + s for s in around]
    if has_high is not None:
        weights[0] = weights[0] * has_high
    if has_low is not None:
        weights[1] = weights[1] * has_low
    total = weights[0]
    for w in weights[1:]:
        total = total + w
    sums = []
    for c in range(3):
        acc = None
        for w, f in zip(weights, neighbours(c)):
            acc = w * f if acc is None else acc + w * f
        sums.append(acc)
    return sums, total, centers


def relax_outside(out, near, s_near, far, inside, surface, at, layer):
    def load(c, side):
        here = s_near[0] if c == 3 else near[c]
        if c == 0:
            here = here + jnp.where(layer == 0, surface[at : at + 1, :], 0.0)
        return here if side == 0 else pltpu.roll(here, 7 if side == 1 else 1, 0)

    sums, total, _ = relax_tile(load, lambda c, here: (far[c], inside[c]), None, None)
    inverse = 1.0 / total
    between = jnp.logical_and(layer > 0, layer < out.shape[1] - 1)
    kept = jnp.logical_and(between, s_near[0] > 0.0)
    for c in range(3):
        out[c] = jnp.where(kept, sums[c] * inverse, 0.0)


def layer_kernel(first_sweep, *refs):
    where_ref, f_in, s_in, before, after, s_before, s_after = refs[:7]
    rest = list(refs[7:-2])
    f_kept, s_kept = refs[-2:]
    surface = rest.pop(0) if first_sweep else None
    if first_sweep:
        face_first, face_last = rest[:2]
        out = rest[6]
        extra = rest[2:6] + rest[7:]
    else:
        out, totals = rest
    step = pl.program_id(0)
    layer = step - 1
    last = pl.num_programs(0) - 2
    slot = step % 2
    ntiles = f_in.shape[2] // 8
    mid, s_mid = f_kept.at[1 - slot], s_kept.at[1 - slot]
    f_refs = {-1: f_kept.at[slot], 0: mid, 1: f_in.at[:, 0]}
    s_refs = {-1: s_kept.at[slot], 0: s_mid, 1: s_in.at[0]}
    outermost = jnp.logical_or(layer == 0, layer == last)
    row = lax.broadcasted_iota(jnp.int32, (8, 1), 0)

    @pl.when(step == 0)
    def _():
        f_kept[1] = f_in[:, 0]
        s_kept[1] = s_in[0]
        if first_sweep:
            far_before, far_after, own_first, own_last, out_before, out_after = extra
            relax_outside(out_before, before, s_before, far_before, own_first, surface, 7, row)
            relax_outside(out_after, after, s_after, far_after, own_last, surface,
                          8 + 8 * ntiles, row)

    has_low = None if first_sweep else jnp.where(layer == 0, 0.0, 1.0)
    has_high = None if first_sweep else jnp.where(layer == last, 0.0, 1.0)
    scale = jnp.where(layer == 1, 1.0, 0.0)
    pinned = jnp.logical_and(layer == 0, where_ref[1] == 1)

    def sweep():
        for t in range(ntiles):
            at = slice(8 * t, 8 * t + 8)

            def load(c, side):
                if c == 3:
                    return s_refs[side][at, :]
                value = f_refs[side][c, at, :]
                if first_sweep and c == 0 and side < 0:
                    value = value + scale * surface[8 * t + 8 : 8 * t + 16, :]
                return value

            def beside(inside, row, f_edge, s_edge):
                def get(c):
                    if c == 3:
                        if inside:
                            return s_mid[row : row + 1, :]
                        return s_edge[0, pl.ds(layer, 1), :]
                    if inside:
                        return mid[c, row : row + 1, :]
                    return f_edge[c, pl.ds(layer, 1), :]
                return get

            above = beside(t > 0, 8 * t - 1, before, s_before)
            below = beside(t < ntiles - 1, 8 * t + 8, after, s_after)

            def rolled(c, here):
                yield jnp.where(row == 7, below(c), pltpu.roll(here, 7, 0))
                yield jnp.where(row == 0, above(c), pltpu.roll(here, 1, 0))

            sums, total, centers = relax_tile(load, rolled, has_high, has_low)
            inverse = 1.0 / total
            if not first_sweep:
                inverse = jnp.where(outermost, 1.0, inverse)
            outs = [part * inverse for part in sums]
            if not first_sweep:
                outs[0] = jnp.where(pinned, centers[0], outs[0])
                totals[0, at, :] = total
            for c in range(3):
                out[c, 0, at, :] = outs[c]

    if first_sweep:
        inner = jnp.logical_and(layer > 0, layer < last)
        pl.when(inner)(sweep)

        @pl.when(layer == last)
        def _():
            out[:, 0] = face_last[...]

        @pl.when(layer == 0)
        def _():
            out[1:3, 0] = face_first[1:3]
            held = mid[0] + surface[8 : 8 + 8 * ntiles, :]
            out[0, 0] = jnp.where(where_ref[1] == 1, held, face_first[0])
    else:
        pl.when(layer >= 0)(sweep)

    f_kept[slot] = f_in[:, 0]
    s_kept[slot] = s_in[0]


def relax_layers(position, field, stiffness, before, after, s_before, s_after, surface=None,
                 faces=(), own=()):
    _, layers, rows, width = field.shape
    first_sweep = surface is not None
    whole = lambda shape: pl.BlockSpec(shape, lambda i, *_: (0,) * len(shape))
    came = lambda k: jnp.minimum(k, layers - 1)
    swept = lambda k: jnp.maximum(k - 1, 0)
    f_spec = lambda at: pl.BlockSpec((3, 1, rows, width), lambda k, *_: (0, at(k), 0, 0))
    f_edge = whole((3, layers, width))
    s_edge = pl.BlockSpec((1, layers, width), lambda k, *_: (3, 0, 0))
    args = [field, stiffness, before, after, s_before, s_after]
    in_specs = [f_spec(came), pl.BlockSpec((1, rows, width), lambda k, *_: (came(k), 0, 0))]
    in_specs += [f_edge, f_edge, s_edge, s_edge]
    out_shape = [jax.ShapeDtypeStruct(field.shape, jnp.float32)]
    out_specs = [f_spec(swept)]
    if not first_sweep:
        out_shape.append(jax.ShapeDtypeStruct((2, rows, width), jnp.float32))
        out_specs.append(
            pl.BlockSpec((1, rows, width), lambda k, *_: (jnp.minimum(swept(k), 1), 0, 0)))
    else:
        args += [surface, *faces, before, after, *own]
        in_specs += [whole(surface.shape)] + [whole((3, rows, width))] * 2
        near = pl.BlockSpec((4, layers, width), lambda i, *_: (0, 0, 0))
        far = pl.BlockSpec((4, layers, width), lambda i, *_: (1, 0, 0))
        in_specs += [far, far, near, near]
        out_shape += [jax.ShapeDtypeStruct((3, layers, width), jnp.float32)] * 2
        out_specs += [f_edge] * 2
    return pl.pallas_call(
        functools.partial(layer_kernel, first_sweep),
        name="relax_layers_first" if first_sweep else "relax_layers_second",
        grid_spec=pltpu.PrefetchScalarGridSpec(
            num_scalar_prefetch=1, grid=(layers + 1,), in_specs=in_specs, out_specs=out_specs,
            scratch_shapes=[pltpu.VMEM((2, 3, rows, width), jnp.float32),
                            pltpu.VMEM((2, rows, width), jnp.float32)],
        ),
        out_shape=out_shape,
        compiler_params=pltpu.CompilerParams(vmem_limit_bytes=VMEM_LIMIT),
    )(position, *args)


def face_sums_kernel(here, inside, s_here, s_inside, sums, totals):
    ntiles = here.shape[2] // 8
    row = lax.broadcasted_iota(jnp.int32, (8, 1), 0)
    for t in range(ntiles):
        at = slice(8 * t, 8 * t + 8)

        def load(c, side):
            if side == 0:
                return s_here[0, at, :] if c == 3 else here[c, 0, at, :]
            return s_inside[0, at, :] if c == 3 else inside[c, 0, at, :]

        def beside(c, tile):
            def take(k, missing, own):
                if missing:
                    return -s_here[0, own : own + 1, :] if c == 3 else 0.0
                return s_here[0, k : k + 1, :] if c == 3 else here[c, 0, k : k + 1, :]

            below = take(8 * t + 8, t == ntiles - 1, 8 * t + 7)
            above = take(8 * t - 1, t == 0, 8 * t)
            yield jnp.where(row == 7, below, pltpu.roll(tile, 7, 0))
            yield jnp.where(row == 0, above, pltpu.roll(tile, 1, 0))

        parts, total, _ = relax_tile(load, beside, None, 0.0)
        for c in range(3):
            sums[c, 0, at, :] = parts[c]
        totals[0, at, :] = total


def face_sums(field, stiffness):
    _, layers, rows, width = field.shape
    outer = lambda i: i * (layers - 1)
    inner = lambda i: 1 + i * (layers - 3)
    f_spec = lambda at: pl.BlockSpec((3, 1, rows, width), lambda i: (0, at(i), 0, 0))
    s_spec = lambda at: pl.BlockSpec((1, rows, width), lambda i: (at(i), 0, 0))
    itself = lambda i: i
    return pl.pallas_call(
        face_sums_kernel,
        name="face_sums",
        grid=(2,),
        in_specs=[f_spec(outer), f_spec(inner), s_spec(outer), s_spec(inner)],
        out_specs=[f_spec(itself), s_spec(itself)],
        out_shape=[jax.ShapeDtypeStruct((3, 2, rows, width), jnp.float32),
                   jax.ShapeDtypeStruct((2, rows, width), jnp.float32)],
        compiler_params=pltpu.CompilerParams(vmem_limit_bytes=VMEM_LIMIT),
    )(field, field, stiffness, stiffness)


def finish_first_kernel(sums, s_here, totals, low, high, s_low, s_high, before, after,
                        s_before, s_after, send_first, send_last, first_row, last_row):
    ntiles = sums.shape[2] // 8
    row = lax.broadcasted_iota(jnp.int32, (8, 1), 0)

    def one(face, outer, s_outer, send):
        layer = face * (s_before.shape[1] - 1)
        for t in range(ntiles):
            at = slice(8 * t, 8 * t + 8)
            here = s_here[0, at, :]
            weight = here + s_outer[0, at, :]
            total = totals[0, at, :] + weight
            values = [sums[c, 0, at, :] + weight * outer[c, at, :] for c in range(3)]
            for wanted, k, f_edge, s_edge in ((0, 0, before, s_before),
                                              (ntiles - 1, 7, after, s_after)):
                if t == wanted:
                    side = jnp.where(row == k, here + s_edge[0, layer : layer + 1, :], 0.0)
                    total = total + side
                    for c in range(3):
                        values[c] = values[c] + side * f_edge[c, layer : layer + 1, :]
            inverse = 1.0 / total
            for c in range(3):
                value = values[c] * inverse
                send[c, at, :] = value
                k = 2 * c + face
                if t == 0:
                    first_row[k : k + 1, :] = value[0:1]
                if t == ntiles - 1:
                    last_row[k : k + 1, :] = value[7:8]

    step = pl.program_id(0)

    @pl.when(step == 0)
    def _():
        first_row[...] = jnp.zeros_like(first_row)
        last_row[...] = jnp.zeros_like(last_row)
        one(0, low, s_low, send_first)

    pl.when(step == 1)(lambda: one(1, high, s_high, send_last))


def finish_first(sums, stiffness, totals, low, high, before, after):
    layers = stiffness.shape[0]
    rows, width = sums.shape[2:]
    block = lambda shape, at: pl.BlockSpec(shape, lambda i: at(i))
    plane = block((3, rows, width), lambda i: (0, 0, 0))
    s_plane = block((1, rows, width), lambda i: (3, 0, 0))
    edge = block((8, width), lambda i: (0, 0))
    f_edge = block((3, layers, width), lambda i: (0, 0, 0))
    s_edge = block((1, layers, width), lambda i: (3, 0, 0))
    face_shape = jax.ShapeDtypeStruct((3, rows, width), jnp.float32)
    edge_shape = jax.ShapeDtypeStruct((8, width), jnp.float32)
    return pl.pallas_call(
        finish_first_kernel,
        name="finish_first",
        grid=(2,),
        in_specs=[block((3, 1, rows, width), lambda i: (0, i, 0, 0)),
                  block((1, rows, width), lambda i: (i * (layers - 1), 0, 0)),
                  block((1, rows, width), lambda i: (i, 0, 0)),
                  plane, plane, s_plane, s_plane, f_edge, f_edge, s_edge, s_edge],
        out_specs=[plane, plane, edge, edge],
        out_shape=[face_shape, face_shape, edge_shape, edge_shape],
        compiler_params=pltpu.CompilerParams(vmem_limit_bytes=VMEM_LIMIT),
    )(sums, stiffness, totals, low, high, low, high, before, after, before, after)


def finish_second_kernel(where_ref, sums, s_here, totals, low, high, s_low, s_high,
                         before, after, s_before, s_after, out):
    ntiles = sums.shape[2] // 8
    pinned = where_ref[1] == 1
    row = lax.broadcasted_iota(jnp.int32, (8, 1), 0)

    def one(face, outer, s_outer):
        layer = face * (s_before.shape[1] - 1)
        for t in range(ntiles):
            at = slice(8 * t, 8 * t + 8)
            here = s_here[0, at, :]
            weight = here + s_outer[0, at, :]
            inverse = 1.0 / (totals[0, at, :] + weight)
            for c in range(3):
                so_far = sums[c, 0, at, :]
                value = so_far + weight * outer[c, at, :]
                k = 2 * c + face
                if t == 0:
                    side = here + s_before[0, layer : layer + 1, :]
                    value = value + jnp.where(row == 0, side * before[k : k + 1, :], 0.0)
                if t == ntiles - 1:
                    side = here + s_after[0, layer : layer + 1, :]
                    value = value + jnp.where(row == 7, side * after[k : k + 1, :], 0.0)
                value = value * inverse
                if face == 0 and c == 0:
                    value = jnp.where(pinned, so_far, value)
                out[c, 0, at, :] = value

    step = pl.program_id(0)
    pl.when(step == 0)(lambda: one(0, low, s_low))
    pl.when(step == 1)(lambda: one(1, high, s_high))


def finish_second(position, field, stiffness, totals, low, high, s_low, s_high,
                  before, after, s_before, s_after):
    _, layers, rows, width = field.shape
    block = lambda shape, at: pl.BlockSpec(shape, lambda i, *_: at(i))
    layer = lambda i: i * (layers - 1)
    plane = block((3, rows, width), lambda i: (0, 0, 0))
    s_plane = block((1, rows, width), lambda i: (3, 0, 0))
    own = block((3, 1, rows, width), lambda i: (0, layer(i), 0, 0))
    edge = block((8, width), lambda i: (0, 0))
    s_edge = block((1, layers, width), lambda i: (3, 0, 0))
    return pl.pallas_call(
        finish_second_kernel,
        name="finish_second",
        grid_spec=pltpu.PrefetchScalarGridSpec(
            num_scalar_prefetch=1, grid=(2,),
            in_specs=[own, block((1, rows, width), lambda i: (layer(i), 0, 0)),
                      block((1, rows, width), lambda i: (i, 0, 0)),
                      plane, plane, s_plane, s_plane, edge, edge, s_edge, s_edge],
            out_specs=own,
        ),
        out_shape=jax.ShapeDtypeStruct(field.shape, jnp.float32),
        input_output_aliases={1: 0},
        compiler_params=pltpu.CompilerParams(vmem_limit_bytes=VMEM_LIMIT),
    )(position, field, stiffness, totals, low, high, s_low, s_high,
      before, after, s_before, s_after)


def per_device(
    displacement,
    stiffness,
    node_list,
    active_count,
    wear_class,
    pressure,
    slip_speed,
    rate_table,
    tile_owner,
    node_cell,
):
    rows, width = displacement.shape[2:]
    position = jnp.stack(
        [lax.axis_index("tan"), (lax.axis_index("depth") == 0).astype(jnp.int32)]
    ).astype(jnp.int32)

    face_first, face_last = pack_faces(displacement, stiffness)
    low, high = shift_both(face_last, face_first, "depth")
    row_first, row_last = pack_rows(displacement, stiffness)
    before, after = shift_both(row_last, row_first, "tan")
    wear = archard(wear_class, pressure, slip_speed, rate_table)
    own, other = gather_wear(wear)
    table = node_cell.reshape(-1, 128)
    tiles_here = wear_class.shape[0]
    tiles = collect(position, tile_owner, tiles_here)
    surface = paint(position, tile_owner, active_count, tiles, own, node_list, table,
                    rows, width, tiles_here)
    sums, totals = face_sums(displacement, stiffness)
    low, high, other, surface = lax.optimization_barrier((low, high, other, surface))
    face_first, face_last, edge_first, edge_last = finish_first(
        sums, stiffness, totals, low, high, before, after
    )
    low_2, high_2 = shift_both(face_last, face_first, "depth")
    surface = paint(position, tile_owner, active_count, tiles, other, node_list, table,
                    rows, width, tiles_here, surface)
    first, before_2, after_2 = relax_layers(
        position, displacement, stiffness, before, after, before, after, surface,
        (face_first, face_last), (row_first, row_last),
    )
    edge_first, edge_last, before_2 = lax.optimization_barrier(
        (edge_first, edge_last, before_2)
    )
    edge_before, edge_after = shift_both(edge_last, edge_first, "tan")
    result, totals = relax_layers(
        position, first, stiffness, before_2, after_2, before, after
    )
    return finish_second(position, result, stiffness, totals, low_2, high_2, low, high,
                         edge_before, edge_after, before, after)


def solution(mesh):
    in_specs = (
        P(None, "depth", "tan", None),
        P("depth", "tan", None),
        P(),
        P(),
        P("tan", None),
        P("tan", None),
        P("tan", None),
        P(),
        P(),
        P(),
    )
    out_specs = P(None, "depth", "tan", None)
    return jax.shard_map(
        per_device, mesh=mesh, in_specs=in_specs, out_specs=out_specs, check_vma=False
    )
```

```python
import functools

import jax
import jax.numpy as jnp
from jax import lax
from jax.experimental import pallas as pl
from jax.experimental.pallas import tpu as pltpu
from jax.sharding import PartitionSpec as P

wear_step = 0.6
hardness = 4.0
GROUP = 8
VMEM_LIMIT = 48 * 1024 * 1024


def shift_both(last, first, axis):
    size = lax.axis_size(axis)
    up = [(i, i + 1) for i in range(size - 1)]
    down = [(j, i) for i, j in up]
    return lax.ppermute(last, axis, up), lax.ppermute(first, axis, down)


def wear_kernel(rates_ref, class_ref, contact_ref, sliding_ref, wear_ref):
    ids = class_ref[...]
    rate = jnp.zeros(ids.shape, jnp.float32)
    for k in range(rates_ref.shape[0]):
        rate = jnp.where(ids == k, rates_ref[k], rate)
    product = contact_ref[...] * sliding_ref[...]
    wear_ref[...] = wear_step * rate * product / (1.0 + product / hardness)


def archard(class_ids, contact, sliding, rates):
    near = pl.BlockSpec(memory_space=pltpu.VMEM)
    return pl.pallas_call(
        wear_kernel,
        name="archard",
        in_specs=[pl.BlockSpec(memory_space=pltpu.SMEM), near, near, near],
        out_specs=near,
        out_shape=jax.ShapeDtypeStruct(contact.shape, jnp.float32),
    )(rates, class_ids, contact, sliding)


def rows_kernel(f_top, s_top, f_bottom, s_bottom, first_ref, last_ref):
    for l in range(f_top.shape[1]):
        for k in range(2):
            first_ref[4 * k + 3, l : l + 1, :] = s_top[l, k : k + 1, :]
            last_ref[4 * k + 3, l : l + 1, :] = s_bottom[l, 7 - k : 8 - k, :]
            for c in range(3):
                first_ref[4 * k + c, l : l + 1, :] = f_top[c, l, k : k + 1, :]
                last_ref[4 * k + c, l : l + 1, :] = f_bottom[c, l, 7 - k : 8 - k, :]


def pack_rows(field, stiffness):
    _, layers, rows, width = field.shape
    bottom = rows // 8 - 1
    f_spec = lambda at: pl.BlockSpec((3, layers, 8, width), lambda i: (0, 0, at, 0))
    s_spec = lambda at: pl.BlockSpec((layers, 8, width), lambda i: (0, at, 0))
    out = jax.ShapeDtypeStruct((8, layers, width), jnp.float32)
    out_spec = pl.BlockSpec((8, layers, width), lambda i: (0, 0, 0))
    return pl.pallas_call(
        rows_kernel,
        name="pack_rows",
        grid=(1,),
        in_specs=[f_spec(0), s_spec(0), f_spec(bottom), s_spec(bottom)],
        out_specs=[out_spec, out_spec],
        out_shape=[out, out],
        compiler_params=pltpu.CompilerParams(vmem_limit_bytes=VMEM_LIMIT),
    )(field, stiffness, field, stiffness)


def faces_kernel(field_ref, stiff_ref, first_ref, last_ref, sems):
    layers = field_ref.shape[1]
    copies = []
    for k, (to, layer) in enumerate(((last_ref, layers - 1), (first_ref, 0))):
        copies.append(pltpu.make_async_copy(
            field_ref.at[:, layer], to.at[pl.ds(0, 3)], sems.at[2 * k]))
        copies.append(pltpu.make_async_copy(
            stiff_ref.at[pl.ds(layer, 1)], to.at[pl.ds(3, 1)], sems.at[2 * k + 1]))
    for copy in copies:
        copy.start()
    for copy in copies:
        copy.wait()


def pack_faces(field, stiffness):
    _, _, rows, width = field.shape
    face = jax.ShapeDtypeStruct((4, rows, width), jnp.float32)
    far = pl.BlockSpec(memory_space=pltpu.HBM)
    near = pl.BlockSpec(memory_space=pltpu.VMEM)
    return pl.pallas_call(
        faces_kernel,
        name="pack_faces",
        in_specs=[far, far],
        out_specs=[near, near],
        out_shape=[face, face],
        scratch_shapes=[pltpu.SemaphoreType.DMA((4,))],
        compiler_params=pltpu.CompilerParams(vmem_limit_bytes=VMEM_LIMIT),
    )(field, stiffness)


def gather_wear(wear):
    size = lax.axis_size("tan")
    groups = [[i for i in range(size) if (i // 2) % 2 == half] for half in range(2)]
    own = lax.all_gather(wear, "tan", axis=0, axis_index_groups=groups, tiled=True)
    return own, lax.ppermute(own, "tan", [(i, i ^ 2) for i in range(size)])


def three_parts(value):
    high = value.astype(jnp.bfloat16).astype(jnp.float32)
    rest = value - high
    middle = rest.astype(jnp.bfloat16).astype(jnp.float32)
    return high, middle, rest - middle


def collect(position, owner, shard_tiles):
    tile = jnp.arange(owner.shape[0], dtype=jnp.int32)
    offset = owner - position[0]
    other = ((tile // (2 * shard_tiles)) ^ (position[0] // 2)) & 1
    kind = jnp.where(offset == 0, 0, jnp.where(offset * offset == 1, 1, 8)) + 2 * other
    mine = kind[None, :] == jnp.arange(4, dtype=jnp.int32)[:, None]
    ahead = jnp.logical_and(tile[None, None, :] < tile[None, :, None], mine[:, None, :])
    place = jnp.where(mine, jnp.sum(jnp.where(ahead, 1, 0), axis=-1), -1)
    lists = jnp.sum(
        jnp.where(place[:, None, :] == tile[None, :, None], tile[None, None, :], 0), axis=-1
    )
    counts = jnp.sum(jnp.where(mine, 1, 0), axis=-1, keepdims=True)
    counts = jnp.broadcast_to(counts, (4, 128))
    return jnp.concatenate([lists, counts], axis=1).astype(jnp.int32).reshape(-1)


def paint_kernel(
    shard_tiles, half, where_ref, owner_ref, count_ref, tiles_ref, wear_ref, list_ref,
    table_ref,
    *refs,
):
    out_ref, acc_ref, edge_ref = refs[-3:]
    room = tiles_ref.shape[0] // 4
    ntile, slots = list_ref.shape
    rows_table = table_ref.shape[0] // ntile
    tile_len = rows_table * 128
    width = out_ref.shape[1]
    rows = out_ref.shape[0] - 16
    me = where_ref[0]
    on_top = where_ref[1]
    out_ref[...] = jnp.zeros_like(out_ref) if half == 0 else refs[0][...]

    @pl.when(on_top == 1)
    def _():
        acc_ref[...] = jnp.zeros_like(acc_ref)
        edge_ref[...] = jnp.zeros_like(edge_ref)

        n_own = tiles_ref[(2 * half + 1) * room - 1]
        n_side = tiles_ref[(2 * half + 2) * room - 1]
        lane = lax.broadcasted_iota(jnp.int32, (1, slots), 1)
        table_row = lax.broadcasted_iota(jnp.int32, (rows_table, slots), 0)
        block = width // 8
        fine = lax.broadcasted_iota(jnp.int32, (block, slots), 0)
        coarse = lax.broadcasted_iota(jnp.int32, (rows * 8, slots), 0)
        fine_edge = lax.broadcasted_iota(jnp.int32, (128, slots), 0)
        edge_blocks = width // 128
        coarse_edge = lax.broadcasted_iota(jnp.int32, (2 * edge_blocks, slots), 0)

        def entry(kind, position, total):
            i = tiles_ref[(2 * half + kind) * room + jnp.minimum(position, total - 1)]
            live = jnp.where(position < total, count_ref[i], 0)
            local = list_ref[pl.ds(i, 1), :] - i * tile_len
            table = table_ref[pl.ds(pl.multiple_of(i * rows_table, 8), rows_table), :]
            column = jnp.broadcast_to(local & 127, (rows_table, slots))
            picked = jnp.take_along_axis(table, column, axis=1)
            cell = jnp.sum(
                jnp.where(table_row == (local >> 7), picked, 0), axis=0, keepdims=True
            )
            shard = i // shard_tiles
            place = (shard // 4) * 2 + shard % 2
            at = place * shard_tiles + i % shard_tiles
            wear = jnp.where(lane < live, wear_ref[pl.ds(at, 1), :], 0.0)
            return i, cell, wear

        def one_hot(mask, value):
            return jnp.where(mask, value, 0.0).astype(jnp.bfloat16)

        def add(into_ref, parts, hot):
            total = into_ref[...]
            for part in parts:
                total = total + lax.dot_general(
                    jnp.concatenate(part, axis=1), hot, (((1,), (1,)), ((), ())),
                    preferred_element_type=jnp.float32,
                )
            into_ref[...] = total

        def own_group(g, carry):
            parts = ([], [], [])
            hots = []
            for j in range(GROUP):
                _, cell, wear = entry(0, g * GROUP + j, n_own)
                col = cell % width
                a_index = (col // block) * rows + cell // width
                hots.append(one_hot(fine == col % block, 1.0))
                mask = coarse == a_index
                for part, value in zip(parts, three_parts(wear)):
                    part.append(one_hot(mask, value))
            add(acc_ref, parts, jnp.concatenate(hots, axis=1))
            return carry

        def side_group(g, carry):
            parts = ([], [], [])
            hots = []
            for j in range(GROUP):
                i, cell, wear = entry(1, g * GROUP + j, n_side)
                below = owner_ref[i] > me
                col = cell % width
                wanted = jnp.where(below, 0, rows - 1)
                shift = jnp.where(below, edge_blocks, 0)
                a_index = jnp.where(cell // width == wanted, col // 128 + shift, -1)
                hots.append(one_hot(fine_edge == col % 128, 1.0))
                mask = coarse_edge == a_index
                for part, value in zip(parts, three_parts(wear)):
                    part.append(one_hot(mask, value))
            add(edge_ref, parts, jnp.concatenate(hots, axis=1))
            return carry

        lax.fori_loop(0, (n_own + GROUP - 1) // GROUP, own_group, 0)
        lax.fori_loop(0, (n_side + GROUP - 1) // GROUP, side_group, 0)
        for j in range(8):
            out_ref[8 : 8 + rows, j * block : (j + 1) * block] += acc_ref[
                j * rows : (j + 1) * rows, :
            ]
        for j in range(edge_blocks):
            out_ref[7:8, j * 128 : (j + 1) * 128] += edge_ref[j : j + 1, :]
            out_ref[8 + rows : 9 + rows, j * 128 : (j + 1) * 128] += edge_ref[
                edge_blocks + j : edge_blocks + j + 1, :
            ]


def paint(position, owner, counts, tiles, wear, lists, table, rows, width, shard_tiles, base=None):
    args = [wear, lists, table] + ([] if base is None else [base])
    return pl.pallas_call(
        functools.partial(paint_kernel, shard_tiles, 0 if base is None else 1),
        name="paint_band",
        in_specs=[pl.BlockSpec(memory_space=pltpu.SMEM)] * 4
        + [pl.BlockSpec(memory_space=pltpu.VMEM)] * len(args),
        out_specs=pl.BlockSpec(memory_space=pltpu.VMEM),
        scratch_shapes=[
            pltpu.VMEM((rows * 8, width // 8), jnp.float32),
            pltpu.VMEM((2 * width // 128, 128), jnp.float32),
        ],
        out_shape=jax.ShapeDtypeStruct((rows + 16, width), jnp.float32),
        compiler_params=pltpu.CompilerParams(vmem_limit_bytes=VMEM_LIMIT),
    )(position, owner, counts, tiles, *args)


def relax_tile(load, beside, has_high, has_low):
    centers = {}

    def neighbours(c):
        here = load(c, 0)
        centers[c] = here
        width = here.shape[1]
        lane = lax.broadcasted_iota(jnp.int32, (here.shape[0], 128), 1)
        yield load(c, 1)
        yield load(c, -1)
        yield from beside(c, here)
        right = pltpu.roll(here, width - 1, 1)
        end = jnp.where(lane == 127, 0.0, right[:, width - 128 :])
        yield jnp.concatenate([right[:, : width - 128], end], axis=1)
        left = pltpu.roll(here, 1, 1)
        end = jnp.where(lane == 0, 0.0, left[:, :128])
        yield jnp.concatenate([end, left[:, 128:]], axis=1)

    around = list(neighbours(3))
    weights = [centers[3] + s for s in around]
    if has_high is not None:
        weights[0] = weights[0] * has_high
    if has_low is not None:
        weights[1] = weights[1] * has_low
    total = weights[0]
    for w in weights[1:]:
        total = total + w
    sums = []
    for c in range(3):
        acc = None
        for w, f in zip(weights, neighbours(c)):
            acc = w * f if acc is None else acc + w * f
        sums.append(acc)
    return sums, total, centers


def relax_outside(out, near, s_near, far, inside, surface, at, layer):
    def load(c, side):
        here = s_near[0] if c == 3 else near[c]
        if c == 0:
            here = here + jnp.where(layer == 0, surface[at : at + 1, :], 0.0)
        return here if side == 0 else pltpu.roll(here, 7 if side == 1 else 1, 0)

    sums, total, _ = relax_tile(load, lambda c, here: (far[c], inside[c]), None, None)
    inverse = 1.0 / total
    between = jnp.logical_and(layer > 0, layer < out.shape[1] - 1)
    kept = jnp.logical_and(between, s_near[0] > 0.0)
    for c in range(3):
        out[c] = jnp.where(kept, sums[c] * inverse, 0.0)


def layer_kernel(first_sweep, *refs):
    where_ref, f_in, s_in, before, after, s_before, s_after = refs[:7]
    rest = list(refs[7:-2])
    f_kept, s_kept = refs[-2:]
    surface = rest.pop(0) if first_sweep else None
    if first_sweep:
        face_first, face_last = rest[:2]
        out = rest[6]
        extra = rest[2:6] + rest[7:]
    else:
        out, totals = rest
    step = pl.program_id(0)
    layer = step - 1
    last = pl.num_programs(0) - 2
    slot = step % 2
    ntiles = f_in.shape[2] // 8
    mid, s_mid = f_kept.at[1 - slot], s_kept.at[1 - slot]
    f_refs = {-1: f_kept.at[slot], 0: mid, 1: f_in.at[:, 0]}
    s_refs = {-1: s_kept.at[slot], 0: s_mid, 1: s_in.at[0]}
    outermost = jnp.logical_or(layer == 0, layer == last)
    row = lax.broadcasted_iota(jnp.int32, (8, 1), 0)

    @pl.when(step == 0)
    def _():
        f_kept[1] = f_in[:, 0]
        s_kept[1] = s_in[0]
        if first_sweep:
            far_before, far_after, own_first, own_last, out_before, out_after = extra
            relax_outside(out_before, before, s_before, far_before, own_first, surface, 7, row)
            relax_outside(out_after, after, s_after, far_after, own_last, surface,
                          8 + 8 * ntiles, row)

    has_low = None if first_sweep else jnp.where(layer == 0, 0.0, 1.0)
    has_high = None if first_sweep else jnp.where(layer == last, 0.0, 1.0)
    scale = jnp.where(layer == 1, 1.0, 0.0)
    pinned = jnp.logical_and(layer == 0, where_ref[1] == 1)

    def sweep():
        for t in range(ntiles):
            at = slice(8 * t, 8 * t + 8)

            def load(c, side):
                if c == 3:
                    return s_refs[side][at, :]
                value = f_refs[side][c, at, :]
                if first_sweep and c == 0 and side < 0:
                    value = value + scale * surface[8 * t + 8 : 8 * t + 16, :]
                return value

            def beside(inside, row, f_edge, s_edge):
                def get(c):
                    if c == 3:
                        if inside:
                            return s_mid[row : row + 1, :]
                        return s_edge[0, pl.ds(layer, 1), :]
                    if inside:
                        return mid[c, row : row + 1, :]
                    return f_edge[c, pl.ds(layer, 1), :]
                return get

            above = beside(t > 0, 8 * t - 1, before, s_before)
            below = beside(t < ntiles - 1, 8 * t + 8, after, s_after)

            def rolled(c, here):
                yield jnp.where(row == 7, below(c), pltpu.roll(here, 7, 0))
                yield jnp.where(row == 0, above(c), pltpu.roll(here, 1, 0))

            sums, total, centers = relax_tile(load, rolled, has_high, has_low)
            inverse = 1.0 / total
            if not first_sweep:
                inverse = jnp.where(outermost, 1.0, inverse)
            outs = [part * inverse for part in sums]
            if not first_sweep:
                outs[0] = jnp.where(pinned, centers[0], outs[0])
                totals[0, at, :] = total
            for c in range(3):
                out[c, 0, at, :] = outs[c]

    if first_sweep:
        inner = jnp.logical_and(layer > 0, layer < last)
        pl.when(inner)(sweep)

        @pl.when(layer == last)
        def _():
            out[:, 0] = face_last[...]

        @pl.when(layer == 0)
        def _():
            out[1:3, 0] = face_first[1:3]
            held = mid[0] + surface[8 : 8 + 8 * ntiles, :]
            out[0, 0] = jnp.where(where_ref[1] == 1, held, face_first[0])
    else:
        pl.when(layer >= 0)(sweep)

    f_kept[slot] = f_in[:, 0]
    s_kept[slot] = s_in[0]


def relax_layers(position, field, stiffness, before, after, s_before, s_after, surface=None,
                 faces=(), own=()):
    _, layers, rows, width = field.shape
    first_sweep = surface is not None
    whole = lambda shape: pl.BlockSpec(shape, lambda i, *_: (0,) * len(shape))
    came = lambda k: jnp.minimum(k, layers - 1)
    swept = lambda k: jnp.maximum(k - 1, 0)
    f_spec = lambda at: pl.BlockSpec((3, 1, rows, width), lambda k, *_: (0, at(k), 0, 0))
    f_edge = whole((3, layers, width))
    s_edge = pl.BlockSpec((1, layers, width), lambda k, *_: (3, 0, 0))
    args = [field, stiffness, before, after, s_before, s_after]
    in_specs = [f_spec(came), pl.BlockSpec((1, rows, width), lambda k, *_: (came(k), 0, 0))]
    in_specs += [f_edge, f_edge, s_edge, s_edge]
    out_shape = [jax.ShapeDtypeStruct(field.shape, jnp.float32)]
    out_specs = [f_spec(swept)]
    if not first_sweep:
        out_shape.append(jax.ShapeDtypeStruct((2, rows, width), jnp.float32))
        out_specs.append(
            pl.BlockSpec((1, rows, width), lambda k, *_: (jnp.minimum(swept(k), 1), 0, 0)))
    else:
        args += [surface, *faces, before, after, *own]
        in_specs += [whole(surface.shape)] + [whole((3, rows, width))] * 2
        near = pl.BlockSpec((4, layers, width), lambda i, *_: (0, 0, 0))
        far = pl.BlockSpec((4, layers, width), lambda i, *_: (1, 0, 0))
        in_specs += [far, far, near, near]
        out_shape += [jax.ShapeDtypeStruct((3, layers, width), jnp.float32)] * 2
        out_specs += [f_edge] * 2
    return pl.pallas_call(
        functools.partial(layer_kernel, first_sweep),
        name="relax_layers_first" if first_sweep else "relax_layers_second",
        grid_spec=pltpu.PrefetchScalarGridSpec(
            num_scalar_prefetch=1, grid=(layers + 1,), in_specs=in_specs, out_specs=out_specs,
            scratch_shapes=[pltpu.VMEM((2, 3, rows, width), jnp.float32),
                            pltpu.VMEM((2, rows, width), jnp.float32)],
        ),
        out_shape=out_shape,
        compiler_params=pltpu.CompilerParams(vmem_limit_bytes=VMEM_LIMIT),
    )(position, *args)


def face_sums_kernel(here, inside, s_here, s_inside, sums, totals):
    ntiles = here.shape[2] // 8
    row = lax.broadcasted_iota(jnp.int32, (8, 1), 0)
    for t in range(ntiles):
        at = slice(8 * t, 8 * t + 8)

        def load(c, side):
            if side == 0:
                return s_here[0, at, :] if c == 3 else here[c, 0, at, :]
            return s_inside[0, at, :] if c == 3 else inside[c, 0, at, :]

        def beside(c, tile):
            def take(k, missing, own):
                if missing:
                    return -s_here[0, own : own + 1, :] if c == 3 else 0.0
                return s_here[0, k : k + 1, :] if c == 3 else here[c, 0, k : k + 1, :]

            below = take(8 * t + 8, t == ntiles - 1, 8 * t + 7)
            above = take(8 * t - 1, t == 0, 8 * t)
            yield jnp.where(row == 7, below, pltpu.roll(tile, 7, 0))
            yield jnp.where(row == 0, above, pltpu.roll(tile, 1, 0))

        parts, total, _ = relax_tile(load, beside, None, 0.0)
        for c in range(3):
            sums[c, 0, at, :] = parts[c]
        totals[0, at, :] = total


def face_sums(field, stiffness):
    _, layers, rows, width = field.shape
    outer = lambda i: i * (layers - 1)
    inner = lambda i: 1 + i * (layers - 3)
    f_spec = lambda at: pl.BlockSpec((3, 1, rows, width), lambda i: (0, at(i), 0, 0))
    s_spec = lambda at: pl.BlockSpec((1, rows, width), lambda i: (at(i), 0, 0))
    itself = lambda i: i
    return pl.pallas_call(
        face_sums_kernel,
        name="face_sums",
        grid=(2,),
        in_specs=[f_spec(outer), f_spec(inner), s_spec(outer), s_spec(inner)],
        out_specs=[f_spec(itself), s_spec(itself)],
        out_shape=[jax.ShapeDtypeStruct((3, 2, rows, width), jnp.float32),
                   jax.ShapeDtypeStruct((2, rows, width), jnp.float32)],
        compiler_params=pltpu.CompilerParams(vmem_limit_bytes=VMEM_LIMIT),
    )(field, field, stiffness, stiffness)


def finish_first_kernel(sums, s_here, totals, low, high, s_low, s_high, before, after,
                        s_before, s_after, send_first, send_last, first_row, last_row):
    ntiles = sums.shape[2] // 8
    row = lax.broadcasted_iota(jnp.int32, (8, 1), 0)

    def one(face, outer, s_outer, send):
        layer = face * (s_before.shape[1] - 1)
        for t in range(ntiles):
            at = slice(8 * t, 8 * t + 8)
            here = s_here[0, at, :]
            weight = here + s_outer[0, at, :]
            total = totals[0, at, :] + weight
            values = [sums[c, 0, at, :] + weight * outer[c, at, :] for c in range(3)]
            for wanted, k, f_edge, s_edge in ((0, 0, before, s_before),
                                              (ntiles - 1, 7, after, s_after)):
                if t == wanted:
                    side = jnp.where(row == k, here + s_edge[0, layer : layer + 1, :], 0.0)
                    total = total + side
                    for c in range(3):
                        values[c] = values[c] + side * f_edge[c, layer : layer + 1, :]
            inverse = 1.0 / total
            for c in range(3):
                value = values[c] * inverse
                send[c, at, :] = value
                k = 2 * c + face
                if t == 0:
                    first_row[k : k + 1, :] = value[0:1]
                if t == ntiles - 1:
                    last_row[k : k + 1, :] = value[7:8]

    step = pl.program_id(0)

    @pl.when(step == 0)
    def _():
        first_row[...] = jnp.zeros_like(first_row)
        last_row[...] = jnp.zeros_like(last_row)
        one(0, low, s_low, send_first)

    pl.when(step == 1)(lambda: one(1, high, s_high, send_last))


def finish_first(sums, stiffness, totals, low, high, before, after):
    layers = stiffness.shape[0]
    rows, width = sums.shape[2:]
    block = lambda shape, at: pl.BlockSpec(shape, lambda i: at(i))
    plane = block((3, rows, width), lambda i: (0, 0, 0))
    s_plane = block((1, rows, width), lambda i: (3, 0, 0))
    edge = block((8, width), lambda i: (0, 0))
    f_edge = block((3, layers, width), lambda i: (0, 0, 0))
    s_edge = block((1, layers, width), lambda i: (3, 0, 0))
    face_shape = jax.ShapeDtypeStruct((3, rows, width), jnp.float32)
    edge_shape = jax.ShapeDtypeStruct((8, width), jnp.float32)
    return pl.pallas_call(
        finish_first_kernel,
        name="finish_first",
        grid=(2,),
        in_specs=[block((3, 1, rows, width), lambda i: (0, i, 0, 0)),
                  block((1, rows, width), lambda i: (i * (layers - 1), 0, 0)),
                  block((1, rows, width), lambda i: (i, 0, 0)),
                  plane, plane, s_plane, s_plane, f_edge, f_edge, s_edge, s_edge],
        out_specs=[plane, plane, edge, edge],
        out_shape=[face_shape, face_shape, edge_shape, edge_shape],
        compiler_params=pltpu.CompilerParams(vmem_limit_bytes=VMEM_LIMIT),
    )(sums, stiffness, totals, low, high, low, high, before, after, before, after)


def finish_second_kernel(where_ref, sums, s_here, totals, low, high, s_low, s_high,
                         before, after, s_before, s_after, out):
    ntiles = sums.shape[2] // 8
    pinned = where_ref[1] == 1
    row = lax.broadcasted_iota(jnp.int32, (8, 1), 0)

    def one(face, outer, s_outer):
        layer = face * (s_before.shape[1] - 1)
        for t in range(ntiles):
            at = slice(8 * t, 8 * t + 8)
            here = s_here[0, at, :]
            weight = here + s_outer[0, at, :]
            inverse = 1.0 / (totals[0, at, :] + weight)
            for c in range(3):
                so_far = sums[c, 0, at, :]
                value = so_far + weight * outer[c, at, :]
                k = 2 * c + face
                if t == 0:
                    side = here + s_before[0, layer : layer + 1, :]
                    value = value + jnp.where(row == 0, side * before[k : k + 1, :], 0.0)
                if t == ntiles - 1:
                    side = here + s_after[0, layer : layer + 1, :]
                    value = value + jnp.where(row == 7, side * after[k : k + 1, :], 0.0)
                value = value * inverse
                if face == 0 and c == 0:
                    value = jnp.where(pinned, so_far, value)
                out[c, 0, at, :] = value

    step = pl.program_id(0)
    pl.when(step == 0)(lambda: one(0, low, s_low))
    pl.when(step == 1)(lambda: one(1, high, s_high))


def finish_second(position, field, stiffness, totals, low, high, s_low, s_high,
                  before, after, s_before, s_after):
    _, layers, rows, width = field.shape
    block = lambda shape, at: pl.BlockSpec(shape, lambda i, *_: at(i))
    layer = lambda i: i * (layers - 1)
    plane = block((3, rows, width), lambda i: (0, 0, 0))
    s_plane = block((1, rows, width), lambda i: (3, 0, 0))
    own = block((3, 1, rows, width), lambda i: (0, layer(i), 0, 0))
    edge = block((8, width), lambda i: (0, 0))
    s_edge = block((1, layers, width), lambda i: (3, 0, 0))
    return pl.pallas_call(
        finish_second_kernel,
        name="finish_second",
        grid_spec=pltpu.PrefetchScalarGridSpec(
            num_scalar_prefetch=1, grid=(2,),
            in_specs=[own, block((1, rows, width), lambda i: (layer(i), 0, 0)),
                      block((1, rows, width), lambda i: (i, 0, 0)),
                      plane, plane, s_plane, s_plane, edge, edge, s_edge, s_edge],
            out_specs=own,
        ),
        out_shape=jax.ShapeDtypeStruct(field.shape, jnp.float32),
        input_output_aliases={1: 0},
        compiler_params=pltpu.CompilerParams(vmem_limit_bytes=VMEM_LIMIT),
    )(position, field, stiffness, totals, low, high, s_low, s_high,
      before, after, s_before, s_after)


def per_device(
    displacement,
    stiffness,
    node_list,
    active_count,
    wear_class,
    pressure,
    slip_speed,
    rate_table,
    tile_owner,
    node_cell,
):
    rows, width = displacement.shape[2:]
    position = jnp.stack(
        [lax.axis_index("tan"), (lax.axis_index("depth") == 0).astype(jnp.int32)]
    ).astype(jnp.int32)

    face_first, face_last = pack_faces(displacement, stiffness)
    low, high = shift_both(face_last, face_first, "depth")
    row_first, row_last = pack_rows(displacement, stiffness)
    before, after = shift_both(row_last, row_first, "tan")
    wear = archard(wear_class, pressure, slip_speed, rate_table)
    own, other = gather_wear(wear)
    table = node_cell.reshape(-1, 128)
    tiles_here = wear_class.shape[0]
    tiles = collect(position, tile_owner, tiles_here)
    surface = paint(position, tile_owner, active_count, tiles, own, node_list, table,
                    rows, width, tiles_here)
    sums, totals = face_sums(displacement, stiffness)
    low, high, other, surface = lax.optimization_barrier((low, high, other, surface))
    face_first, face_last, edge_first, edge_last = finish_first(
        sums, stiffness, totals, low, high, before, after
    )
    low_2, high_2 = shift_both(face_last, face_first, "depth")
    surface = paint(position, tile_owner, active_count, tiles, other, node_list, table,
                    rows, width, tiles_here, surface)
    first, before_2, after_2 = relax_layers(
        position, displacement, stiffness, before, after, before, after, surface,
        (face_first, face_last), (row_first, row_last),
    )
    edge_first, edge_last, before_2 = lax.optimization_barrier(
        (edge_first, edge_last, before_2)
    )
    edge_before, edge_after = shift_both(edge_last, edge_first, "tan")
    result, totals = relax_layers(
        position, first, stiffness, before_2, after_2, before, after
    )
    return finish_second(position, result, stiffness, totals, low_2, high_2, low, high,
                         edge_before, edge_after, before, after)


def solution(mesh):
    in_specs = (
        P(None, "depth", "tan", None),
        P("depth", "tan", None),
        P(),
        P(),
        P("tan", None),
        P("tan", None),
        P("tan", None),
        P(),
        P(),
        P(),
    )
    out_specs = P(None, "depth", "tan", None)
    return jax.shard_map(
        per_device, mesh=mesh, in_specs=in_specs, out_specs=out_specs, check_vma=False
    )
```
